32 devices in a mesh: ty: 2 (over y), tx: 4 (over x, core), ha: 4 (over z).
Axes of the slice: x: 2, y: 2, z: 4, core: 2. Of those that a mesh axis runs over, the one named last changes fastest.
Arguments:
- queries: bfloat16 [4, 16, 128, 5120], P(None, 'ty', 'tx', 'ha'), may hold values from -8 to 8
- keys_now: bfloat16 [4, 16, 128, 5120], P(None, 'ty', 'tx', 'ha'), may hold values from -8 to 8
- values_now: bfloat16 [4, 16, 128, 5120], P(None, 'ty', 'tx', 'ha'), may hold values from -6 to 6
- query_gain: float32 [5120], P('ha'), may hold values from 0.6 to 2
- key_gain: float32 [5120], P('ha'), may hold values from 0.6 to 2
- cached_keys: bfloat16 [512, 32, 5120], P(('ty', 'tx'), None, 'ha'), may hold values from -6 to 6
- cached_values: bfloat16 [512, 32, 5120], P(('ty', 'tx'), None, 'ha'), may hold values from -6 to 6
- block_lists: int32 [8, 48], P(('ty', 'tx')), may hold values from 0 to 511, as said below
- block_counts: int32 [8], P(('ty', 'tx')), may hold values from 6 to 48
Outputs:
- attended: bfloat16 [4, 16, 128, 5120], P(None, 'ty', 'tx', 'ha')
The draws below stay inside these ranges and needn't reach their ends.
Inputs may be any that keep to these rules, and one draw needn't show every extreme that they name: `block_lists`: each tile's 48 entries are distinct. The owner of id i is tile i // 64, tiles counted row by row over the tile grid. Of a tile's 48 entries, valid or not, at most 8 have the same owner, and some owner tile holds exactly 8 entries of every tile's list.
All inputs are finite; a program needn't handle non-finite values.
Results may differ from the reference program's by a relative error of at most 0.012.
The reference program's roundings to bfloat16 on the way count: a program that leaves them out, or rounds other values in their place, can miss the bound.
Values may be sent and summed in bfloat16 or wider, within the bound.
A program may use at most 128 MiB of HBM per device.

```python
import math
import jax
import jax.numpy as jnp
from jax import lax

HD = 128
FRAMES = 4
TH = 8
TW = 32
HALO = 4
NB = 48
HEADS = 40
FEAT = 5120
GH = 16
GW = 128
TOKB = 32
BPT = 64
TILES = 8
NBLK = 512
CAP = 8
N_TY = 2
N_TX = 4


def spread_field(key, salt_value):
    extent = (FRAMES, GH, GW, FEAT)
    column = jnp.arange(FEAT, dtype=jnp.float32)
    scramble = (jnp.arange(FEAT, dtype=jnp.int32) * 613 % 1009).astype(jnp.float32) / 1009.0
    baseline = jax.random.normal(jax.random.fold_in(key, salt_value), extent, jnp.float32)
    exponent = 0.3 * column / FEAT + 0.7 * scramble
    row_scale = jnp.exp(jax.random.uniform(jax.random.fold_in(key, salt_value + 1), (FRAMES, GH, GW, 1), jnp.float32, -1.2, 1.1))
    return baseline * 0.08 * jnp.power(10.0, exponent) * row_scale


def draw_queries(key, part):
    sampled = spread_field(key, 11)
    return jnp.clip(sampled, -8.0, 8.0).astype(jnp.bfloat16)


def draw_keys_now(key, part):
    sampled = spread_field(key, 21)
    return jnp.clip(sampled, -8.0, 8.0).astype(jnp.bfloat16)


def draw_block_lists(key, part):
    slot_total = TILES * CAP
    favourite = jax.random.randint(jax.random.fold_in(key, 5), (), 0, TILES)
    start_block = jax.random.randint(jax.random.fold_in(key, 6), (TILES, TILES), 0, BPT)
    slot_no = jnp.arange(slot_total, dtype=jnp.int32)
    slot_owner = slot_no // CAP
    slot_rank = slot_no % CAP

    def one_list(tile_no):
        tile_key = jax.random.fold_in(key, tile_no + 100)
        random_score = jax.random.randint(jax.random.fold_in(tile_key, 1), (slot_total,), 0, 262144)
        priority = jnp.where(slot_owner == favourite, slot_rank - CAP, random_score * slot_total + slot_no)
        picked = jnp.argsort(priority, stable=True)[:NB]
        shuffle_score = jax.random.randint(jax.random.fold_in(tile_key, 2), (NB,), 0, 262144) * NB + jnp.arange(NB, dtype=jnp.int32)
        shuffled = picked[jnp.argsort(shuffle_score, stable=True)]
        owner_list = slot_owner[shuffled]
        within = (start_block[tile_no, owner_list] + slot_rank[shuffled]) % BPT
        return (owner_list * BPT + within).astype(jnp.int32)
    return jax.vmap(one_list)(jnp.arange(TILES, dtype=jnp.int32))


def draw_block_counts(key, part):
    lower = NB // 8 + jax.random.randint(jax.random.fold_in(key, 31), (TILES,), 0, NB // 4 + 1)
    ranking = jax.random.permutation(jax.random.fold_in(key, 32), TILES)
    return jnp.where(ranking < max(1, TILES // 8), NB, lower).astype(jnp.int32)


def steps_of(rng, dims, cuts, low, largest):
    loudness, own = 1.0, jax.random.fold_in(rng, 6)
    for dim, blocks in cuts:
        heights = jnp.exp(jax.random.uniform(jax.random.fold_in(own, dim), (blocks,), jnp.float32, low / len(cuts), largest / len(cuts)))
        loudness = loudness * jnp.repeat(heights, dims[dim] // blocks).reshape([-1 if axis == dim else 1 for axis in range(len(dims))])
    return loudness


def gaussian(rng, shape, width, reach, cuts=(), kind=jnp.bfloat16):
    drawn = jax.random.normal(rng, shape, jnp.float32) * width
    if len(cuts) > 0:
        drawn = steps_of(rng, shape, cuts, -0.22, 0.18) * drawn
    return jnp.clip(drawn, min=-reach, max=reach).astype(kind)


def setup_inputs(seed: int = 0) -> dict:
    splits = jax.random.split(jax.random.key(seed), 10)
    return {
        "queries": draw_queries(jax.random.fold_in(splits[9], 71), 0),
        "keys_now": draw_keys_now(jax.random.fold_in(splits[9], 71), 0),
        "values_now": gaussian(splits[2], (FRAMES, GH, GW, FEAT), 1.0, 6.0, ((1, 2), (2, 4), (3, 4))),
        "query_gain": jnp.clip(jnp.exp(math.log(2.0) - 1.2039728 * jax.random.uniform(splits[3], (FEAT,), jnp.float32) ** steps_of(splits[3], (FEAT,), ((0, 4),), -0.2, 0.2)), 0.6, 2.0),
        "key_gain": jnp.clip(jnp.exp(math.log(2.0) - 1.2039728 * jax.random.uniform(splits[4], (FEAT,), jnp.float32) ** steps_of(splits[4], (FEAT,), ((0, 4),), -0.2, 0.2)), 0.6, 2.0),
        "cached_keys": gaussian(splits[5], (NBLK, TOKB, FEAT), 1.0, 6.0, ((0, 8), (2, 4))),
        "cached_values": gaussian(splits[6], (NBLK, TOKB, FEAT), 1.0, 6.0, ((0, 8), (2, 4))),
        "block_lists": draw_block_lists(jax.random.fold_in(splits[9], 71), 0),
        "block_counts": draw_block_counts(jax.random.fold_in(splits[9], 71), 0),
    }


epsilon = 1e-06
masked_score = -1e+30

def normed(values_in, gain_vector):
    widened = values_in.astype(jnp.float32)
    mean_square = lax.optimization_barrier(jnp.sum(widened * widened, axis=-1, keepdims=True)) / FEAT
    return (widened * lax.rsqrt(mean_square + epsilon) * gain_vector).astype(jnp.bfloat16)

def reference(queries, keys_now, values_now, query_gain, key_gain, cached_keys, cached_values, block_lists, block_counts):
    normed_query = lax.optimization_barrier(normed(queries, query_gain))
    normed_key = normed(keys_now, key_gain)
    margins = ((0, 0), (HALO, HALO), (HALO, HALO), (0, 0))
    key_padded = lax.optimization_barrier(jnp.pad(normed_key, margins))
    value_padded = jnp.pad(values_now, margins)
    span_rows = TH + 2 * HALO
    span_cols = TW + 2 * HALO
    query_frame = jnp.repeat(jnp.arange(FRAMES, dtype=jnp.int32), TH * TW)
    key_frame = jnp.repeat(jnp.arange(FRAMES, dtype=jnp.int32), span_rows * span_cols)
    scaling = HD ** (-0.5)

    def one_tile(tile_no):
        tile_row = tile_no // N_TX
        tile_col = tile_no % N_TX
        anchor = jnp.zeros((), jnp.int32)
        first_row = (tile_row * TH).astype(jnp.int32)
        first_col = (tile_col * TW).astype(jnp.int32)
        query_tile = lax.dynamic_slice(normed_query, (anchor, first_row, first_col, anchor), (FRAMES, TH, TW, FEAT))
        query_tile = query_tile.reshape(-1, HEADS, HD).astype(jnp.float32)
        key_tile = lax.dynamic_slice(key_padded, (anchor, first_row, first_col, anchor), (FRAMES, span_rows, span_cols, FEAT))
        key_tile = key_tile.reshape(-1, HEADS, HD).astype(jnp.float32)
        value_tile = lax.dynamic_slice(value_padded, (anchor, first_row, first_col, anchor), (FRAMES, span_rows, span_cols, FEAT))
        value_tile = value_tile.reshape(-1, HEADS, HD).astype(jnp.float32)
        grid_row = first_row - HALO + jnp.arange(span_rows, dtype=jnp.int32)
        grid_col = first_col - HALO + jnp.arange(span_cols, dtype=jnp.int32)
        inside = ((grid_row >= 0) & (grid_row < GH))[:, None] & ((grid_col >= 0) & (grid_col < GW))[None, :]
        inside = jnp.tile(inside.reshape(-1), FRAMES)
        visible = (key_frame[None, :] <= query_frame[:, None]) & inside[None, :]
        listed = block_lists[tile_no]
        far_keys = jnp.take(cached_keys, listed, axis=0).reshape(-1, HEADS, HD).astype(jnp.float32)
        far_values = jnp.take(cached_values, listed, axis=0).reshape(-1, HEADS, HD).astype(jnp.float32)
        usable = jnp.repeat(jnp.arange(NB, dtype=jnp.int32) < block_counts[tile_no], TOKB)
        near_scores = jnp.einsum('qhd,khd->hqk', query_tile, key_tile) * scaling
        near_scores = jnp.where(visible[None], near_scores, masked_score)
        far_scores = jnp.einsum('qhd,khd->hqk', query_tile, far_keys) * scaling
        far_scores = jnp.where(usable[None, None], far_scores, masked_score)
        row_max = jnp.maximum(lax.optimization_barrier(jnp.max(near_scores, axis=-1)), lax.optimization_barrier(jnp.max(far_scores, axis=-1)))
        near_exp = jnp.exp(near_scores - row_max[..., None])
        far_exp = jnp.exp(far_scores - row_max[..., None])
        totals = lax.optimization_barrier(jnp.sum(near_exp, axis=-1)) + lax.optimization_barrier(jnp.sum(far_exp, axis=-1))
        near_weights = lax.optimization_barrier(near_exp.astype(jnp.bfloat16)).astype(jnp.float32)
        far_weights = lax.optimization_barrier(far_exp.astype(jnp.bfloat16)).astype(jnp.float32)
        weighted = jnp.einsum('hqk,khd->hqd', near_weights, value_tile)
        weighted = weighted + jnp.einsum('hqk,khd->hqd', far_weights, far_values)
        result = (weighted / totals[..., None]).astype(jnp.bfloat16)
        return jnp.transpose(result, (1, 0, 2)).reshape(-1, FEAT)
    all_tiles = lax.map(one_tile, jnp.arange(TILES, dtype=jnp.int32))
    all_tiles = all_tiles.reshape(N_TY, N_TX, FRAMES, TH, TW, FEAT)
    return jnp.transpose(all_tiles, (2, 0, 3, 1, 4, 5)).reshape(FRAMES, GH, GW, FEAT)
```

```python
import functools
import math

import jax
import jax.numpy as jnp
from jax import lax
from jax.experimental import pallas as pl
from jax.experimental.pallas import tpu as pltpu
from jax.sharding import PartitionSpec as P

HD = 128
HALO = 4
CHUNK = 16

epsilon = 1e-06
masked_score = -1e30
log2_scale = HD ** (-0.5) * math.log2(math.e)


def neighbours(cells, axis, dim, width):
    count = lax.axis_size(axis)
    size = cells.shape[dim]
    head = lax.slice_in_dim(cells, 0, width, axis=dim)
    tail = lax.slice_in_dim(cells, size - width, size, axis=dim)
    where_am_i = lax.axis_index(axis)
    if count == 2:
        mine = jnp.where(where_am_i == 0, tail, head)
        got = lax.ppermute(mine, axis, [(0, 1), (1, 0)])
        return [(got, jnp.bool_(True))]
    ends = count - 1
    before = lax.ppermute(tail, axis, [(i, i + 1) for i in range(ends)])
    after = lax.ppermute(head, axis, [(i + 1, i) for i in range(ends)])
    return [(before, where_am_i > 0), (after, where_am_i < ends)]


def slot_ranks(owners):
    length = owners.shape[-1]
    earlier = lax.broadcasted_iota(jnp.int32, (length, length), 1) < lax.broadcasted_iota(
        jnp.int32, (length, length), 0
    )
    same_owner = owners[..., :, None] == owners[..., None, :]
    return jnp.sum(jnp.where(same_owner & earlier, 1, 0), axis=-1).astype(jnp.int32)


def near_kernel(frames, per_query, n_parts, q_ref, bias_ref, *refs):
    parts_k = refs[:n_parts]
    parts_v = refs[n_parts : 2 * n_parts]
    acc_ref, ml_ref, kbuf, vbuf = refs[2 * n_parts :]
    span = kbuf.shape[0] // frames
    for f in range(frames):
        start = f * span
        for k_ref, v_ref in zip(parts_k, parts_v):
            rows = k_ref.shape[1]
            kbuf[start : start + rows, :] = k_ref[f]
            vbuf[start : start + rows, :HD] = v_ref[f]
            start += rows
    vbuf[:, HD:] = jnp.ones((vbuf.shape[0], HD), jnp.bfloat16)
    for f in range(frames):
        keys = (f + 1) * span
        s = lax.dot_general(
            q_ref[f], kbuf[:keys], (((1,), (1,)), ((), ())), preferred_element_type=jnp.float32
        )
        s = s + bias_ref[:, :keys]
        m = jnp.max(s, axis=1, keepdims=True) * log2_scale
        p = jnp.exp2(s * log2_scale - m).astype(jnp.bfloat16)
        o = jnp.dot(p, vbuf[:keys], preferred_element_type=jnp.float32)
        acc_ref[f] = o[:, :HD]
        lane = lax.broadcasted_iota(jnp.int32, (per_query, HD), 1)
        ml_ref[0, f] = jnp.where(lane < HD // 2, m, o[:, HD:])


def far_kernel(
    frames, per_query, tokens, count_ref, slot_ref, q_ref, acc_in, ml_in, k_ref, v_ref, out_ref,
    kbuf, vbuf, m_sc, l_sc, acc_sc,
):
    count = count_ref[0]
    vbuf[:, HD:] = jnp.ones((vbuf.shape[0], HD), jnp.bfloat16)
    for f in range(frames):
        ml = ml_in[0, f]
        m_sc[f] = jnp.broadcast_to(ml[:, :1], (per_query, HD))
        l_sc[f] = jnp.broadcast_to(ml[:, HD // 2 : HD // 2 + 1], (per_query, HD))
        acc_sc[f] = acc_in[f]

    def chunk(c, carry):
        for i in range(CHUNK):
            slot = slot_ref[c * CHUNK + i]
            kbuf[i * tokens : (i + 1) * tokens, :] = k_ref[slot, 0]
            vbuf[i * tokens : (i + 1) * tokens, :HD] = v_ref[slot, 0]
        place = lax.broadcasted_iota(jnp.int32, (1, CHUNK * tokens), 1)
        bias = jnp.where(place < (count - c * CHUNK) * tokens, 0.0, masked_score)
        for f in range(frames):
            s = lax.dot_general(
                q_ref[f], kbuf[...], (((1,), (1,)), ((), ())), preferred_element_type=jnp.float32
            )
            s = s + bias
            m_old = m_sc[f]
            m_new = jnp.maximum(m_old, jnp.max(s, axis=1, keepdims=True) * log2_scale)
            p = jnp.exp2(s * log2_scale - m_new[:, :1]).astype(jnp.bfloat16)
            o = jnp.dot(p, vbuf[...], preferred_element_type=jnp.float32)
            a = jnp.exp2(m_old - m_new)
            acc_sc[f] = acc_sc[f] * a + o[:, :HD]
            l_sc[f] = l_sc[f] * a + o[:, HD:]
            m_sc[f] = m_new
        return carry

    lax.fori_loop(0, (count + CHUNK - 1) // CHUNK, chunk, 0)
    for f in range(frames):
        out_ref[f] = (acc_sc[f] / l_sc[f]).astype(jnp.bfloat16)


def near_attention(query, parts_k, parts_v, bias):
    frames, per_query, features = query.shape
    heads = features // HD
    span = sum(part.shape[1] for part in parts_k)

    def spec(rows):
        return pl.BlockSpec((frames, rows, HD), lambda h: (0, 0, h))

    part_specs = [spec(part.shape[1]) for part in parts_k]
    keys = frames * span
    return pl.pallas_call(
        functools.partial(near_kernel, frames, per_query, len(parts_k)),
        grid=(heads,),
        in_specs=[spec(per_query), pl.BlockSpec((1, keys), lambda h: (0, 0))]
        + part_specs
        + part_specs,
        out_specs=[
            spec(per_query),
            pl.BlockSpec((1, frames, per_query, HD), lambda h: (h, 0, 0, 0)),
        ],
        out_shape=[
            jax.ShapeDtypeStruct((frames, per_query, features), jnp.float32),
            jax.ShapeDtypeStruct((heads, frames, per_query, HD), jnp.float32),
        ],
        scratch_shapes=[
            pltpu.VMEM((keys, HD), jnp.bfloat16),
            pltpu.VMEM((keys, 2 * HD), jnp.bfloat16),
        ],
        compiler_params=pltpu.CompilerParams(vmem_limit_bytes=60 << 20),
        cost_estimate=pl.CostEstimate(
            flops=heads * frames * per_query * keys * HD * 6,
            bytes_accessed=30 << 20,
            transcendentals=heads * frames * per_query * keys,
        ),
        name="near",
    )(query, bias, *parts_k, *parts_v)


def pick_kernel(total, group, wanted_ref, keys_ref, values_ref, out_ref, held, in_sem, out_sem):
    groups = total // group

    def fetch(i, carry):
        block = wanted_ref[i]
        sem = in_sem.at[i // group]
        pltpu.make_async_copy(keys_ref.at[block], held.at[i, 0], sem).start()
        pltpu.make_async_copy(values_ref.at[block], held.at[i, 1], sem).start()
        return carry

    lax.fori_loop(0, total, fetch, 0)
    for g in range(groups):
        part = pl.ds(g * group, group)
        pltpu.make_async_copy(held.at[part], held.at[part], in_sem.at[g]).wait()
        pltpu.make_async_copy(held.at[part], out_ref.at[part], out_sem.at[g]).start()
    for g in range(groups):
        part = pl.ds(g * group, group)
        pltpu.make_async_copy(held.at[part], out_ref.at[part], out_sem.at[g]).wait()


def pick_blocks(wanted, keys, values):
    total = wanted.shape[0]
    group = 8 if total % 8 == 0 else 1
    shape = (total, 2) + keys.shape[1:]
    return pl.pallas_call(
        functools.partial(pick_kernel, total, group),
        grid_spec=pltpu.PrefetchScalarGridSpec(
            num_scalar_prefetch=1,
            grid=(),
            in_specs=[pl.BlockSpec(memory_space=pl.ANY)] * 2,
            out_specs=pl.BlockSpec(memory_space=pl.ANY),
            scratch_shapes=[
                pltpu.VMEM(shape, keys.dtype),
                pltpu.SemaphoreType.DMA((total // group,)),
                pltpu.SemaphoreType.DMA((total // group,)),
            ],
        ),
        out_shape=jax.ShapeDtypeStruct(shape, keys.dtype),
        compiler_params=pltpu.CompilerParams(vmem_limit_bytes=60 << 20),
        cost_estimate=pl.CostEstimate(flops=0, bytes_accessed=20 << 20, transcendentals=0),
        name="pick",
    )(wanted, keys, values)


def far_attention(query, acc, ml, blocks, count, slots):
    frames, per_query, features = query.shape
    all_slots, _, tokens, width = blocks.shape
    heads = width // HD
    spec = pl.BlockSpec((frames, per_query, HD), lambda h, *_: (0, 0, h))
    k_spec = pl.BlockSpec((all_slots, 1, tokens, HD), lambda h, *_: (0, 0, 0, h))
    v_spec = pl.BlockSpec((all_slots, 1, tokens, HD), lambda h, *_: (0, 1, 0, h))
    return pl.pallas_call(
        functools.partial(far_kernel, frames, per_query, tokens),
        grid_spec=pltpu.PrefetchScalarGridSpec(
            num_scalar_prefetch=2,
            grid=(heads,),
            in_specs=[
                spec,
                spec,
                pl.BlockSpec((1, frames, per_query, HD), lambda h, *_: (h, 0, 0, 0)),
                k_spec,
                v_spec,
            ],
            out_specs=pl.BlockSpec((frames, per_query, HD), lambda h, *_: (0, 0, h)),
            scratch_shapes=[
                pltpu.VMEM((CHUNK * tokens, HD), jnp.bfloat16),
                pltpu.VMEM((CHUNK * tokens, 2 * HD), jnp.bfloat16),
                pltpu.VMEM((frames, per_query, HD), jnp.float32),
                pltpu.VMEM((frames, per_query, HD), jnp.float32),
                pltpu.VMEM((frames, per_query, HD), jnp.float32),
            ],
        ),
        out_shape=jax.ShapeDtypeStruct((frames, per_query, width), jnp.bfloat16),
        compiler_params=pltpu.CompilerParams(vmem_limit_bytes=60 << 20),
        cost_estimate=pl.CostEstimate(
            flops=heads * frames * per_query * 1536 * HD * 6,
            bytes_accessed=30 << 20,
            transcendentals=heads * frames * per_query * 1536,
        ),
        name="far",
    )(count, slots, query, acc, ml, blocks, blocks)


def general(
    queries,
    keys_now,
    values_now,
    query_gain,
    key_gain,
    cached_keys,
    cached_values,
    block_lists,
    block_counts,
):
    frames, tile_rows, tile_cols, features = queries.shape
    owners_all = lax.axis_size("ty") * lax.axis_size("tx")
    full_width = features * lax.axis_size("ha")
    per_query = tile_rows * tile_cols
    per_tile, block_tokens = cached_keys.shape[:2]

    listed = block_lists[0]
    list_length = listed.shape[0]
    owners = listed // per_tile
    within = listed % per_tile
    slot_rank = slot_ranks(owners)
    capacity = max(2, 4 * list_length // (3 * owners_all))
    target = owners * capacity + slot_rank
    all_slots = lax.broadcasted_iota(jnp.int32, (1, owners_all * capacity), 1)
    matches = target[:, None] == all_slots
    outgoing = jnp.sum(jnp.where(matches, within[:, None], 0), axis=0).reshape(owners_all, capacity)
    wanted = lax.all_to_all(outgoing, ("ty", "tx"), split_axis=0, concat_axis=0, tiled=True)
    wanted = wanted.reshape(-1)

    out = pick_blocks(wanted, cached_keys, cached_values)
    now_keys, now_values, _ = lax.optimization_barrier((keys_now, values_now, wanted))
    paired = jnp.stack([now_keys, now_values])
    row_parts = neighbours(paired, "ty", 2, HALO)
    column = jnp.concatenate(
        [jnp.concatenate([part[..., :HALO, :], part[..., -HALO:, :]], axis=3) for part in
         [paired] + [got for got, _ in row_parts]],
        axis=2,
    )
    column_parts = neighbours(column, "tx", 3, HALO)
    out, column_got = lax.optimization_barrier((out, [got for got, _ in column_parts]))
    column_parts = [(got, ok) for got, (_, ok) in zip(column_got, column_parts)]
    back = lax.all_to_all(
        out.reshape((owners_all, capacity) + out.shape[1:]),
        ("ty", "tx"),
        split_axis=0,
        concat_axis=0,
        tiled=True,
    )
    far_blocks = back.reshape((-1,) + out.shape[1:])

    query_wide = queries.astype(jnp.float32)
    key_wide = keys_now.astype(jnp.float32)
    query_sq, key_sq = lax.psum(
        (jnp.sum(query_wide * query_wide, axis=-1), jnp.sum(key_wide * key_wide, axis=-1)), "ha"
    )

    def normed(wide, squares, gain):
        return (wide * lax.rsqrt(squares / full_width + epsilon)[..., None] * gain).astype(
            jnp.bfloat16
        )

    normed_key = normed(key_wide, key_sq, key_gain)
    normed_query = normed(query_wide, query_sq, query_gain)

    ok_rows = [jnp.ones((tile_rows,), bool)] + [
        jnp.broadcast_to(ok, (HALO,)) for _, ok in row_parts
    ]
    ok_rows = jnp.concatenate(ok_rows)
    margins_k, margins_v = [], []
    oks = [jnp.ones((per_query,), bool)]
    for got, ok in row_parts:
        oks.append(jnp.broadcast_to(ok, (HALO * tile_cols,)))
    for got, ok in column_parts:
        oks.append(jnp.repeat(ok_rows & ok, HALO))
    for got, _ in row_parts + column_parts:
        margins_k.append(got[0].reshape(frames, -1, features).astype(jnp.float32))
        margins_v.append(got[1].reshape(frames, -1, features))
    margin_sq = lax.psum(
        jnp.concatenate([jnp.sum(part * part, axis=-1) for part in margins_k], axis=1), "ha"
    )
    parts_k = [normed_key.reshape(frames, -1, features)]
    at = 0
    for part in margins_k:
        parts_k.append(normed(part, margin_sq[:, at : at + part.shape[1]], key_gain))
        at += part.shape[1]
    parts_v = [values_now.reshape(frames, -1, features)] + margins_v
    bias = jnp.where(jnp.concatenate(oks), 0.0, masked_score).astype(jnp.float32)
    bias = jnp.tile(bias, frames)[None]

    flat_query = normed_query.reshape(frames, per_query, features)
    acc, ml = near_attention(flat_query, parts_k, parts_v, bias)
    padding = (-list_length) % CHUNK
    slots = jnp.pad(target, (0, padding))
    attended = far_attention(flat_query, acc, ml, far_blocks, block_counts, slots)
    return attended.reshape(frames, tile_rows, tile_cols, features)


def share_kernel(rows, cols, depth, lists_ref, sums_ref, all_lists, total_ref, got, send_sem, recv_sem):
    ty, tx, ha = lax.axis_index("ty"), lax.axis_index("tx"), lax.axis_index("ha")
    tiles = rows * cols
    me = ty * cols + tx
    peers = []
    for o in range(1, tiles):
        tile = lax.rem(me + o, tiles)
        peers.append((lax.div(tile, cols), lax.rem(tile, cols), ha))
    for o in range(1, depth):
        peers.append((ty, tx, lax.rem(ha + o, depth)))
    barrier = pltpu.get_barrier_semaphore()
    for peer in peers:
        pl.semaphore_signal(barrier, inc=1, device_id=peer, device_id_type=pl.DeviceIdType.MESH)
    all_lists[me] = lists_ref[...]
    got[0] = sums_ref[...]
    pl.semaphore_wait(barrier, len(peers))
    copies = []
    for i, peer in enumerate(peers):
        if i < tiles - 1:
            src, dst = all_lists.at[me], all_lists.at[me]
        else:
            src, dst = got.at[0], got.at[i - tiles + 2]
        copy = pltpu.make_async_remote_copy(
            src_ref=src,
            dst_ref=dst,
            send_sem=send_sem.at[i],
            recv_sem=recv_sem.at[i],
            device_id=peer,
            device_id_type=pl.DeviceIdType.MESH,
        )
        copy.start()
        copies.append(copy)
    for i, copy in enumerate(copies):
        copy.wait_send()
    for i in range(len(peers)):
        if i < tiles - 1:
            tile = lax.rem(me + 2 * tiles - 1 - i, tiles)
            slot = all_lists.at[tile]
        else:
            slot = got.at[i - tiles + 2]
        pltpu.make_async_copy(slot, slot, recv_sem.at[i]).wait()
    parts = [got[lax.rem(z - ha + depth, depth)] for z in range(depth)]
    total = parts[0]
    for part in parts[1:]:
        total = total + part
    total_ref[...] = total


def share(lists, sums):
    rows, cols, depth = (lax.axis_size(a) for a in ("ty", "tx", "ha"))
    tiles = rows * cols
    vmem = pl.BlockSpec(memory_space=pltpu.VMEM)
    return pl.pallas_call(
        functools.partial(share_kernel, rows, cols, depth),
        in_specs=[vmem, vmem],
        out_specs=[vmem, vmem],
        out_shape=[
            jax.ShapeDtypeStruct((tiles,) + lists.shape, jnp.int32),
            jax.ShapeDtypeStruct(sums.shape, jnp.float32),
        ],
        scratch_shapes=[
            pltpu.VMEM((depth,) + sums.shape, jnp.float32),
            pltpu.SemaphoreType.DMA((tiles + depth - 2,)),
            pltpu.SemaphoreType.DMA((tiles + depth - 2,)),
        ],
        compiler_params=pltpu.CompilerParams(collective_id=0, has_side_effects=True),
        name="share",
    )(lists, sums)


def pack_kernel(sizes, wanted_ref, count_ref, keys_ref, values_ref, *refs):
    outs, sem = refs[: len(sizes)], refs[len(sizes)]
    base = 0
    for part, size in enumerate(sizes):
        out_ref = outs[part]

        def fetch(i, carry, out_ref=out_ref, base=base):
            block = wanted_ref[base + i]
            pltpu.make_async_copy(keys_ref.at[block], out_ref.at[i, 0], sem.at[base + i]).start()
            pltpu.make_async_copy(values_ref.at[block], out_ref.at[i, 1], sem.at[base + i]).start()
            return carry

        lax.fori_loop(0, count_ref[part], fetch, 0)
        base += size
    base = 0
    for part, size in enumerate(sizes):
        out_ref = outs[part]

        def settle(i, carry, out_ref=out_ref, base=base):
            pltpu.make_async_copy(out_ref.at[i], out_ref.at[i], sem.at[base + i]).wait()
            return carry

        lax.fori_loop(0, count_ref[part], settle, 0)
        base += size


def pack(wanted, counts, keys, values, sizes):
    hbm = pl.BlockSpec(memory_space=pl.ANY)
    return pl.pallas_call(
        functools.partial(pack_kernel, sizes),
        grid_spec=pltpu.PrefetchScalarGridSpec(
            num_scalar_prefetch=2,
            grid=(),
            in_specs=[hbm, hbm],
            out_specs=[hbm] * len(sizes),
            scratch_shapes=[pltpu.SemaphoreType.DMA((sum(sizes),))],
        ),
        out_shape=[
            jax.ShapeDtypeStruct((size, 2) + keys.shape[1:], keys.dtype) for size in sizes
        ],
        compiler_params=pltpu.CompilerParams(vmem_limit_bytes=60 << 20),
        cost_estimate=pl.CostEstimate(flops=0, bytes_accessed=16 << 20, transcendentals=0),
        name="pack",
    )(wanted, counts, keys, values)


def edge_kernel(frames, per_query, n_parts, q_ref, acc_in, ml_in, bias_ref, *refs):
    parts_k = refs[:n_parts]
    parts_v = refs[n_parts : 2 * n_parts]
    acc_ref, ml_ref, kbuf, vbuf = refs[2 * n_parts :]
    span = kbuf.shape[0] // frames
    for f in range(frames):
        start = f * span
        for k_ref, v_ref in zip(parts_k, parts_v):
            rows = k_ref.shape[1]
            kbuf[start : start + rows, :] = k_ref[f]
            vbuf[start : start + rows, :HD] = v_ref[f]
            start += rows
    vbuf[:, HD:] = jnp.ones((vbuf.shape[0], HD), jnp.bfloat16)
    for f in range(frames):
        keys = (f + 1) * span
        s = lax.dot_general(
            q_ref[f], kbuf[:keys], (((1,), (1,)), ((), ())), preferred_element_type=jnp.float32
        )
        s = s + bias_ref[:, :keys]
        ml = ml_in[0, f]
        m_old = ml[:, :1]
        m = jnp.maximum(m_old, jnp.max(s, axis=1, keepdims=True) * log2_scale)
        p = jnp.exp2(s * log2_scale - m).astype(jnp.bfloat16)
        o = jnp.dot(p, vbuf[:keys], preferred_element_type=jnp.float32)
        a = jnp.exp2(m_old - m)
        acc_ref[f] = acc_in[f] * a + o[:, :HD]
        lane = lax.broadcasted_iota(jnp.int32, (per_query, HD), 1)
        ml_ref[0, f] = jnp.where(lane < HD // 2, m, ml * a + o[:, HD:])


def own_kernel(frames, per_query, q_ref, k_ref, v_ref, acc_ref, ml_ref, vbuf):
    vbuf[:, HD:] = jnp.ones((vbuf.shape[0], HD), jnp.bfloat16)
    span = k_ref.shape[1]
    vbuf[:, :HD] = v_ref[...].reshape(frames * span, HD)
    kbuf = k_ref[...].reshape(frames * span, HD)
    for f in range(frames):
        keys = (f + 1) * span
        s = lax.dot_general(
            q_ref[f], kbuf[:keys], (((1,), (1,)), ((), ())), preferred_element_type=jnp.float32
        )
        m = jnp.max(s, axis=1, keepdims=True) * log2_scale
        p = jnp.exp2(s * log2_scale - m).astype(jnp.bfloat16)
        o = jnp.dot(p, vbuf[:keys], preferred_element_type=jnp.float32)
        acc_ref[f] = o[:, :HD]
        lane = lax.broadcasted_iota(jnp.int32, (per_query, HD), 1)
        ml_ref[0, f] = jnp.where(lane < HD // 2, m, o[:, HD:])


def state_specs(frames, per_query):
    return [
        pl.BlockSpec((frames, per_query, HD), lambda h, *_: (0, 0, h)),
        pl.BlockSpec((1, frames, per_query, HD), lambda h, *_: (h, 0, 0, 0)),
    ]


def state_shapes(frames, per_query, features):
    return [
        jax.ShapeDtypeStruct((frames, per_query, features), jnp.float32),
        jax.ShapeDtypeStruct((features // HD, frames, per_query, HD), jnp.float32),
    ]


def own_attention(query, key, value):
    frames, per_query, features = query.shape
    heads = features // HD

    def spec(rows):
        return pl.BlockSpec((frames, rows, HD), lambda h: (0, 0, h))

    keys = frames * key.shape[1]
    return pl.pallas_call(
        functools.partial(own_kernel, frames, per_query),
        grid=(heads,),
        in_specs=[spec(per_query), spec(key.shape[1]), spec(key.shape[1])],
        out_specs=state_specs(frames, per_query),
        out_shape=state_shapes(frames, per_query, features),
        scratch_shapes=[pltpu.VMEM((keys, 2 * HD), jnp.bfloat16)],
        compiler_params=pltpu.CompilerParams(vmem_limit_bytes=60 << 20),
        cost_estimate=pl.CostEstimate(
            flops=heads * frames * per_query * keys * HD * 6,
            bytes_accessed=18 << 20,
            transcendentals=heads * frames * per_query * keys,
        ),
        name="own",
    )(query, key, value)


def edge_attention(query, acc, ml, parts_k, parts_v, bias):
    frames, per_query, features = query.shape
    heads = features // HD
    span = sum(part.shape[1] for part in parts_k)

    def spec(rows):
        return pl.BlockSpec((frames, rows, HD), lambda h: (0, 0, h))

    part_specs = [spec(part.shape[1]) for part in parts_k]
    keys = frames * span
    return pl.pallas_call(
        functools.partial(edge_kernel, frames, per_query, len(parts_k)),
        grid=(heads,),
        in_specs=[spec(per_query)]
        + state_specs(frames, per_query)
        + [pl.BlockSpec((1, keys), lambda h: (0, 0))]
        + part_specs
        + part_specs,
        out_specs=state_specs(frames, per_query),
        out_shape=state_shapes(frames, per_query, features),
        scratch_shapes=[
            pltpu.VMEM((keys, HD), jnp.bfloat16),
            pltpu.VMEM((keys, 2 * HD), jnp.bfloat16),
        ],
        compiler_params=pltpu.CompilerParams(vmem_limit_bytes=60 << 20),
        cost_estimate=pl.CostEstimate(
            flops=heads * frames * per_query * keys * HD * 6,
            bytes_accessed=30 << 20,
            transcendentals=heads * frames * per_query * keys,
        ),
        name="edge",
    )(query, acc, ml, bias, *parts_k, *parts_v)


STEP = 8
OWN, SIB, SIDE, ABOVE, RELAY, BELOW = 0, 1, 2, 4, 6, 8


def blocks_kernel(sources, last, frames, per_query, length, code_ref, q_ref, acc_in, ml_in, *refs):
    n_src = len(sources) + (1 if sources[0] == OWN else 0)
    srcs = refs[:n_src]
    refs = refs[n_src:]
    if last:
        out_ref, held, sem, n_ref, m_sc, l_sc, acc_sc = refs
    else:
        acc_ref, ml_ref, held, sem, n_ref, m_sc, l_sc, acc_sc = refs
    head = pl.program_id(0)
    tokens = held.shape[2]

    @pl.when(head == 0)
    def _():
        def fetch(j, n):
            code = code_ref[j]
            source, place = code // 64, code % 64
            hit = jnp.int32(0)
            at = 0
            for name in sources:
                here = source == name
                hit = hit + here.astype(jnp.int32)
                if name == OWN:

                    @pl.when(here)
                    def _(at=at):
                        pltpu.make_async_copy(srcs[at].at[place], held.at[n, 0], sem.at[n]).start()
                        pltpu.make_async_copy(srcs[at + 1].at[place], held.at[n, 1], sem.at[n]).start()

                    at += 2
                else:

                    @pl.when(here)
                    def _(at=at):
                        pltpu.make_async_copy(srcs[at].at[place], held.at[n], sem.at[n]).start()

                    at += 1
            return n + hit

        n = lax.fori_loop(0, length, fetch, jnp.int32(0))
        n_ref[0] = n

        def blank(p, carry):
            held[p] = jnp.zeros(held.shape[1:], held.dtype)
            return carry

        lax.fori_loop(n, (n + STEP - 1) // STEP * STEP, blank, 0)

        def settle(p, carry):
            pltpu.make_async_copy(held.at[p], held.at[p], sem.at[p]).wait()
            return carry

        lax.fori_loop(0, n, settle, 0)

    n = n_ref[0]
    lanes = pl.ds(pl.multiple_of(head * HD, HD), HD)
    ones = jnp.ones((STEP * tokens, HD), jnp.bfloat16)
    for f in range(frames):
        ml = ml_in[0, f]
        m_sc[f] = jnp.broadcast_to(ml[:, :1], (per_query, HD))
        l_sc[f] = jnp.broadcast_to(ml[:, HD // 2 : HD // 2 + 1], (per_query, HD))
        acc_sc[f] = acc_in[f]

    def chunk(c, carry):
        part = pl.ds(c * STEP, STEP)
        k = held[part, 0, :, lanes].reshape(STEP * tokens, HD)
        v = held[part, 1, :, lanes].reshape(STEP * tokens, HD)
        v = jnp.concatenate([v, ones], axis=1)
        place = lax.broadcasted_iota(jnp.int32, (1, STEP * tokens), 1)
        bias = jnp.where(place < (n - c * STEP) * tokens, 0.0, masked_score)
        for f in range(frames):
            s = lax.dot_general(
                q_ref[f], k, (((1,), (1,)), ((), ())), preferred_element_type=jnp.float32
            )
            s = s + bias
            m_old = m_sc[f]
            m_new = jnp.maximum(m_old, jnp.max(s, axis=1, keepdims=True) * log2_scale)
            p = jnp.exp2(s * log2_scale - m_new[:, :1]).astype(jnp.bfloat16)
            o = jnp.dot(p, v, preferred_element_type=jnp.float32)
            a = jnp.exp2(m_old - m_new)
            acc_sc[f] = acc_sc[f] * a + o[:, :HD]
            l_sc[f] = l_sc[f] * a + o[:, HD:]
            m_sc[f] = m_new
        return carry

    lax.fori_loop(0, (n + STEP - 1) // STEP, chunk, 0)
    for f in range(frames):
        if last:
            out_ref[f] = (acc_sc[f] / l_sc[f]).astype(jnp.bfloat16)
        else:
            acc_ref[f] = acc_sc[f]
            lane = lax.broadcasted_iota(jnp.int32, (per_query, HD), 1)
            ml_ref[0, f] = jnp.where(lane < HD // 2, m_sc[f], l_sc[f])


def blocks_attention(codes, query, acc, ml, sources, arrays, last, name):
    frames, per_query, features = query.shape
    heads = features // HD
    length = codes.shape[0]
    tokens = arrays[0].shape[-2]
    most = -(-length // STEP) * STEP
    q_spec = pl.BlockSpec((frames, per_query, HD), lambda h, *_: (0, 0, h))
    if last:
        out_specs = q_spec
        out_shape = jax.ShapeDtypeStruct(query.shape, jnp.bfloat16)
    else:
        out_specs = state_specs(frames, per_query)
        out_shape = state_shapes(frames, per_query, features)
    work = 12 * tokens
    return pl.pallas_call(
        functools.partial(blocks_kernel, sources, last, frames, per_query, length),
        grid_spec=pltpu.PrefetchScalarGridSpec(
            num_scalar_prefetch=1,
            grid=(heads,),
            in_specs=[q_spec]
            + state_specs(frames, per_query)
            + [pl.BlockSpec(memory_space=pl.ANY)] * len(arrays),
            out_specs=out_specs,
            scratch_shapes=[
                pltpu.VMEM((most, 2, tokens, features), jnp.bfloat16),
                pltpu.SemaphoreType.DMA((most,)),
                pltpu.SMEM((1,), jnp.int32),
                pltpu.VMEM((frames, per_query, HD), jnp.float32),
                pltpu.VMEM((frames, per_query, HD), jnp.float32),
                pltpu.VMEM((frames, per_query, HD), jnp.float32),
            ],
        ),
        out_shape=out_shape,
        compiler_params=pltpu.CompilerParams(vmem_limit_bytes=60 << 20),
        cost_estimate=pl.CostEstimate(
            flops=heads * frames * per_query * work * HD * 6,
            bytes_accessed=24 << 20,
            transcendentals=heads * frames * per_query * work,
        ),
        name=name,
    )(codes, query, acc, ml, *arrays)


def count_where(matches, weights=None):
    return jnp.sum(jnp.where(matches, 1 if weights is None else weights, 0), axis=-1).astype(jnp.int32)


def plan(lists, counts, tile, per_tile, cols, capacity):
    tiles, length = lists.shape
    entry = jnp.arange(tiles * length, dtype=jnp.int32)
    to, place = entry // length, entry % length
    valid = place < jnp.repeat(counts, length)
    ids = lists.reshape(-1)
    owner, within = ids // per_tile, ids % per_tile
    far_row = owner // cols != to // cols
    far_col = (owner % cols) // 2 != (to % cols) // 2
    near_kind = jnp.where(owner == to, 0, 1)
    kind = jnp.where(far_row, jnp.where(far_col, 4, 3), jnp.where(far_col, 2, near_kind))
    group = jnp.where(valid, owner * 5 + kind, -1)
    rank = count_where((group[:, None] == group[None, :]) & (entry[None, :] < entry[:, None]))
    groups = jnp.arange(tiles * 5, dtype=jnp.int32)
    sizes = count_where(groups[:, None] == group[None, :]).reshape(tiles, 5)
    diagonal = count_where(
        jnp.arange(tiles, dtype=jnp.int32)[None, :] == owner[:, None], sizes[:, 4][None, :]
    )
    rank = rank + jnp.where(kind == 3, diagonal, 0)
    mine = valid & (owner == tile)
    base = jnp.where(kind >= 3, 0, jnp.where(kind == 2, 4 * capacity, 6 * capacity))
    slot = jnp.where(mine & (kind > 0), base + rank, -1)
    wanted = count_where(
        jnp.arange(7 * capacity, dtype=jnp.int32)[:, None] == slot[None, :], within[None, :]
    )
    mine_sizes = lax.dynamic_index_in_dim(sizes, tile, 0, keepdims=False)
    sends = jnp.stack([mine_sizes[3] + mine_sizes[4], mine_sizes[2], mine_sizes[1]])
    other_core = (owner % 2 != to % 2).astype(jnp.int32)
    source = jnp.where(kind < 2, kind, 2 * kind - 2 + other_core)
    source = jnp.where(kind == 3, ABOVE + other_core, source)
    source = jnp.where(kind == 4, RELAY + other_core, source)
    code = source * 64 + jnp.where(kind == 0, within, rank)
    code = jnp.where(valid, code, 1 << 20)
    code = lax.dynamic_slice_in_dim(code, tile * length, length)
    across = jnp.max(sizes[:, 3] + sizes[:, 4])
    relayed = jnp.max(sizes[:, 4])
    beside = jnp.max(sizes[:, 2])
    return code, wanted, sends, across, relayed, beside


def swap(array, axis, distance):
    count = lax.axis_size(axis)
    return lax.ppermute(array, axis, [(i, i ^ distance) for i in range(count)])


def tied(*arrays):
    return lax.optimization_barrier(arrays)


def local(
    queries,
    keys_now,
    values_now,
    query_gain,
    key_gain,
    cached_keys,
    cached_values,
    block_lists,
    block_counts,
):
    if lax.axis_size("ty") != 2 or lax.axis_size("tx") != 4:
        return general(
            queries,
            keys_now,
            values_now,
            query_gain,
            key_gain,
            cached_keys,
            cached_values,
            block_lists,
            block_counts,
        )
    frames, tile_rows, tile_cols, features = queries.shape
    rows, cols = lax.axis_size("ty"), lax.axis_size("tx")
    tiles = rows * cols
    full_width = features * lax.axis_size("ha")
    per_query = tile_rows * tile_cols
    per_tile = cached_keys.shape[0]
    length = block_lists.shape[1]
    capacity = 4 * length // (3 * tiles)
    row, col = lax.axis_index("ty"), lax.axis_index("tx")
    tile = row * cols + col

    def border(cells):
        return lax.dynamic_slice_in_dim(cells, (1 - row) * (tile_rows - HALO), HALO, axis=1)

    value_rows = swap(border(values_now), "ty", 1)

    query_wide = queries.astype(jnp.float32)
    key_wide = keys_now.astype(jnp.float32)
    squares = jnp.stack(
        [jnp.sum(query_wide * query_wide, axis=-1), jnp.sum(key_wide * key_wide, axis=-1)]
    )
    note = jnp.concatenate([block_lists[0], block_counts])
    note = jnp.pad(note, (0, HD - note.shape[0]))
    note = jnp.broadcast_to(note[None], (8, HD))
    notes, squares = share(note, squares.reshape(-1, HD))
    squares = squares.reshape((2,) + queries.shape[:3])
    lists, counts = notes[:, 0, :length], notes[:, 0, length]

    codes, wanted, sends, across, relayed, beside = plan(
        lists, counts, tile, per_tile, cols, capacity
    )
    for_across, for_beside, for_core = pack(
        wanted, sends, cached_keys, cached_values, (4 * capacity, 2 * capacity, capacity)
    )

    def normed(wide, square, gain):
        return (wide * lax.rsqrt(square / full_width + epsilon)[..., None] * gain).astype(
            jnp.bfloat16
        )

    normed_query = normed(query_wide, squares[0], query_gain)
    normed_key = normed(key_wide, squares[1], key_gain)
    key_border = border(normed_key)

    ok_rows = jnp.concatenate([jnp.ones((tile_rows,), bool), jnp.ones((HALO,), bool)])
    oks = [jnp.ones((HALO * tile_cols,), bool)]
    for ok in (col > 0, col < cols - 1):
        oks.append(jnp.repeat(ok_rows & ok, HALO))
    bias = jnp.where(jnp.concatenate(oks), 0.0, masked_score).astype(jnp.float32)
    bias = jnp.tile(bias, frames)[None]

    def columns(cells, rows_got):
        both = jnp.concatenate([cells, rows_got], axis=1)
        head, tail = both[:, :, :HALO], both[:, :, -HALO:]
        before = lax.ppermute(tail, "tx", [(i, i + 1) for i in range(cols - 1)])
        after = lax.ppermute(head, "tx", [(i + 1, i) for i in range(cols - 1)])
        return [part.reshape(frames, -1, features) for part in (before, after)]

    def rest(sizes, operands):
        n_across, n_relayed, n_beside = sizes
        (
            normed_query,
            normed_key,
            values_now,
            key_border,
            value_rows,
            for_across,
            for_beside,
            for_core,
            cached_keys,
            cached_values,
            codes,
            bias,
        ) = operands
        place = codes % 64
        moved = (codes // 64 >= ABOVE) & (codes // 64 < RELAY) & (place >= n_relayed)
        codes = jnp.where(moved, codes + (BELOW - ABOVE) * 64 - n_relayed, codes)
        first, second = for_across[:n_relayed], for_across[n_relayed:n_across]
        side = for_beside[:n_beside]

        above = swap(first, "ty", 1)
        beside = swap(side, "tx", 2)
        sibling = swap(for_core, "tx", 1)
        query = normed_query.reshape(frames, per_query, features)
        acc, ml = own_attention(
            query,
            normed_key.reshape(frames, per_query, features),
            values_now.reshape(frames, per_query, features),
        )
        value_cols = columns(values_now, value_rows)
        above, key_border = tied(above, key_border)
        key_rows = swap(key_border, "ty", 1)
        relay = swap(above, "tx", 2)
        above_core = swap(above, "tx", 1)
        beside_core = swap(beside, "tx", 1)
        acc, ml = blocks_attention(
            codes,
            query,
            acc,
            ml,
            (OWN, SIB, SIDE, SIDE + 1),
            (cached_keys, cached_values, sibling, beside, beside_core),
            False,
            "blocks_early",
        )
        key_rows, second = tied(key_rows, second)
        below = swap(second, "ty", 1)
        key_cols = columns(normed_key, key_rows)
        parts_k = [key_rows.reshape(frames, -1, features)] + key_cols
        parts_v = [value_rows.reshape(frames, -1, features)] + value_cols
        acc, ml = edge_attention(query, acc, ml, parts_k, parts_v, bias)
        relay_core = swap(relay, "tx", 1)
        below_core = swap(below, "tx", 1)
        return blocks_attention(
            codes,
            query,
            acc,
            ml,
            (ABOVE, ABOVE + 1, RELAY, RELAY + 1, BELOW, BELOW + 1),
            (above, above_core, relay, relay_core, below, below_core),
            True,
            "blocks_late",
        )

    classes = [
        (3 * capacity // 2, capacity + 1, capacity + 1),
        (7 * capacity // 4, capacity + 2, capacity + 2),
        (2 * capacity, 3 * capacity // 2, 3 * capacity // 2),
        (5 * capacity // 2, 2 * capacity, 2 * capacity),
        (4 * capacity, 2 * capacity, 2 * capacity),
    ]
    which = jnp.int32(0)
    for a, r, b in classes[:-1]:
        which = which + ((across > a) | (relayed > r) | (beside > b)).astype(jnp.int32)
    attended = lax.switch(
        which,
        [functools.partial(rest, sizes) for sizes in classes],
        (
            normed_query,
            normed_key,
            values_now,
            key_border,
            value_rows,
            for_across,
            for_beside,
            for_core,
            cached_keys,
            cached_values,
            codes,
            bias,
        ),
    )
    return attended.reshape(frames, tile_rows, tile_cols, features)


def solution(mesh):
    return jax.shard_map(
        local,
        mesh=mesh,
        in_specs=(
            P(None, "ty", "tx", "ha"),
            P(None, "ty", "tx", "ha"),
            P(None, "ty", "tx", "ha"),
            P("ha"),
            P("ha"),
            P(("ty", "tx"), None, "ha"),
            P(("ty", "tx"), None, "ha"),
            P(("ty", "tx"), None),
            P(("ty", "tx")),
        ),
        out_specs=P(None, "ty", "tx", "ha"),
        check_vma=False,
    )
```

```python
import functools
import math

import jax
import jax.numpy as jnp
from jax import lax
from jax.experimental import pallas as pl
from jax.experimental.pallas import tpu as pltpu
from jax.sharding import PartitionSpec as P

HD = 128
HALO = 4
CHUNK = 16

epsilon = 1e-06
masked_score = -1e30
log2_scale = HD ** (-0.5) * math.log2(math.e)


def neighbours(cells, axis, dim, width):
    count = lax.axis_size(axis)
    size = cells.shape[dim]
    head = lax.slice_in_dim(cells, 0, width, axis=dim)
    tail = lax.slice_in_dim(cells, size - width, size, axis=dim)
    where_am_i = lax.axis_index(axis)
    if count == 2:
        mine = jnp.where(where_am_i == 0, tail, head)
        got = lax.ppermute(mine, axis, [(0, 1), (1, 0)])
        return [(got, jnp.bool_(True))]
    ends = count - 1
    before = lax.ppermute(tail, axis, [(i, i + 1) for i in range(ends)])
    after = lax.ppermute(head, axis, [(i + 1, i) for i in range(ends)])
    return [(before, where_am_i > 0), (after, where_am_i < ends)]


def slot_ranks(owners):
    length = owners.shape[-1]
    earlier = lax.broadcasted_iota(jnp.int32, (length, length), 1) < lax.broadcasted_iota(
        jnp.int32, (length, length), 0
    )
    same_owner = owners[..., :, None] == owners[..., None, :]
    return jnp.sum(jnp.where(same_owner & earlier, 1, 0), axis=-1).astype(jnp.int32)


def near_kernel(frames, per_query, n_parts, q_ref, bias_ref, *refs):
    parts_k = refs[:n_parts]
    parts_v = refs[n_parts : 2 * n_parts]
    acc_ref, ml_ref, kbuf, vbuf = refs[2 * n_parts :]
    span = kbuf.shape[0] // frames
    for f in range(frames):
        start = f * span
        for k_ref, v_ref in zip(parts_k, parts_v):
            rows = k_ref.shape[1]
            kbuf[start : start + rows, :] = k_ref[f]
            vbuf[start : start + rows, :HD] = v_ref[f]
            start += rows
    vbuf[:, HD:] = jnp.ones((vbuf.shape[0], HD), jnp.bfloat16)
    for f in range(frames):
        keys = (f + 1) * span
        s = lax.dot_general(
            q_ref[f], kbuf[:keys], (((1,), (1,)), ((), ())), preferred_element_type=jnp.float32
        )
        s = s + bias_ref[:, :keys]
        m = jnp.max(s, axis=1, keepdims=True) * log2_scale
        p = jnp.exp2(s * log2_scale - m).astype(jnp.bfloat16)
        o = jnp.dot(p, vbuf[:keys], preferred_element_type=jnp.float32)
        acc_ref[f] = o[:, :HD]
        lane = lax.broadcasted_iota(jnp.int32, (per_query, HD), 1)
        ml_ref[0, f] = jnp.where(lane < HD // 2, m, o[:, HD:])


def far_kernel(
    frames, per_query, tokens, count_ref, slot_ref, q_ref, acc_in, ml_in, k_ref, v_ref, out_ref,
    kbuf, vbuf, m_sc, l_sc, acc_sc,
):
    count = count_ref[0]
    vbuf[:, HD:] = jnp.ones((vbuf.shape[0], HD), jnp.bfloat16)
    for f in range(frames):
        ml = ml_in[0, f]
        m_sc[f] = jnp.broadcast_to(ml[:, :1], (per_query, HD))
        l_sc[f] = jnp.broadcast_to(ml[:, HD // 2 : HD // 2 + 1], (per_query, HD))
        acc_sc[f] = acc_in[f]

    def chunk(c, carry):
        for i in range(CHUNK):
            slot = slot_ref[c * CHUNK + i]
            kbuf[i * tokens : (i + 1) * tokens, :] = k_ref[slot, 0]
            vbuf[i * tokens : (i + 1) * tokens, :HD] = v_ref[slot, 0]
        place = lax.broadcasted_iota(jnp.int32, (1, CHUNK * tokens), 1)
        bias = jnp.where(place < (count - c * CHUNK) * tokens, 0.0, masked_score)
        for f in range(frames):
            s = lax.dot_general(
                q_ref[f], kbuf[...], (((1,), (1,)), ((), ())), preferred_element_type=jnp.float32
            )
            s = s + bias
            m_old = m_sc[f]
            m_new = jnp.maximum(m_old, jnp.max(s, axis=1, keepdims=True) * log2_scale)
            p = jnp.exp2(s * log2_scale - m_new[:, :1]).astype(jnp.bfloat16)
            o = jnp.dot(p, vbuf[...], preferred_element_type=jnp.float32)
            a = jnp.exp2(m_old - m_new)
            acc_sc[f] = acc_sc[f] * a + o[:, :HD]
            l_sc[f] = l_sc[f] * a + o[:, HD:]
            m_sc[f] = m_new
        return carry

    lax.fori_loop(0, (count + CHUNK - 1) // CHUNK, chunk, 0)
    for f in range(frames):
        out_ref[f] = (acc_sc[f] / l_sc[f]).astype(jnp.bfloat16)


def near_attention(query, parts_k, parts_v, bias):
    frames, per_query, features = query.shape
    heads = features // HD
    span = sum(part.shape[1] for part in parts_k)

    def spec(rows):
        return pl.BlockSpec((frames, rows, HD), lambda h: (0, 0, h))

    part_specs = [spec(part.shape[1]) for part in parts_k]
    keys = frames * span
    return pl.pallas_call(
        functools.partial(near_kernel, frames, per_query, len(parts_k)),
        grid=(heads,),
        in_specs=[spec(per_query), pl.BlockSpec((1, keys), lambda h: (0, 0))]
        + part_specs
        + part_specs,
        out_specs=[
            spec(per_query),
            pl.BlockSpec((1, frames, per_query, HD), lambda h: (h, 0, 0, 0)),
        ],
        out_shape=[
            jax.ShapeDtypeStruct((frames, per_query, features), jnp.float32),
            jax.ShapeDtypeStruct((heads, frames, per_query, HD), jnp.float32),
        ],
        scratch_shapes=[
            pltpu.VMEM((keys, HD), jnp.bfloat16),
            pltpu.VMEM((keys, 2 * HD), jnp.bfloat16),
        ],
        compiler_params=pltpu.CompilerParams(vmem_limit_bytes=60 << 20),
        cost_estimate=pl.CostEstimate(
            flops=heads * frames * per_query * keys * HD * 6,
            bytes_accessed=30 << 20,
            transcendentals=heads * frames * per_query * keys,
        ),
        name="near",
    )(query, bias, *parts_k, *parts_v)


def pick_kernel(total, group, wanted_ref, keys_ref, values_ref, out_ref, held, in_sem, out_sem):
    groups = total // group

    def fetch(i, carry):
        block = wanted_ref[i]
        sem = in_sem.at[i // group]
        pltpu.make_async_copy(keys_ref.at[block], held.at[i, 0], sem).start()
        pltpu.make_async_copy(values_ref.at[block], held.at[i, 1], sem).start()
        return carry

    lax.fori_loop(0, total, fetch, 0)
    for g in range(groups):
        part = pl.ds(g * group, group)
        pltpu.make_async_copy(held.at[part], held.at[part], in_sem.at[g]).wait()
        pltpu.make_async_copy(held.at[part], out_ref.at[part], out_sem.at[g]).start()
    for g in range(groups):
        part = pl.ds(g * group, group)
        pltpu.make_async_copy(held.at[part], out_ref.at[part], out_sem.at[g]).wait()


def pick_blocks(wanted, keys, values):
    total = wanted.shape[0]
    group = 8 if total % 8 == 0 else 1
    shape = (total, 2) + keys.shape[1:]
    return pl.pallas_call(
        functools.partial(pick_kernel, total, group),
        grid_spec=pltpu.PrefetchScalarGridSpec(
            num_scalar_prefetch=1,
            grid=(),
            in_specs=[pl.BlockSpec(memory_space=pl.ANY)] * 2,
            out_specs=pl.BlockSpec(memory_space=pl.ANY),
            scratch_shapes=[
                pltpu.VMEM(shape, keys.dtype),
                pltpu.SemaphoreType.DMA((total // group,)),
                pltpu.SemaphoreType.DMA((total // group,)),
            ],
        ),
        out_shape=jax.ShapeDtypeStruct(shape, keys.dtype),
        compiler_params=pltpu.CompilerParams(vmem_limit_bytes=60 << 20),
        cost_estimate=pl.CostEstimate(flops=0, bytes_accessed=20 << 20, transcendentals=0),
        name="pick",
    )(wanted, keys, values)


def far_attention(query, acc, ml, blocks, count, slots):
    frames, per_query, features = query.shape
    all_slots, _, tokens, width = blocks.shape
    heads = width // HD
    spec = pl.BlockSpec((frames, per_query, HD), lambda h, *_: (0, 0, h))
    k_spec = pl.BlockSpec((all_slots, 1, tokens, HD), lambda h, *_: (0, 0, 0, h))
    v_spec = pl.BlockSpec((all_slots, 1, tokens, HD), lambda h, *_: (0, 1, 0, h))
    return pl.pallas_call(
        functools.partial(far_kernel, frames, per_query, tokens),
        grid_spec=pltpu.PrefetchScalarGridSpec(
            num_scalar_prefetch=2,
            grid=(heads,),
            in_specs=[
                spec,
                spec,
                pl.BlockSpec((1, frames, per_query, HD), lambda h, *_: (h, 0, 0, 0)),
                k_spec,
                v_spec,
            ],
            out_specs=pl.BlockSpec((frames, per_query, HD), lambda h, *_: (0, 0, h)),
            scratch_shapes=[
                pltpu.VMEM((CHUNK * tokens, HD), jnp.bfloat16),
                pltpu.VMEM((CHUNK * tokens, 2 * HD), jnp.bfloat16),
                pltpu.VMEM((frames, per_query, HD), jnp.float32),
                pltpu.VMEM((frames, per_query, HD), jnp.float32),
                pltpu.VMEM((frames, per_query, HD), jnp.float32),
            ],
        ),
        out_shape=jax.ShapeDtypeStruct((frames, per_query, width), jnp.bfloat16),
        compiler_params=pltpu.CompilerParams(vmem_limit_bytes=60 << 20),
        cost_estimate=pl.CostEstimate(
            flops=heads * frames * per_query * 1536 * HD * 6,
            bytes_accessed=30 << 20,
            transcendentals=heads * frames * per_query * 1536,
        ),
        name="far",
    )(count, slots, query, acc, ml, blocks, blocks)


def general(
    queries,
    keys_now,
    values_now,
    query_gain,
    key_gain,
    cached_keys,
    cached_values,
    block_lists,
    block_counts,
):
    frames, tile_rows, tile_cols, features = queries.shape
    owners_all = lax.axis_size("ty") * lax.axis_size("tx")
    full_width = features * lax.axis_size("ha")
    per_query = tile_rows * tile_cols
    per_tile, block_tokens = cached_keys.shape[:2]

    listed = block_lists[0]
    list_length = listed.shape[0]
    owners = listed // per_tile
    within = listed % per_tile
    slot_rank = slot_ranks(owners)
    capacity = max(2, 4 * list_length // (3 * owners_all))
    target = owners * capacity + slot_rank
    all_slots = lax.broadcasted_iota(jnp.int32, (1, owners_all * capacity), 1)
    matches = target[:, None] == all_slots
    outgoing = jnp.sum(jnp.where(matches, within[:, None], 0), axis=0).reshape(owners_all, capacity)
    wanted = lax.all_to_all(outgoing, ("ty", "tx"), split_axis=0, concat_axis=0, tiled=True)
    wanted = wanted.reshape(-1)

    out = pick_blocks(wanted, cached_keys, cached_values)
    now_keys, now_values, _ = lax.optimization_barrier((keys_now, values_now, wanted))
    paired = jnp.stack([now_keys, now_values])
    row_parts = neighbours(paired, "ty", 2, HALO)
    column = jnp.concatenate(
        [jnp.concatenate([part[..., :HALO, :], part[..., -HALO:, :]], axis=3) for part in
         [paired] + [got for got, _ in row_parts]],
        axis=2,
    )
    column_parts = neighbours(column, "tx", 3, HALO)
    out, column_got = lax.optimization_barrier((out, [got for got, _ in column_parts]))
    column_parts = [(got, ok) for got, (_, ok) in zip(column_got, column_parts)]
    back = lax.all_to_all(
        out.reshape((owners_all, capacity) + out.shape[1:]),
        ("ty", "tx"),
        split_axis=0,
        concat_axis=0,
        tiled=True,
    )
    far_blocks = back.reshape((-1,) + out.shape[1:])

    query_wide = queries.astype(jnp.float32)
    key_wide = keys_now.astype(jnp.float32)
    query_sq, key_sq = lax.psum(
        (jnp.sum(query_wide * query_wide, axis=-1), jnp.sum(key_wide * key_wide, axis=-1)), "ha"
    )

    def normed(wide, squares, gain):
        return (wide * lax.rsqrt(squares / full_width + epsilon)[..., None] * gain).astype(
            jnp.bfloat16
        )

    normed_key = normed(key_wide, key_sq, key_gain)
    normed_query = normed(query_wide, query_sq, query_gain)

    ok_rows = [jnp.ones((tile_rows,), bool)] + [
        jnp.broadcast_to(ok, (HALO,)) for _, ok in row_parts
    ]
    ok_rows = jnp.concatenate(ok_rows)
    margins_k, margins_v = [], []
    oks = [jnp.ones((per_query,), bool)]
    for got, ok in row_parts:
        oks.append(jnp.broadcast_to(ok, (HALO * tile_cols,)))
    for got, ok in column_parts:
        oks.append(jnp.repeat(ok_rows & ok, HALO))
    for got, _ in row_parts + column_parts:
        margins_k.append(got[0].reshape(frames, -1, features).astype(jnp.float32))
        margins_v.append(got[1].reshape(frames, -1, features))
    margin_sq = lax.psum(
        jnp.concatenate([jnp.sum(part * part, axis=-1) for part in margins_k], axis=1), "ha"
    )
    parts_k = [normed_key.reshape(frames, -1, features)]
    at = 0
    for part in margins_k:
        parts_k.append(normed(part, margin_sq[:, at : at + part.shape[1]], key_gain))
        at += part.shape[1]
    parts_v = [values_now.reshape(frames, -1, features)] + margins_v
    bias = jnp.where(jnp.concatenate(oks), 0.0, masked_score).astype(jnp.float32)
    bias = jnp.tile(bias, frames)[None]

    flat_query = normed_query.reshape(frames, per_query, features)
    acc, ml = near_attention(flat_query, parts_k, parts_v, bias)
    padding = (-list_length) % CHUNK
    slots = jnp.pad(target, (0, padding))
    attended = far_attention(flat_query, acc, ml, far_blocks, block_counts, slots)
    return attended.reshape(frames, tile_rows, tile_cols, features)


def share_kernel(rows, cols, depth, lists_ref, sums_ref, all_lists, total_ref, got, send_sem, recv_sem):
    ty, tx, ha = lax.axis_index("ty"), lax.axis_index("tx"), lax.axis_index("ha")
    tiles = rows * cols
    me = ty * cols + tx
    peers = []
    for o in range(1, tiles):
        tile = lax.rem(me + o, tiles)
        peers.append((lax.div(tile, cols), lax.rem(tile, cols), ha))
    for o in range(1, depth):
        peers.append((ty, tx, lax.rem(ha + o, depth)))
    barrier = pltpu.get_barrier_semaphore()
    for peer in peers:
        pl.semaphore_signal(barrier, inc=1, device_id=peer, device_id_type=pl.DeviceIdType.MESH)
    all_lists[me] = lists_ref[...]
    got[0] = sums_ref[...]
    pl.semaphore_wait(barrier, len(peers))
    copies = []
    for i, peer in enumerate(peers):
        if i < tiles - 1:
            src, dst = all_lists.at[me], all_lists.at[me]
        else:
            src, dst = got.at[0], got.at[i - tiles + 2]
        copy = pltpu.make_async_remote_copy(
            src_ref=src,
            dst_ref=dst,
            send_sem=send_sem.at[i],
            recv_sem=recv_sem.at[i],
            device_id=peer,
            device_id_type=pl.DeviceIdType.MESH,
        )
        copy.start()
        copies.append(copy)
    for i, copy in enumerate(copies):
        copy.wait_send()
    for i in range(len(peers)):
        if i < tiles - 1:
            tile = lax.rem(me + 2 * tiles - 1 - i, tiles)
            slot = all_lists.at[tile]
        else:
            slot = got.at[i - tiles + 2]
        pltpu.make_async_copy(slot, slot, recv_sem.at[i]).wait()
    parts = [got[lax.rem(z - ha + depth, depth)] for z in range(depth)]
    total = parts[0]
    for part in parts[1:]:
        total = total + part
    total_ref[...] = total


def share(lists, sums):
    rows, cols, depth = (lax.axis_size(a) for a in ("ty", "tx", "ha"))
    tiles = rows * cols
    vmem = pl.BlockSpec(memory_space=pltpu.VMEM)
    return pl.pallas_call(
        functools.partial(share_kernel, rows, cols, depth),
        in_specs=[vmem, vmem],
        out_specs=[vmem, vmem],
        out_shape=[
            jax.ShapeDtypeStruct((tiles,) + lists.shape, jnp.int32),
            jax.ShapeDtypeStruct(sums.shape, jnp.float32),
        ],
        scratch_shapes=[
            pltpu.VMEM((depth,) + sums.shape, jnp.float32),
            pltpu.SemaphoreType.DMA((tiles + depth - 2,)),
            pltpu.SemaphoreType.DMA((tiles + depth - 2,)),
        ],
        compiler_params=pltpu.CompilerParams(collective_id=0, has_side_effects=True),
        name="share",
    )(lists, sums)


def late_heads(heads):
    last = max(1, heads // 5)
    middle = max(1, 3 * heads // 10)
    return [(0, heads - middle - last), (heads - middle - last, middle), (heads - last, last)]


def fused_kernel(sizes, heads, early_ref, late_ref, count_ref, *refs):
    n_across, n_relayed, n_beside, n_core, n_early, n_late = sizes
    (
        q_high, q_low, key, value, key_side, value_side,
        across, beside, core, own,
        out_ref,
        qh, ql, k_own, v_own, k_side, v_side, k_rows, v_rows, k_corner, v_corner, k_give, v_give,
        early, late, kbuf, vbuf, m_sc, l_sc, acc_sc, out_sc,
        load_sem, send_sem, recv_sem, out_sem,
    ) = refs
    ty, tx, ha = lax.axis_index("ty"), lax.axis_index("tx"), lax.axis_index("ha")
    cols = lax.axis_size("tx")
    frames, per_query = qh.shape[:2]
    width = k_rows.shape[1] // HALO
    tokens = early.shape[2]
    opposite = (1 - ty, tx, ha)
    partner = (ty, lax.rem(tx + 2, cols), ha)
    sibling = (ty, tx + 1 - 2 * lax.rem(tx, 2), ha)
    left, right = (ty, tx - 1, ha), (ty, tx + 1, ha)
    has_left, has_right = tx > 0, tx < cols - 1
    mesh_id = pl.DeviceIdType.MESH

    barrier = pltpu.get_barrier_semaphore()
    for peer in (opposite, partner, sibling, (ty, 3 - tx, ha)):
        pl.semaphore_signal(barrier, inc=1, device_id=peer, device_id_type=mesh_id)

    loads = []
    n_slots, n_late_slots = early.shape[0], late.shape[0]
    first_keys = pl.ds(0, tokens)
    local_copies = [
        (q_high, qh),
        (q_low, ql),
        (key, k_own),
        (value, v_own),
        (own, early.at[pl.ds(0, n_core)]),
        (key.at[0, first_keys], early.at[n_slots - 1, 0]),
        (value.at[0, first_keys], early.at[n_slots - 1, 1]),
        (key.at[0, first_keys], late.at[n_late_slots - 1, 0]),
        (value.at[0, first_keys], late.at[n_late_slots - 1, 1]),
    ]
    for i, (src, dst) in enumerate(local_copies):
        copy = pltpu.make_async_copy(src, dst, load_sem.at[i])
        copy.start()
        loads.append(copy)

    pl.semaphore_wait(barrier, 4)

    started = []
    ends = iter(range(64))

    def send(src, dst, peer):
        i = next(ends)
        copy = pltpu.make_async_remote_copy(
            src_ref=src, dst_ref=dst, send_sem=send_sem.at[i], recv_sem=recv_sem.at[i],
            device_id=peer, device_id_type=mesh_id,
        )
        copy.start()
        started.append(copy)
        return copy

    def give_sides(src, dst, side_first, side_last):
        i, j = next(ends), next(ends)

        def to_left():
            return pltpu.make_async_remote_copy(
                src_ref=side_first(src), dst_ref=side_last(dst), send_sem=send_sem.at[i],
                recv_sem=recv_sem.at[i], device_id=left, device_id_type=mesh_id,
            )

        def to_right():
            return pltpu.make_async_remote_copy(
                src_ref=side_last(src), dst_ref=side_first(dst), send_sem=send_sem.at[j],
                recv_sem=recv_sem.at[j], device_id=right, device_id_type=mesh_id,
            )

        @pl.when(has_left)
        def _():
            to_left().start()

        @pl.when(has_right)
        def _():
            to_right().start()

        @pl.when(jnp.logical_not(has_right))
        def _():
            pltpu.make_async_copy(side_last(src), side_last(dst), recv_sem.at[i]).start()

        @pl.when(jnp.logical_not(has_left))
        def _():
            pltpu.make_async_copy(side_first(src), side_first(dst), recv_sem.at[j]).start()

        def wait():
            pltpu.make_async_copy(side_last(dst), side_last(dst), recv_sem.at[i]).wait()
            pltpu.make_async_copy(side_first(dst), side_first(dst), recv_sem.at[j]).wait()

        def settle():
            @pl.when(has_left)
            def _():
                to_left().wait_send()

            @pl.when(has_right)
            def _():
                to_right().wait_send()

        return wait, settle

    def whole(i):
        return lambda ref: ref.at[i]

    above = late.at[pl.ds(0, n_relayed)]
    below = late.at[pl.ds(n_relayed, n_across - n_relayed)]
    got_above = send(across.at[pl.ds(0, n_relayed)], above, opposite)
    k_side_wait, k_side_settle = give_sides(key_side, k_side, whole(0), whole(1))
    v_side_wait, v_side_settle = give_sides(value_side, v_side, whole(0), whole(1))
    got_core = send(core, early.at[pl.ds(n_core, n_core)], sibling)
    beside_at = early.at[pl.ds(2 * n_core, n_beside)]
    got_beside = send(beside.at[pl.ds(0, n_beside)], beside_at, partner)
    got_below = send(across.at[pl.ds(n_relayed, n_across - n_relayed)], below, opposite)
    tile_rows = key.shape[1] // width
    rows = pl.ds((1 - ty) * (tile_rows - HALO), HALO)
    cuts = late_heads(heads)
    got_rows = []
    for first, count in cuts:
        lanes = pl.ds(first * HD, count * HD)
        pair = []
        for src, dst in ((k_own, k_rows), (v_own, v_rows)):
            if src is k_own and first == 0:
                loads[2].wait()
            if src is v_own and first == 0:
                loads[3].wait()
            source = src.at[:, pl.ds((1 - ty) * (tile_rows - HALO) * width, HALO * width), lanes]
            target = dst.at[:, :, lanes]
            pair.append((source, target))
        got_rows.append(pair)
    rows_out = []
    for (first, count), pair in zip(cuts, got_rows):
        rows_out.append([send(source, target, opposite) for source, target in pair])

    loads[0].wait()
    loads[1].wait()
    k_side_wait()
    v_side_wait()

    def lanes_of(h):
        return pl.ds(pl.multiple_of(h * HD, HD), HD)

    left_weight = jnp.where(has_left, 1.0, 0.0)
    right_weight = jnp.where(has_right, 1.0, 0.0)

    def put(at, k, v, weight=None):
        n = k.shape[0]
        kbuf[at : at + n, :] = k
        if weight is None:
            vbuf[at : at + n, :HD] = v
            vbuf[at : at + n, HD:] = jnp.ones((n, HD), jnp.bfloat16)
        else:
            weight = jnp.full((n, HD), weight, jnp.float32).astype(jnp.bfloat16)
            vbuf[at : at + n, :HD] = v * weight
            vbuf[at : at + n, HD:] = weight

    def attend(h, f, keys, first, last=False):
        lanes = lanes_of(h)
        q = jnp.concatenate([qh[f, :, lanes], ql[f, :, lanes]], axis=1)
        k = kbuf[:keys]
        s = lax.dot_general(
            q, jnp.concatenate([k, k], axis=1), (((1,), (1,)), ((), ())),
            preferred_element_type=jnp.float32,
        )
        m = jnp.max(s, axis=1, keepdims=True)
        if not first:
            m_old = m_sc[h, f]
            m = jnp.maximum(m_old, m)
        else:
            m = jnp.broadcast_to(m, (per_query, HD))
        p = jnp.exp2(s - m[:, :1]).astype(jnp.bfloat16)
        o = jnp.dot(p, vbuf[:keys], preferred_element_type=jnp.float32)
        acc, l = o[:, :HD], o[:, HD:]
        if not first:
            a = jnp.exp2(m_old - m)
            acc = acc_sc[h, f] * a + acc
            l = l_sc[h, f] * a + l
        if last:
            out_sc[f, :, lanes] = (acc / l).astype(jnp.bfloat16)
        else:
            m_sc[h, f] = m
            acc_sc[h, f] = acc
            l_sc[h, f] = l

    def own_part(h, carry):
        lanes = lanes_of(h)
        span = per_query + 2 * k_side.shape[2]
        side = k_side.shape[2]
        for f in range(frames):
            at = f * span
            put(at, k_own[f, :, lanes], v_own[f, :, lanes])
            put(at + per_query, k_side[0, f, :, lanes], v_side[0, f, :, lanes], left_weight)
            put(at + per_query + side, k_side[1, f, :, lanes], v_side[1, f, :, lanes], right_weight)
        for f in range(frames):
            attend(h, f, (f + 1) * span, True)
        return carry

    lax.fori_loop(0, heads // 2, own_part, 0)
    got_beside.wait_recv()
    got_beside_core = send(beside_at, early.at[pl.ds(2 * n_core + n_beside, n_beside)], sibling)
    lax.fori_loop(heads // 2, heads, own_part, 0)
    got_above.wait_recv()
    relayed = late.at[pl.ds(2 * n_across, n_relayed)]
    got_relay = send(above, relayed, partner)
    got_above_core = send(above, late.at[pl.ds(n_across, n_relayed)], sibling)

    def blocks_part(pool, slots_ref, n, valid):
        def part(h, carry):
            lanes = lanes_of(h)
            for i in range(n):
                slot = slots_ref[i]
                weight = jnp.where(i < valid, 1.0, 0.0)
                put(i * tokens, pool[slot, 0, :, lanes], pool[slot, 1, :, lanes], weight)
            for f in range(frames):
                attend(h, f, n * tokens, False)
            return carry

        return part

    got_core.wait_recv()
    for copy in loads[4:]:
        copy.wait()
    got_beside_core.wait_recv()
    lax.fori_loop(0, heads, blocks_part(early, early_ref, n_early, count_ref[0]), 0)

    got_below.wait_recv()
    got_below_core = send(
        below, late.at[pl.ds(n_across + n_relayed, n_across - n_relayed)], sibling
    )
    got_relay.wait_recv()
    got_relay_core = send(relayed, late.at[pl.ds(2 * n_across + n_relayed, n_relayed)], sibling)
    got_above_core.wait_recv()
    got_below_core.wait_recv()
    got_relay_core.wait_recv()
    lax.fori_loop(0, heads, blocks_part(late, late_ref, n_late, count_ref[1]), 0)

    def rows_part(h, carry):
        lanes = lanes_of(h)
        body = HALO * width
        edge = HALO * HALO
        span = body + 2 * edge
        for f in range(frames):
            at = f * span
            put(at, k_rows[f, :, lanes], v_rows[f, :, lanes])
            put(at + body, k_corner[0, f, :, lanes], v_corner[0, f, :, lanes], left_weight)
            put(at + body + edge, k_corner[1, f, :, lanes], v_corner[1, f, :, lanes], right_weight)
        for f in range(frames):
            attend(h, f, (f + 1) * span, False, True)
        return carry

    settles = [k_side_settle, v_side_settle]
    outs = []
    for cut, (first, count) in enumerate(cuts):
        for copy in rows_out[cut]:
            copy.wait_recv()

        def cut_corners(h, carry):
            lanes = lanes_of(h)
            for rows_ref, give in ((k_rows, k_give), (v_rows, v_give)):
                for f in range(frames):
                    wide = rows_ref[f, :, lanes].astype(jnp.float32)
                    for side, start in ((0, 0), (1, width - HALO)):
                        cells = [
                            wide[r * width + start : r * width + start + HALO] for r in range(HALO)
                        ]
                        give[side, f, :, lanes] = jnp.concatenate(cells, axis=0).astype(jnp.bfloat16)
            return carry

        lax.fori_loop(first, first + count, cut_corners, 0)
        lanes = pl.ds(first * HD, count * HD)

        def side_of(i, lanes=lanes):
            return lambda ref: ref.at[i, :, :, lanes]

        waits = []
        for give, take in ((k_give, k_corner), (v_give, v_corner)):
            wait, settle = give_sides(give, take, side_of(0), side_of(1))
            waits.append(wait)
            settles.append(settle)
        for wait in waits:
            wait()
        lax.fori_loop(first, first + count, rows_part, 0)
        copy = pltpu.make_async_copy(out_sc.at[:, :, lanes], out_ref.at[:, :, lanes], out_sem.at[cut])
        copy.start()
        outs.append(copy)
    for copy in started:
        copy.wait_send()
    for settle in settles:
        settle()
    for copy in outs:
        copy.wait()

def fused(sizes, number, early_slots, late_slots, valid, arrays):
    n_across, n_relayed, n_beside, n_core, n_early, n_late = sizes
    q_high, _, key, _, key_side, _, across = arrays[:7]
    frames, per_query, features = key.shape
    heads = features // HD
    side = key_side.shape[2]
    tokens = across.shape[2]
    n_rows = per_query * HALO * HALO // side
    kind = jnp.bfloat16
    hbm = pl.BlockSpec(memory_space=pl.ANY)
    smem = pl.BlockSpec(memory_space=pltpu.SMEM)
    n_keys = max(
        frames * (per_query + 2 * side),
        frames * (n_rows + 2 * HALO * HALO),
        n_early * tokens,
        n_late * tokens,
    )
    n_ends = 40
    state = pltpu.VMEM((heads, frames, per_query, HD), jnp.float32)
    corner = pltpu.VMEM((2, frames, HALO * HALO, features), kind)
    scores = heads * frames * per_query * n_keys * 2
    return pl.pallas_call(
        functools.partial(fused_kernel, sizes, heads),
        in_specs=[smem] * 3 + [hbm] * len(arrays),
        out_specs=hbm,
        out_shape=jax.ShapeDtypeStruct(key.shape, kind),
        scratch_shapes=[pltpu.VMEM(key.shape, kind)] * 4
        + [pltpu.VMEM(key_side.shape, kind)] * 2
        + [pltpu.VMEM((frames, n_rows, features), kind)] * 2
        + [corner] * 4
        + [
            pltpu.VMEM((2 * n_core + 2 * n_beside + 1, 2, tokens, features), kind),
            pltpu.VMEM((2 * n_across + 2 * n_relayed + 1, 2, tokens, features), kind),
            pltpu.VMEM((n_keys, HD), kind),
            pltpu.VMEM((n_keys, 2 * HD), kind),
            state,
            state,
            state,
            pltpu.VMEM(key.shape, kind),
            pltpu.SemaphoreType.DMA((9,)),
            pltpu.SemaphoreType.DMA((n_ends,)),
            pltpu.SemaphoreType.DMA((n_ends,)),
            pltpu.SemaphoreType.DMA((3,)),
        ],
        compiler_params=pltpu.CompilerParams(
            collective_id=number, has_side_effects=True, vmem_limit_bytes=62 << 20
        ),
        cost_estimate=pl.CostEstimate(
            flops=scores * HD * 6, bytes_accessed=60 << 20, transcendentals=scores
        ),
        name="fused",
    )(early_slots, late_slots, valid, *arrays)


def pack_kernel(sizes, wanted_ref, count_ref, keys_ref, values_ref, *refs):
    outs, held, in_sem, out_sem = refs[: len(sizes)], *refs[len(sizes) :]

    def each(step):
        base = 0
        for part, size in enumerate(sizes):
            lax.fori_loop(0, count_ref[part], functools.partial(step, outs[part], base), 0)
            base += size

    def fetch(out_ref, base, i, carry):
        block, at = wanted_ref[base + i], base + i
        pltpu.make_async_copy(keys_ref.at[block], held.at[at, 0], in_sem.at[at]).start()
        pltpu.make_async_copy(values_ref.at[block], held.at[at, 1], in_sem.at[at]).start()
        return carry

    def store(out_ref, base, i, carry):
        at = base + i
        pltpu.make_async_copy(held.at[at], held.at[at], in_sem.at[at]).wait()
        pltpu.make_async_copy(held.at[at], out_ref.at[i], out_sem.at[at]).start()
        return carry

    def settle(out_ref, base, i, carry):
        at = base + i
        pltpu.make_async_copy(held.at[at], out_ref.at[i], out_sem.at[at]).wait()
        return carry

    each(fetch)
    each(store)
    each(settle)


def pack(wanted, counts, keys, values, sizes):
    hbm = pl.BlockSpec(memory_space=pl.ANY)
    total = sum(sizes)
    return pl.pallas_call(
        functools.partial(pack_kernel, sizes),
        grid_spec=pltpu.PrefetchScalarGridSpec(
            num_scalar_prefetch=2,
            grid=(),
            in_specs=[hbm, hbm],
            out_specs=[hbm] * len(sizes),
            scratch_shapes=[
                pltpu.VMEM((total, 2) + keys.shape[1:], keys.dtype),
                pltpu.SemaphoreType.DMA((total,)),
                pltpu.SemaphoreType.DMA((total,)),
            ],
        ),
        out_shape=[
            jax.ShapeDtypeStruct((size, 2) + keys.shape[1:], keys.dtype) for size in sizes
        ],
        compiler_params=pltpu.CompilerParams(vmem_limit_bytes=60 << 20),
        cost_estimate=pl.CostEstimate(flops=0, bytes_accessed=16 << 20, transcendentals=0),
        name="pack",
    )(wanted, counts, keys, values)


def count_where(matches, weights=None):
    return jnp.sum(jnp.where(matches, 1 if weights is None else weights, 0), axis=-1).astype(
        jnp.int32
    )


def plan(lists, counts, tile, per_tile, cols, capacity, classes):
    tiles, length = lists.shape
    entry = jnp.arange(tiles * length, dtype=jnp.int32)
    to, place = entry // length, entry % length
    valid = place < jnp.repeat(counts, length)
    ids = lists.reshape(-1)
    owner, within = ids // per_tile, ids % per_tile
    far_row = owner // cols != to // cols
    far_col = (owner % cols) // 2 != (to % cols) // 2
    near_kind = jnp.where(owner == to, 0, 1)
    kind = jnp.where(far_row, jnp.where(far_col, 4, 3), jnp.where(far_col, 2, near_kind))
    group = jnp.where(valid, owner * 5 + kind, -1)
    rank = count_where((group[:, None] == group[None, :]) & (entry[None, :] < entry[:, None]))
    groups = jnp.arange(tiles * 5, dtype=jnp.int32)
    sizes = count_where(groups[:, None] == group[None, :]).reshape(tiles, 5)
    diagonal = count_where(
        jnp.arange(tiles, dtype=jnp.int32)[None, :] == owner[:, None], sizes[:, 4][None, :]
    )
    rank = rank + jnp.where(kind == 3, diagonal, 0)
    base = jnp.where(kind == 2, 4 * capacity, jnp.where(kind == 1, 6 * capacity, 7 * capacity))
    base = jnp.where(kind >= 3, 0, base)
    slot = jnp.where(valid & (owner == tile), base + rank, -1)
    wanted = count_where(
        jnp.arange(8 * capacity, dtype=jnp.int32)[:, None] == slot[None, :], within[None, :]
    )
    mine = lax.dynamic_index_in_dim(sizes, tile, 0, keepdims=False)
    sends = jnp.stack([mine[3] + mine[4], mine[2], mine[1], mine[0]])

    sides = jnp.arange(tiles * 2, dtype=jnp.int32)
    side = jnp.where(valid, to * 2 + far_row, -1)
    halves = jnp.max(count_where(sides[:, None] == side[None, :]).reshape(tiles, 2), axis=0)
    need = jnp.stack(
        [
            jnp.max(sizes[:, 3] + sizes[:, 4]),
            jnp.max(sizes[:, 4]),
            jnp.max(sizes[:, 2]),
            jnp.max(sizes[:, :2]),
            halves[0],
            halves[1],
        ]
    )
    limits = jnp.array(classes, jnp.int32)
    fits = jnp.all(need[None, :] <= limits, axis=1)
    which = jnp.sum(jnp.logical_not(fits)).astype(jnp.int32)
    n_across, n_relayed, n_beside = (
        jnp.sum(jnp.where(jnp.arange(len(classes)) == which, limits[:, i], 0)).astype(jnp.int32)
        for i in range(3)
    )

    def here(values):
        return lax.dynamic_slice_in_dim(values, tile * length, length)

    kind, rank, valid, far_row = here(kind), here(rank), here(valid), here(far_row)
    other_core = here(owner) % 2 != tile % 2
    early = jnp.where(kind == 0, 0, capacity)
    early = jnp.where(kind == 2, 2 * capacity + jnp.where(other_core, n_beside, 0), early) + rank
    late = jnp.where(kind == 3, 0, 2 * n_across)
    late = late + jnp.where(other_core, jnp.where(kind == 3, n_across, n_relayed), 0) + rank
    at = jnp.arange(length, dtype=jnp.int32)

    def table(member, slots, blank):
        member = member & valid
        order = count_where(member[None, :] & (at[None, :] < at[:, None]))
        found = count_where(
            member[None, :] & (order[None, :] == at[:, None]), slots[None, :] + 1
        )
        return jnp.where(found > 0, found - 1, blank), jnp.sum(member).astype(jnp.int32)

    early_slots, early_count = table(~far_row, early, 2 * capacity + 2 * n_beside)
    late_slots, late_count = table(far_row, late, 2 * n_across + 2 * n_relayed)
    return wanted, sends, which, early_slots, late_slots, jnp.stack([early_count, late_count])


def rounded(values):
    return lax.reduce_precision(values, 8, 7)


def local(*args):
    if lax.axis_size("ty") != 2 or lax.axis_size("tx") != 4:
        return general(*args)
    queries, keys_now, values_now, query_gain, key_gain = args[:5]
    cached_keys, cached_values, block_lists, block_counts = args[5:]
    frames, tile_rows, tile_cols, features = queries.shape
    rows, cols = lax.axis_size("ty"), lax.axis_size("tx")
    tiles = rows * cols
    full_width = features * lax.axis_size("ha")
    per_query = tile_rows * tile_cols
    per_tile = cached_keys.shape[0]
    length = block_lists.shape[1]
    capacity = 4 * length // (3 * tiles)
    tile = lax.axis_index("ty") * cols + lax.axis_index("tx")

    query_wide = queries.astype(jnp.float32)
    key_wide = keys_now.astype(jnp.float32)
    squares = jnp.stack(
        [jnp.sum(query_wide * query_wide, axis=-1), jnp.sum(key_wide * key_wide, axis=-1)]
    )
    note = jnp.concatenate([block_lists[0], block_counts])
    note = jnp.pad(note, (0, HD - note.shape[0]))
    note = jnp.broadcast_to(note[None], (8, HD))
    notes, squares = share(note, squares.reshape(-1, HD))
    squares = squares.reshape((2,) + queries.shape[:3])
    lists, counts = notes[:, 0, :length], notes[:, 0, length]

    c = capacity
    classes = [
        (3 * c // 2, c + 1, c + 2, c, 7 * c // 2, 7 * c // 2),
        (7 * c // 4, c + 2, c + 2, c, 7 * c // 2, 7 * c // 2),
        (2 * c, 3 * c // 2, 3 * c // 2, c, 4 * c, 4 * c),
        (5 * c // 2, 7 * c // 4, 7 * c // 4, c, 4 * c, 4 * c),
    ]
    wanted, sends, which, early_slots, late_slots, valid = plan(
        lists, counts, tile, per_tile, cols, capacity, classes
    )
    packed = pack(wanted, sends, cached_keys, cached_values, (4 * c, 2 * c, c, c))

    def normed(wide, square, gain):
        return rounded(wide * lax.rsqrt(square / full_width + epsilon)[..., None] * gain)

    flat = (frames, per_query, features)
    query = normed(query_wide, squares[0], query_gain).reshape(flat) * log2_scale
    query_high = rounded(query)
    query_low = (query - query_high).astype(jnp.bfloat16)
    query_high = query_high.astype(jnp.bfloat16)
    key = normed(key_wide, squares[1], key_gain).astype(jnp.bfloat16)

    def sides(cells):
        both = jnp.stack([cells[:, :, :HALO], cells[:, :, -HALO:]])
        return both.reshape(2, frames, tile_rows * HALO, features)

    arrays = [
        query_high,
        query_low,
        key.reshape(flat),
        values_now.reshape(flat),
        sides(key),
        sides(values_now),
        *packed,
    ]

    def send(number, operands):
        early_slots, late_slots, valid, arrays, _ = operands
        sizes = classes[number]
        out = fused(
            sizes, number + 1, early_slots[: sizes[4]], late_slots[: sizes[5]], valid, arrays
        )
        return out.reshape(queries.shape)

    def plain(operands):
        return general(*operands[-1])

    branches = [functools.partial(send, number) for number in range(len(classes))] + [plain]
    return lax.switch(which, branches, (early_slots, late_slots, valid, arrays, args))


def solution(mesh):
    return jax.shard_map(
        local,
        mesh=mesh,
        in_specs=(
            P(None, "ty", "tx", "ha"),
            P(None, "ty", "tx", "ha"),
            P(None, "ty", "tx", "ha"),
            P("ha"),
            P("ha"),
            P(("ty", "tx"), None, "ha"),
            P(("ty", "tx"), None, "ha"),
            P(("ty", "tx"), None),
            P(("ty", "tx")),
        ),
        out_specs=P(None, "ty", "tx", "ha"),
        check_vma=False,
    )
```

```python
import functools
import math

import jax
import jax.numpy as jnp
from jax import lax
from jax.experimental import pallas as pl
from jax.experimental.pallas import tpu as pltpu
from jax.sharding import PartitionSpec as P

HD = 128
HALO = 4
CHUNK = 16

epsilon = 1e-06
masked_score = -1e30
log2_scale = HD ** (-0.5) * math.log2(math.e)


def neighbours(cells, axis, dim, width):
    count = lax.axis_size(axis)
    size = cells.shape[dim]
    head = lax.slice_in_dim(cells, 0, width, axis=dim)
    tail = lax.slice_in_dim(cells, size - width, size, axis=dim)
    where_am_i = lax.axis_index(axis)
    if count == 2:
        mine = jnp.where(where_am_i == 0, tail, head)
        got = lax.ppermute(mine, axis, [(0, 1), (1, 0)])
        return [(got, jnp.bool_(True))]
    ends = count - 1
    before = lax.ppermute(tail, axis, [(i, i + 1) for i in range(ends)])
    after = lax.ppermute(head, axis, [(i + 1, i) for i in range(ends)])
    return [(before, where_am_i > 0), (after, where_am_i < ends)]


def slot_ranks(owners):
    length = owners.shape[-1]
    earlier = lax.broadcasted_iota(jnp.int32, (length, length), 1) < lax.broadcasted_iota(
        jnp.int32, (length, length), 0
    )
    same_owner = owners[..., :, None] == owners[..., None, :]
    return jnp.sum(jnp.where(same_owner & earlier, 1, 0), axis=-1).astype(jnp.int32)


def near_kernel(frames, per_query, n_parts, q_ref, bias_ref, *refs):
    parts_k = refs[:n_parts]
    parts_v = refs[n_parts : 2 * n_parts]
    acc_ref, ml_ref, kbuf, vbuf = refs[2 * n_parts :]
    span = kbuf.shape[0] // frames
    for f in range(frames):
        start = f * span
        for k_ref, v_ref in zip(parts_k, parts_v):
            rows = k_ref.shape[1]
            kbuf[start : start + rows, :] = k_ref[f]
            vbuf[start : start + rows, :HD] = v_ref[f]
            start += rows
    vbuf[:, HD:] = jnp.ones((vbuf.shape[0], HD), jnp.bfloat16)
    for f in range(frames):
        keys = (f + 1) * span
        s = lax.dot_general(
            q_ref[f], kbuf[:keys], (((1,), (1,)), ((), ())), preferred_element_type=jnp.float32
        )
        s = s + bias_ref[:, :keys]
        m = jnp.max(s, axis=1, keepdims=True) * log2_scale
        p = jnp.exp2(s * log2_scale - m).astype(jnp.bfloat16)
        o = jnp.dot(p, vbuf[:keys], preferred_element_type=jnp.float32)
        acc_ref[f] = o[:, :HD]
        lane = lax.broadcasted_iota(jnp.int32, (per_query, HD), 1)
        ml_ref[0, f] = jnp.where(lane < HD // 2, m, o[:, HD:])


def far_kernel(
    frames, per_query, tokens, count_ref, slot_ref, q_ref, acc_in, ml_in, k_ref, v_ref, out_ref,
    kbuf, vbuf, m_sc, l_sc, acc_sc,
):
    count = count_ref[0]
    vbuf[:, HD:] = jnp.ones((vbuf.shape[0], HD), jnp.bfloat16)
    for f in range(frames):
        ml = ml_in[0, f]
        m_sc[f] = jnp.broadcast_to(ml[:, :1], (per_query, HD))
        l_sc[f] = jnp.broadcast_to(ml[:, HD // 2 : HD // 2 + 1], (per_query, HD))
        acc_sc[f] = acc_in[f]

    def chunk(c, carry):
        for i in range(CHUNK):
            slot = slot_ref[c * CHUNK + i]
            kbuf[i * tokens : (i + 1) * tokens, :] = k_ref[slot, 0]
            vbuf[i * tokens : (i + 1) * tokens, :HD] = v_ref[slot, 0]
        place = lax.broadcasted_iota(jnp.int32, (1, CHUNK * tokens), 1)
        bias = jnp.where(place < (count - c * CHUNK) * tokens, 0.0, masked_score)
        for f in range(frames):
            s = lax.dot_general(
                q_ref[f], kbuf[...], (((1,), (1,)), ((), ())), preferred_element_type=jnp.float32
            )
            s = s + bias
            m_old = m_sc[f]
            m_new = jnp.maximum(m_old, jnp.max(s, axis=1, keepdims=True) * log2_scale)
            p = jnp.exp2(s * log2_scale - m_new[:, :1]).astype(jnp.bfloat16)
            o = jnp.dot(p, vbuf[...], preferred_element_type=jnp.float32)
            a = jnp.exp2(m_old - m_new)
            acc_sc[f] = acc_sc[f] * a + o[:, :HD]
            l_sc[f] = l_sc[f] * a + o[:, HD:]
            m_sc[f] = m_new
        return carry

    lax.fori_loop(0, (count + CHUNK - 1) // CHUNK, chunk, 0)
    for f in range(frames):
        out_ref[f] = (acc_sc[f] / l_sc[f]).astype(jnp.bfloat16)


def near_attention(query, parts_k, parts_v, bias):
    frames, per_query, features = query.shape
    heads = features // HD
    span = sum(part.shape[1] for part in parts_k)

    def spec(rows):
        return pl.BlockSpec((frames, rows, HD), lambda h: (0, 0, h))

    part_specs = [spec(part.shape[1]) for part in parts_k]
    keys = frames * span
    return pl.pallas_call(
        functools.partial(near_kernel, frames, per_query, len(parts_k)),
        grid=(heads,),
        in_specs=[spec(per_query), pl.BlockSpec((1, keys), lambda h: (0, 0))]
        + part_specs
        + part_specs,
        out_specs=[
            spec(per_query),
            pl.BlockSpec((1, frames, per_query, HD), lambda h: (h, 0, 0, 0)),
        ],
        out_shape=[
            jax.ShapeDtypeStruct((frames, per_query, features), jnp.float32),
            jax.ShapeDtypeStruct((heads, frames, per_query, HD), jnp.float32),
        ],
        scratch_shapes=[
            pltpu.VMEM((keys, HD), jnp.bfloat16),
            pltpu.VMEM((keys, 2 * HD), jnp.bfloat16),
        ],
        compiler_params=pltpu.CompilerParams(vmem_limit_bytes=60 << 20),
        cost_estimate=pl.CostEstimate(
            flops=heads * frames * per_query * keys * HD * 6,
            bytes_accessed=30 << 20,
            transcendentals=heads * frames * per_query * keys,
        ),
        name="near",
    )(query, bias, *parts_k, *parts_v)


def pick_kernel(total, group, wanted_ref, keys_ref, values_ref, out_ref, held, in_sem, out_sem):
    groups = total // group

    def fetch(i, carry):
        block = wanted_ref[i]
        sem = in_sem.at[i // group]
        pltpu.make_async_copy(keys_ref.at[block], held.at[i, 0], sem).start()
        pltpu.make_async_copy(values_ref.at[block], held.at[i, 1], sem).start()
        return carry

    lax.fori_loop(0, total, fetch, 0)
    for g in range(groups):
        part = pl.ds(g * group, group)
        pltpu.make_async_copy(held.at[part], held.at[part], in_sem.at[g]).wait()
        pltpu.make_async_copy(held.at[part], out_ref.at[part], out_sem.at[g]).start()
    for g in range(groups):
        part = pl.ds(g * group, group)
        pltpu.make_async_copy(held.at[part], out_ref.at[part], out_sem.at[g]).wait()


def pick_blocks(wanted, keys, values):
    total = wanted.shape[0]
    group = 8 if total % 8 == 0 else 1
    shape = (total, 2) + keys.shape[1:]
    return pl.pallas_call(
        functools.partial(pick_kernel, total, group),
        grid_spec=pltpu.PrefetchScalarGridSpec(
            num_scalar_prefetch=1,
            grid=(),
            in_specs=[pl.BlockSpec(memory_space=pl.ANY)] * 2,
            out_specs=pl.BlockSpec(memory_space=pl.ANY),
            scratch_shapes=[
                pltpu.VMEM(shape, keys.dtype),
                pltpu.SemaphoreType.DMA((total // group,)),
                pltpu.SemaphoreType.DMA((total // group,)),
            ],
        ),
        out_shape=jax.ShapeDtypeStruct(shape, keys.dtype),
        compiler_params=pltpu.CompilerParams(vmem_limit_bytes=60 << 20),
        cost_estimate=pl.CostEstimate(flops=0, bytes_accessed=20 << 20, transcendentals=0),
        name="pick",
    )(wanted, keys, values)


def far_attention(query, acc, ml, blocks, count, slots):
    frames, per_query, features = query.shape
    all_slots, _, tokens, width = blocks.shape
    heads = width // HD
    spec = pl.BlockSpec((frames, per_query, HD), lambda h, *_: (0, 0, h))
    k_spec = pl.BlockSpec((all_slots, 1, tokens, HD), lambda h, *_: (0, 0, 0, h))
    v_spec = pl.BlockSpec((all_slots, 1, tokens, HD), lambda h, *_: (0, 1, 0, h))
    return pl.pallas_call(
        functools.partial(far_kernel, frames, per_query, tokens),
        grid_spec=pltpu.PrefetchScalarGridSpec(
            num_scalar_prefetch=2,
            grid=(heads,),
            in_specs=[
                spec,
                spec,
                pl.BlockSpec((1, frames, per_query, HD), lambda h, *_: (h, 0, 0, 0)),
                k_spec,
                v_spec,
            ],
            out_specs=pl.BlockSpec((frames, per_query, HD), lambda h, *_: (0, 0, h)),
            scratch_shapes=[
                pltpu.VMEM((CHUNK * tokens, HD), jnp.bfloat16),
                pltpu.VMEM((CHUNK * tokens, 2 * HD), jnp.bfloat16),
                pltpu.VMEM((frames, per_query, HD), jnp.float32),
                pltpu.VMEM((frames, per_query, HD), jnp.float32),
                pltpu.VMEM((frames, per_query, HD), jnp.float32),
            ],
        ),
        out_shape=jax.ShapeDtypeStruct((frames, per_query, width), jnp.bfloat16),
        compiler_params=pltpu.CompilerParams(vmem_limit_bytes=60 << 20),
        cost_estimate=pl.CostEstimate(
            flops=heads * frames * per_query * 1536 * HD * 6,
            bytes_accessed=30 << 20,
            transcendentals=heads * frames * per_query * 1536,
        ),
        name="far",
    )(count, slots, query, acc, ml, blocks, blocks)


def general(
    queries,
    keys_now,
    values_now,
    query_gain,
    key_gain,
    cached_keys,
    cached_values,
    block_lists,
    block_counts,
):
    frames, tile_rows, tile_cols, features = queries.shape
    owners_all = lax.axis_size("ty") * lax.axis_size("tx")
    full_width = features * lax.axis_size("ha")
    per_query = tile_rows * tile_cols
    per_tile, block_tokens = cached_keys.shape[:2]

    listed = block_lists[0]
    list_length = listed.shape[0]
    owners = listed // per_tile
    within = listed % per_tile
    slot_rank = slot_ranks(owners)
    capacity = max(2, 4 * list_length // (3 * owners_all))
    target = owners * capacity + slot_rank
    all_slots = lax.broadcasted_iota(jnp.int32, (1, owners_all * capacity), 1)
    matches = target[:, None] == all_slots
    outgoing = jnp.sum(jnp.where(matches, within[:, None], 0), axis=0).reshape(owners_all, capacity)
    wanted = lax.all_to_all(outgoing, ("ty", "tx"), split_axis=0, concat_axis=0, tiled=True)
    wanted = wanted.reshape(-1)

    out = pick_blocks(wanted, cached_keys, cached_values)
    now_keys, now_values, _ = lax.optimization_barrier((keys_now, values_now, wanted))
    paired = jnp.stack([now_keys, now_values])
    row_parts = neighbours(paired, "ty", 2, HALO)
    column = jnp.concatenate(
        [jnp.concatenate([part[..., :HALO, :], part[..., -HALO:, :]], axis=3) for part in
         [paired] + [got for got, _ in row_parts]],
        axis=2,
    )
    column_parts = neighbours(column, "tx", 3, HALO)
    out, column_got = lax.optimization_barrier((out, [got for got, _ in column_parts]))
    column_parts = [(got, ok) for got, (_, ok) in zip(column_got, column_parts)]
    back = lax.all_to_all(
        out.reshape((owners_all, capacity) + out.shape[1:]),
        ("ty", "tx"),
        split_axis=0,
        concat_axis=0,
        tiled=True,
    )
    far_blocks = back.reshape((-1,) + out.shape[1:])

    query_wide = queries.astype(jnp.float32)
    key_wide = keys_now.astype(jnp.float32)
    query_sq, key_sq = lax.psum(
        (jnp.sum(query_wide * query_wide, axis=-1), jnp.sum(key_wide * key_wide, axis=-1)), "ha"
    )

    def normed(wide, squares, gain):
        return (wide * lax.rsqrt(squares / full_width + epsilon)[..., None] * gain).astype(
            jnp.bfloat16
        )

    normed_key = normed(key_wide, key_sq, key_gain)
    normed_query = normed(query_wide, query_sq, query_gain)

    ok_rows = [jnp.ones((tile_rows,), bool)] + [
        jnp.broadcast_to(ok, (HALO,)) for _, ok in row_parts
    ]
    ok_rows = jnp.concatenate(ok_rows)
    margins_k, margins_v = [], []
    oks = [jnp.ones((per_query,), bool)]
    for got, ok in row_parts:
        oks.append(jnp.broadcast_to(ok, (HALO * tile_cols,)))
    for got, ok in column_parts:
        oks.append(jnp.repeat(ok_rows & ok, HALO))
    for got, _ in row_parts + column_parts:
        margins_k.append(got[0].reshape(frames, -1, features).astype(jnp.float32))
        margins_v.append(got[1].reshape(frames, -1, features))
    margin_sq = lax.psum(
        jnp.concatenate([jnp.sum(part * part, axis=-1) for part in margins_k], axis=1), "ha"
    )
    parts_k = [normed_key.reshape(frames, -1, features)]
    at = 0
    for part in margins_k:
        parts_k.append(normed(part, margin_sq[:, at : at + part.shape[1]], key_gain))
        at += part.shape[1]
    parts_v = [values_now.reshape(frames, -1, features)] + margins_v
    bias = jnp.where(jnp.concatenate(oks), 0.0, masked_score).astype(jnp.float32)
    bias = jnp.tile(bias, frames)[None]

    flat_query = normed_query.reshape(frames, per_query, features)
    acc, ml = near_attention(flat_query, parts_k, parts_v, bias)
    padding = (-list_length) % CHUNK
    slots = jnp.pad(target, (0, padding))
    attended = far_attention(flat_query, acc, ml, far_blocks, block_counts, slots)
    return attended.reshape(frames, tile_rows, tile_cols, features)


def share_kernel(rows, cols, count_ref, list_ref, notes_ref, send_sem, recv_sem):
    ty, tx, ha = lax.axis_index("ty"), lax.axis_index("tx"), lax.axis_index("ha")
    tiles = rows * cols
    me = ty * cols + tx
    peers = []
    for o in range(1, tiles):
        tile = lax.rem(me + o, tiles)
        peers.append((lax.div(tile, cols), lax.rem(tile, cols), ha))
    barrier = pltpu.get_barrier_semaphore()
    for peer in peers:
        pl.semaphore_signal(barrier, inc=1, device_id=peer, device_id_type=pl.DeviceIdType.MESH)
    notes_ref[me] = jnp.full(notes_ref.shape[1:], count_ref[0], jnp.int32)
    notes_ref[me, :, : list_ref.shape[1]] = list_ref[...]
    pl.semaphore_wait(barrier, tiles - 1)
    copies = []
    for i, peer in enumerate(peers):
        copy = pltpu.make_async_remote_copy(
            src_ref=notes_ref.at[me],
            dst_ref=notes_ref.at[me],
            send_sem=send_sem.at[i],
            recv_sem=recv_sem.at[i],
            device_id=peer,
            device_id_type=pl.DeviceIdType.MESH,
        )
        copy.start()
        copies.append(copy)
    for copy in copies:
        copy.wait_send()
    for i in range(tiles - 1):
        slot = notes_ref.at[lax.rem(me + 2 * tiles - 1 - i, tiles)]
        pltpu.make_async_copy(slot, slot, recv_sem.at[i]).wait()


def share(block_lists, block_counts):
    rows, cols = lax.axis_size("ty"), lax.axis_size("tx")
    tiles = rows * cols
    vmem = pl.BlockSpec(memory_space=pltpu.VMEM)
    return pl.pallas_call(
        functools.partial(share_kernel, rows, cols),
        in_specs=[pl.BlockSpec(memory_space=pltpu.SMEM), vmem],
        out_specs=vmem,
        out_shape=jax.ShapeDtypeStruct((tiles, 1, HD), jnp.int32),
        scratch_shapes=[pltpu.SemaphoreType.DMA((tiles - 1,))] * 2,
        compiler_params=pltpu.CompilerParams(collective_id=0, has_side_effects=True),
        name="share",
    )(block_counts, block_lists)


def plan_kernel(
    sizes, classes, length, per_tile, notes_ref, keys_ref, values_ref, across, beside, core, own,
    early_ref, late_ref, facts_ref, held, in_sem, out_sem, number_ref, slot_ref,
):
    tiles = notes_ref.shape[0]
    cols = lax.axis_size("tx")
    me = lax.axis_index("ty") * cols + lax.axis_index("tx")
    capacity = sizes[3]
    shift = per_tile.bit_length() - 1

    def owner_of(block):
        return lax.shift_right_logical(block, shift) if per_tile == 1 << shift else block // per_tile

    def pair(tile):
        return tile - lax.rem(tile, 2)

    def clear(i, carry):
        number_ref[i] = 0
        return carry

    lax.fori_loop(0, tiles * tiles, clear, 0)

    sections = [
        (0, (pair(me ^ 6), pair(me ^ 6) + 1, pair(me ^ 4), pair(me ^ 4) + 1)),
        (sizes[0], (pair(me ^ 2), pair(me ^ 2) + 1)),
        (sizes[0] + sizes[1], (me ^ 1,)),
        (sizes[0] + sizes[1] + sizes[2], (me,)),
    ]
    counts = []
    for start, targets in sections:
        at = jnp.int32(start)
        for target in targets:

            def scan(j, at, target=target):
                block = notes_ref[target, 0, j]
                owner = owner_of(block)
                cell = owner * tiles + target
                number_ref[cell] = number_ref[cell] + 1
                mine = owner == me

                @pl.when(mine)
                def _():
                    here = block - me * per_tile
                    pltpu.make_async_copy(keys_ref.at[here], held.at[at, 0], in_sem.at[at]).start()
                    pltpu.make_async_copy(values_ref.at[here], held.at[at, 1], in_sem.at[at]).start()

                return at + mine.astype(jnp.int32)

            at = lax.fori_loop(0, notes_ref[target, 0, length], scan, at)
        counts.append(at - start)

    for (start, _), count, out_ref in zip(sections, counts, (across, beside, core, own)):

        def store(i, carry, start=start, out_ref=out_ref):
            at = start + i
            pltpu.make_async_copy(held.at[at], held.at[at], in_sem.at[at]).wait()
            pltpu.make_async_copy(held.at[at], out_ref.at[i], out_sem.at[at]).start()
            return carry

        lax.fori_loop(0, count, store, 0)

    def number(owner, target):
        return number_ref[owner * tiles + target]

    def both(owner, target):
        return number(owner, target) + number(owner, target + 1)

    def most(owner, carry):
        diagonal = both(owner, pair(owner ^ 6))
        most_across, most_diagonal, most_beside = carry
        return (
            jnp.maximum(most_across, diagonal + both(owner, pair(owner ^ 4))),
            jnp.maximum(most_diagonal, diagonal),
            jnp.maximum(most_beside, both(owner, pair(owner ^ 2))),
        )

    need = lax.fori_loop(0, tiles, most, (jnp.int32(0),) * 3)
    which = jnp.int32(0)
    for limits in classes:
        short = (need[0] > limits[0]) | (need[1] > limits[1]) | (need[2] > limits[2])
        which = which + short.astype(jnp.int32)
    n_across, n_relayed, n_beside = (jnp.int32(classes[-1][i]) for i in range(3))
    for i, limits in reversed(list(enumerate(classes))):
        n_across = jnp.where(which == i, limits[0], n_across)
        n_relayed = jnp.where(which == i, limits[1], n_relayed)
        n_beside = jnp.where(which == i, limits[2], n_beside)

    def place(owner, carry):
        flip = owner ^ me
        other = lax.rem(flip, 2)
        before = jnp.where(lax.rem(me, 2) == 1, number(owner, pair(me)), 0)
        diagonal = both(owner, pair(owner ^ 6))
        near = jnp.where(flip == 0, 0, capacity)
        early = jnp.where(flip >= 2, 2 * capacity + other * n_beside + before, near)
        straight = other * n_across + diagonal + before
        turned = 2 * n_across + other * n_relayed + before
        late = jnp.where(flip >= 6, turned, straight)
        slot_ref[owner] = jnp.where(flip >= 4, late, early)
        return carry

    lax.fori_loop(0, tiles, place, 0)

    def blank(i, carry):
        early_ref[i] = 2 * capacity + 2 * n_beside
        late_ref[i] = 2 * n_across + 2 * n_relayed
        return carry

    lax.fori_loop(0, 4 * capacity, blank, 0)

    def point(j, carry):
        n_early, n_late = carry
        owner = owner_of(notes_ref[me, 0, j])
        slot = slot_ref[owner]
        slot_ref[owner] = slot + 1
        far = (owner ^ me) >= 4

        @pl.when(far)
        def _():
            late_ref[n_late] = slot

        @pl.when(jnp.logical_not(far))
        def _():
            early_ref[n_early] = slot

        step = far.astype(jnp.int32)
        return n_early + 1 - step, n_late + step

    n_early, n_late = lax.fori_loop(
        0, notes_ref[me, 0, length], point, (jnp.int32(0), jnp.int32(0))
    )
    facts_ref[0] = n_early
    facts_ref[1] = n_late
    facts_ref[2] = which

    for (start, _), count, out_ref in zip(sections, counts, (across, beside, core, own)):

        def settle(i, carry, start=start, out_ref=out_ref):
            at = start + i
            pltpu.make_async_copy(held.at[at], out_ref.at[i], out_sem.at[at]).wait()
            return carry

        lax.fori_loop(0, count, settle, 0)


def plan(notes, keys, values, capacity, classes, length):
    hbm = pl.BlockSpec(memory_space=pl.ANY)
    smem = pl.BlockSpec(memory_space=pltpu.SMEM)
    sizes = (4 * capacity, 2 * capacity, capacity, capacity)
    total, tiles = sum(sizes), notes.shape[0]
    return pl.pallas_call(
        functools.partial(plan_kernel, sizes, classes, length, keys.shape[0]),
        in_specs=[smem, hbm, hbm],
        out_specs=[hbm] * 4 + [smem] * 3,
        out_shape=[
            jax.ShapeDtypeStruct((size, 2) + keys.shape[1:], keys.dtype) for size in sizes
        ]
        + [jax.ShapeDtypeStruct((n,), jnp.int32) for n in (4 * capacity, 4 * capacity, 3)],
        scratch_shapes=[
            pltpu.VMEM((total, 2) + keys.shape[1:], keys.dtype),
            pltpu.SemaphoreType.DMA((total,)),
            pltpu.SemaphoreType.DMA((total,)),
            pltpu.SMEM((tiles * tiles,), jnp.int32),
            pltpu.SMEM((tiles,), jnp.int32),
        ],
        compiler_params=pltpu.CompilerParams(vmem_limit_bytes=60 << 20),
        cost_estimate=pl.CostEstimate(flops=0, bytes_accessed=16 << 20, transcendentals=0),
        name="plan",
    )(notes, keys, values)


def late_heads(heads):
    last = max(1, heads // 5)
    middle = max(1, 3 * heads // 10)
    return [(0, heads - middle - last), (heads - middle - last, middle), (heads - last, last)]


def fused_kernel(sizes, heads, early_ref, late_ref, facts_ref, *refs):
    n_across, n_relayed, n_beside, n_core = sizes
    (
        query, key, value, query_gain, key_gain, across, beside, core, own,
        out_ref,
        qh, qt, k_own, v_own, k_side, v_side, k_edge, v_edge, k_rows, v_rows,
        k_corner, v_corner, k_give, v_give,
        early, late, kbuf, vbuf, vtail, m_sc, acc_sc, sums,
        load_sem, send_sem, recv_sem, out_sem,
    ) = refs
    ty, tx, ha = lax.axis_index("ty"), lax.axis_index("tx"), lax.axis_index("ha")
    cols, depth = lax.axis_size("tx"), lax.axis_size("ha")
    frames, per_query, features = qh.shape
    width = k_rows.shape[1] // HALO
    tile_rows = per_query // width
    tokens = early.shape[2]
    n_slots = early_ref.shape[0]
    opposite = (1 - ty, tx, ha)
    partner = (ty, lax.rem(tx + 2, cols), ha)
    sibling = (ty, tx + 1 - 2 * lax.rem(tx, 2), ha)
    left, right = (ty, tx - 1, ha), (ty, tx + 1, ha)
    has_left, has_right = tx > 0, tx < cols - 1
    mesh_id = pl.DeviceIdType.MESH
    cuts = late_heads(heads)

    barrier = pltpu.get_barrier_semaphore()
    peers = [opposite, partner, sibling, (ty, 3 - tx, ha)]
    depth_peers = [(ty, tx, lax.rem(ha + o, depth)) for o in range(1, depth)]
    for peer in peers + depth_peers:
        pl.semaphore_signal(barrier, inc=1, device_id=peer, device_id_type=mesh_id)

    first_keys = pl.ds(0, tokens)
    n_early, n_late = early.shape[0], late.shape[0]
    def local_copies():
        return [
            (query, qh),
            (key, k_own),
            (value, v_own),
            (own, early.at[pl.ds(0, n_core)]),
            (value.at[0, first_keys], early.at[n_early - 1, 1]),
            (value.at[0, first_keys], late.at[n_late - 1, 1]),
        ]

    def load(i):
        return pltpu.make_async_copy(*local_copies()[i], load_sem.at[i])

    for i in range(len(local_copies())):
        load(i).start()

    pl.semaphore_wait(barrier, len(peers + depth_peers))

    started = []
    ends = iter(range(64))

    class Sent:
        def __init__(self, views, peer):
            self.views, self.peer, self.end = views, peer, next(ends)
            started.append(self)

        def copy(self):
            src, dst = self.views()
            return pltpu.make_async_remote_copy(
                src_ref=src, dst_ref=dst, send_sem=send_sem.at[self.end],
                recv_sem=recv_sem.at[self.end], device_id=self.peer, device_id_type=mesh_id,
            )

        def wait_recv(self):
            self.copy().wait_recv()

        def wait_send(self):
            self.copy().wait_send()

    def send(views, peer):
        sent = Sent(views, peer)
        sent.copy().start()
        return sent

    def give_sides(src, dst, side_first, side_last):
        i, j = next(ends), next(ends)

        def to_left():
            return pltpu.make_async_remote_copy(
                src_ref=side_first(src), dst_ref=side_last(dst), send_sem=send_sem.at[i],
                recv_sem=recv_sem.at[i], device_id=left, device_id_type=mesh_id,
            )

        def to_right():
            return pltpu.make_async_remote_copy(
                src_ref=side_last(src), dst_ref=side_first(dst), send_sem=send_sem.at[j],
                recv_sem=recv_sem.at[j], device_id=right, device_id_type=mesh_id,
            )

        @pl.when(has_left)
        def _():
            to_left().start()

        @pl.when(has_right)
        def _():
            to_right().start()

        @pl.when(jnp.logical_not(has_right))
        def _():
            pltpu.make_async_copy(side_last(src), side_last(dst), recv_sem.at[i]).start()

        @pl.when(jnp.logical_not(has_left))
        def _():
            pltpu.make_async_copy(side_first(src), side_first(dst), recv_sem.at[j]).start()

        def wait():
            pltpu.make_async_copy(side_last(dst), side_last(dst), recv_sem.at[i]).wait()
            pltpu.make_async_copy(side_first(dst), side_first(dst), recv_sem.at[j]).wait()

        def settle():
            @pl.when(has_left)
            def _():
                to_left().wait_send()

            @pl.when(has_right)
            def _():
                to_right().wait_send()

        return wait, settle

    def lanes_of(h):
        return pl.ds(pl.multiple_of(h * HD, HD), HD)

    n_below = n_across - n_relayed

    def slots(pool, first, count):
        return pool.at[pl.ds(first, count)]

    def above():
        return slots(late, 0, n_relayed)

    def below():
        return slots(late, n_relayed, n_below)

    def beside_at():
        return slots(early, 2 * n_core, n_beside)

    def relayed():
        return slots(late, 2 * n_across, n_relayed)

    got_above = send(lambda: (slots(across, 0, n_relayed), above()), opposite)
    got_beside = send(lambda: (slots(beside, 0, n_beside), beside_at()), partner)
    got_core = send(lambda: (core, slots(early, n_core, n_core)), sibling)
    got_below = send(lambda: (slots(across, n_relayed, n_below), below()), opposite)

    load(0).wait()
    load(1).wait()
    ones = jnp.ones((8, HD), jnp.float32)
    for at, ref in ((0, qh), (frames, k_own)):
        for f in range(frames):

            def add(h, total, ref=ref, f=f):
                wide = ref[f, :, lanes_of(h)].astype(jnp.float32)
                return total + wide * wide

            total = lax.fori_loop(0, heads, add, jnp.zeros((per_query, HD), jnp.float32))
            line = lax.dot_general(
                ones, total, (((1,), (1,)), ((), ())), preferred_element_type=jnp.float32,
                precision=lax.Precision.HIGHEST,
            )
            sums[0, :, (at + f) * per_query : (at + f + 1) * per_query] = line[:1]
    got_sums = [
        send(lambda o=o: (sums.at[0], sums.at[o]), depth_peers[o - 1]) for o in range(1, depth)
    ]
    load(2).wait()
    for copy in got_sums:
        copy.wait_recv()
    total = sums[ha]
    for z in range(1, depth):
        total = total + sums[lax.rem(ha - z + depth, depth)]
    scale = lax.rsqrt(total / (features * depth) + epsilon)

    for f in range(frames):
        scales = []
        for at in (0, frames):
            line = scale[:, (at + f) * per_query : (at + f + 1) * per_query]
            scales.append(jnp.broadcast_to(line, (HD, per_query)).T)

        def norm(h, carry, f=f, scales=scales):
            lanes = lanes_of(h)
            q = qh[f, :, lanes].astype(jnp.float32) * scales[0] * query_gain[:, lanes]
            q = q.astype(jnp.bfloat16).astype(jnp.float32) * log2_scale
            q = q.T
            high = q.astype(jnp.bfloat16)
            qt[h, f, :HD] = high
            qt[h, f, HD:] = (q - high.astype(jnp.float32)).astype(jnp.bfloat16)
            k = k_own[f, :, lanes].astype(jnp.float32) * scales[1] * key_gain[:, lanes]
            k_own[f, :, lanes] = k.astype(jnp.bfloat16)
            return carry

        lax.fori_loop(0, heads, norm, 0)

    def narrow(source, give, n_rows, first, count):
        def cut(h, carry):
            lanes = lanes_of(h)
            for f in range(frames):
                wide = source[f, :, lanes].astype(jnp.float32)
                for i, start in ((0, 0), (1, width - HALO)):
                    cells = [
                        wide[r * width + start : r * width + start + HALO] for r in range(n_rows)
                    ]
                    give[i, f, :, lanes] = jnp.concatenate(cells, axis=0).astype(jnp.bfloat16)
            return carry

        lax.fori_loop(first, first + count, cut, 0)

    rows_out = []
    rows_at = pl.ds((1 - ty) * (tile_rows - HALO) * width, HALO * width)
    for first, count in cuts:
        lanes = pl.ds(first * HD, count * HD)
        rows_out.append(
            [
                send(
                    lambda src=src, dst=dst, lanes=lanes: (
                        src.at[:, rows_at, lanes],
                        dst.at[:, :, lanes],
                    ),
                    opposite,
                )
                for src, dst in ((k_own, k_rows), (v_own, v_rows))
            ]
        )

    def whole(i):
        return lambda ref: ref.at[i]

    narrow(k_own, k_edge, tile_rows, 0, heads)
    narrow(v_own, v_edge, tile_rows, 0, heads)
    k_side_wait, k_side_settle = give_sides(k_edge, k_side, whole(0), whole(1))
    v_side_wait, v_side_settle = give_sides(v_edge, v_side, whole(0), whole(1))

    def put(at, k, v):
        n = k.shape[0]
        kbuf[at : at + n, :HD] = k
        kbuf[at : at + n, HD:] = k
        vbuf[at : at + n, :] = v

    def attend(h, *jobs):
        jobs = list(zip(jobs[::2], jobs[1::2]))
        scores = [
            jnp.dot(kbuf[:keys], qt[h, f], preferred_element_type=jnp.float32) for f, keys in jobs
        ]
        old = [m_sc[h, f, :1] for f, _ in jobs]
        held = [acc_sc[h, f] for f, _ in jobs]
        new = [jnp.maximum(m, jnp.max(s, axis=0, keepdims=True)) for m, s in zip(old, scores)]
        weights = [jnp.exp2(s - m).astype(jnp.bfloat16) for s, m in zip(scores, new)]
        sums_now = [
            jnp.dot(vtail[:, :keys], p, preferred_element_type=jnp.float32)
            for (_, keys), p in zip(jobs, weights)
        ]
        for (f, _), acc, m_old, m, o in zip(jobs, held, old, new, sums_now):
            acc_sc[h, f] = acc * jnp.exp2(m_old - m) + o
            m_sc[h, f] = jnp.broadcast_to(m, m_sc.shape[2:])

    span = per_query
    n_rows = k_rows.shape[1]
    parts = ((k_side, v_side), (k_corner, v_corner))
    pad = span - n_rows - 2 * sum(k.shape[2] for k, _ in parts)

    def put_own(h):
        lanes = lanes_of(h)
        m_sc[h] = jnp.full(m_sc.shape[1:], masked_score, jnp.float32)
        acc_sc[h] = jnp.zeros(acc_sc.shape[1:], jnp.float32)
        for f in range(frames):
            put(f * span, k_own[f, :, lanes], v_own[f, :, lanes])

    def put_rows(h):
        lanes = lanes_of(h)
        for f in range(frames):
            at = f * span
            put(at, k_rows[f, :, lanes], v_rows[f, :, lanes])
            at += n_rows
            for k, v in parts:
                for i in (0, 1):
                    put(at, k[i, f, :, lanes], v[i, f, :, lanes])
                    at += k.shape[2]
            if pad:
                put(at, k_rows[f, :pad, lanes], v_rows[f, :pad, lanes])

    def put_blocks(h, pool, slots_ref):
        lanes = lanes_of(h)
        for i in range(n_slots):
            slot = slots_ref[i]
            put(i * tokens, pool[slot, 0, :, lanes], pool[slot, 1, :, lanes])

    n_keys = frames * span
    spot = lax.broadcasted_iota(jnp.int32, (vtail.shape[0] - HD, n_keys), 1)

    def weigh(weight):
        vtail[HD:] = weight.astype(jnp.bfloat16)

    def weigh_blocks(valid):
        weigh(jnp.where(spot < valid * tokens, 1.0, 0.0))

    def weigh_rows():
        within = lax.rem(spot, span)
        weight = jnp.where(within < n_rows, 1.0, 0.0)
        at = n_rows
        for k, _ in parts:
            for there in (has_left, has_right):
                inside = (within >= at) & (within < at + k.shape[2])
                weight = jnp.where(inside, jnp.where(there, 1.0, 0.0), weight)
                at += k.shape[2]
        weigh(weight)

    assert n_slots * tokens == n_keys and pad >= 0
    settles = [k_side_settle, v_side_settle]

    def before_early():
        got_beside.wait_recv()
        later.append(
            send(
                lambda: (beside_at(), slots(early, 2 * n_core + n_beside, n_beside)), sibling
            )
        )
        got_above.wait_recv()
        later.append(send(lambda: (above(), relayed()), partner))
        later.append(send(lambda: (above(), slots(late, n_across, n_relayed)), sibling))
        got_core.wait_recv()
        for i in range(3, len(local_copies())):
            load(i).wait()
        for pool, at in ((early, n_early), (late, n_late)):
            pool[at - 1, 0] = k_own[0, :tokens]
        later[0].wait_recv()

    def before_late():
        got_below.wait_recv()
        later.append(send(lambda: (below(), slots(late, n_across + n_relayed, n_below)), sibling))
        later[1].wait_recv()
        later.append(
            send(
                lambda: (relayed(), slots(late, 2 * n_across + n_relayed, n_relayed)), sibling
            )
        )
        for i in (2, 3, 4):
            later[i].wait_recv()

    def before_cut(cut, first, count):
        if cut == 0:
            k_side_wait()
            v_side_wait()
        for copy in rows_out[cut]:
            copy.wait_recv()
        narrow(k_rows, k_give, HALO, first, count)
        narrow(v_rows, v_give, HALO, first, count)
        lanes = pl.ds(first * HD, count * HD)

        def side_of(i):
            return lambda ref: ref.at[i, :, :, lanes]

        waits = []
        for give, take in ((k_give, k_corner), (v_give, v_corner)):
            wait, settle = give_sides(give, take, side_of(0), side_of(1))
            waits.append(wait)
            settles.append(settle)
        for wait in waits:
            wait()

    later = []

    def give_out(cut):
        lanes = pl.ds(cuts[cut][0] * HD, cuts[cut][1] * HD)
        return pltpu.make_async_copy(qh.at[:, :, lanes], out_ref.at[:, :, lanes], out_sem.at[cut])

    first_cut = cuts[0][1]
    starts = (0, heads, 2 * heads, 2 * heads + first_cut, 3 * heads + first_cut)

    def step(i, carry):
        own_now, early_now = i < starts[1], (i >= starts[1]) & (i < starts[2])
        late_now = (i >= starts[3]) & (i < starts[4])
        rows_now = ((i >= starts[2]) & (i < starts[3])) | (i >= starts[4])
        h = jnp.where(i < starts[1], i, i - heads)
        h = jnp.where(i < starts[2], h, i - starts[2])
        h = jnp.where(i < starts[3], h, i - starts[3])
        h = jnp.where(i < starts[4], h, i - starts[4] + first_cut)
        final = (late_now & (h < first_cut)) | (i >= starts[4])

        @pl.when(i == starts[0])
        def _():
            weigh(jnp.ones(spot.shape, jnp.float32))

        @pl.when(i == starts[1])
        def _():
            before_early()
            weigh_blocks(facts_ref[0])

        @pl.when((i == starts[2]) | (i == starts[4]))
        def _():
            weigh_rows()

        @pl.when(i == starts[3])
        def _():
            before_late()
            weigh_blocks(facts_ref[1])

        for cut, (first, count) in enumerate(cuts):

            @pl.when(rows_now & (h == first))
            def _(cut=cut, first=first, count=count):
                before_cut(cut, first, count)

        @pl.when(own_now)
        def _():
            put_own(h)

        @pl.when(early_now)
        def _():
            put_blocks(h, early, early_ref)

        @pl.when(late_now)
        def _():
            put_blocks(h, late, late_ref)

        @pl.when(rows_now)
        def _():
            put_rows(h)

        vtail[:HD] = vbuf[...].T * vtail[HD : HD + 1]

        @pl.when(own_now | rows_now)
        def _():
            for pair in range(0, frames, 2):
                attend(h, pair, (pair + 1) * span, pair + 1, (pair + 2) * span)

        @pl.when(early_now | late_now)
        def _():
            def both(pair, carry):
                attend(h, 2 * pair, n_keys, 2 * pair + 1, n_keys)
                return carry

            lax.fori_loop(0, frames // 2, both, 0)

        @pl.when(final)
        def _():
            for f in range(frames):
                done = acc_sc[h, f, :HD] / acc_sc[h, f, HD : HD + 1]
                qh[f, :, lanes_of(h)] = done.T.astype(jnp.bfloat16)

        for cut, (first, count) in enumerate(cuts):

            @pl.when(final & (h == first + count - 1))
            def _(cut=cut):
                give_out(cut).start()

        return carry

    lax.fori_loop(0, 4 * heads, step, 0)
    for copy in started:
        copy.wait_send()
    for settle in settles:
        settle()
    for cut in range(len(cuts)):
        give_out(cut).wait()


def fused(sizes, number, early_slots, late_slots, facts, arrays):
    n_across, n_relayed, n_beside, n_core = sizes
    key, across = arrays[1], arrays[5]
    frames, tile_rows, width, features = key.shape
    per_query = tile_rows * width
    heads = features // HD
    depth = lax.axis_size("ha")
    tokens = across.shape[2]
    side, n_rows, edge = tile_rows * HALO, width * HALO, HALO * HALO
    kind = jnp.bfloat16
    hbm = pl.BlockSpec(memory_space=pl.ANY)
    smem = pl.BlockSpec(memory_space=pltpu.SMEM)
    vmem = pl.BlockSpec(memory_space=pltpu.VMEM)
    n_keys = max(
        frames * per_query, frames * (n_rows + 2 * side + 2 * edge), early_slots.shape[0] * tokens
    )
    n_ends = 40
    flat = (frames, per_query, features)
    whole = pltpu.VMEM(flat, kind)
    sides = pltpu.VMEM((2, frames, side, features), kind)
    corner = pltpu.VMEM((2, frames, edge, features), kind)
    rows = pltpu.VMEM((frames, n_rows, features), kind)
    scores = heads * frames * per_query * n_keys * 2
    query, key, value = (array.reshape(flat) for array in arrays[:3])
    gains = [array.reshape(1, features) for array in arrays[3:5]]
    return pl.pallas_call(
        functools.partial(fused_kernel, sizes, heads),
        in_specs=[smem] * 3 + [hbm] * 3 + [vmem] * 2 + [hbm] * 4,
        out_specs=hbm,
        out_shape=jax.ShapeDtypeStruct(flat, kind),
        scratch_shapes=[
            whole,
            pltpu.VMEM((heads, frames, 2 * HD, per_query), kind),
            whole,
            whole,
        ]
        + [sides] * 4
        + [rows] * 2
        + [corner] * 4
        + [
            pltpu.VMEM((2 * n_core + 2 * n_beside + 1, 2, tokens, features), kind),
            pltpu.VMEM((2 * n_across + 2 * n_relayed + 1, 2, tokens, features), kind),
            pltpu.VMEM((n_keys, 2 * HD), kind),
            pltpu.VMEM((n_keys, HD), kind),
            pltpu.VMEM((HD + 16, n_keys), kind),
            pltpu.VMEM((heads, frames, 8, per_query), jnp.float32),
            pltpu.VMEM((heads, frames, HD + 16, per_query), jnp.float32),
            pltpu.VMEM((depth, 1, 2 * frames * per_query), jnp.float32),
            pltpu.SemaphoreType.DMA((8,)),
            pltpu.SemaphoreType.DMA((n_ends,)),
            pltpu.SemaphoreType.DMA((n_ends,)),
            pltpu.SemaphoreType.DMA((len(late_heads(heads)),)),
        ],
        compiler_params=pltpu.CompilerParams(
            collective_id=number, has_side_effects=True, vmem_limit_bytes=63 << 20
        ),
        cost_estimate=pl.CostEstimate(
            flops=scores * HD * 6, bytes_accessed=60 << 20, transcendentals=scores
        ),
        name="fused",
    )(early_slots, late_slots, facts, query, key, value, *gains, *arrays[5:])


def local(*args):
    if lax.axis_size("ty") != 2 or lax.axis_size("tx") != 4:
        return general(*args)
    cached_keys, cached_values, block_lists, block_counts = args[5:]
    length = block_lists.shape[1]
    c = 4 * length // (3 * lax.axis_size("ty") * lax.axis_size("tx"))
    notes = share(block_lists, block_counts)
    classes = [
        (3 * c // 2 - 1, 5 * c // 4, 5 * c // 4),
        (7 * c // 4, 11 * c // 8, 11 * c // 8),
        (2 * c, 3 * c // 2, 3 * c // 2),
        (5 * c // 2, 2 * c, 2 * c),
    ]
    *packed, early_slots, late_slots, facts = plan(
        notes, cached_keys, cached_values, c, classes, length
    )

    def send(number, operands):
        early_slots, late_slots, facts, packed, args = operands
        sizes = classes[number] + (c,)
        out = fused(
            sizes, number + 1, early_slots, late_slots, facts, list(args[:5]) + list(packed)
        )
        return out.reshape(args[0].shape)

    def plain(operands):
        return general(*operands[-1])

    branches = [functools.partial(send, number) for number in range(len(classes))] + [plain]
    return lax.switch(facts[2], branches, (early_slots, late_slots, facts, packed, args))


def solution(mesh):
    return jax.shard_map(
        local,
        mesh=mesh,
        in_specs=(
            P(None, "ty", "tx", "ha"),
            P(None, "ty", "tx", "ha"),
            P(None, "ty", "tx", "ha"),
            P("ha"),
            P("ha"),
            P(("ty", "tx"), None, "ha"),
            P(("ty", "tx"), None, "ha"),
            P(("ty", "tx"), None),
            P(("ty", "tx")),
        ),
        out_specs=P(None, "ty", "tx", "ha"),
        check_vma=False,
    )
```

```python
import functools
import math

import jax
import jax.numpy as jnp
from jax import lax
from jax.experimental import pallas as pl
from jax.experimental.pallas import tpu as pltpu
from jax.sharding import PartitionSpec as P

HD = 128
HALO = 4
CHUNK = 16

epsilon = 1e-06
masked_score = -1e30
log2_scale = HD ** (-0.5) * math.log2(math.e)


def neighbours(cells, axis, dim, width):
    count = lax.axis_size(axis)
    size = cells.shape[dim]
    head = lax.slice_in_dim(cells, 0, width, axis=dim)
    tail = lax.slice_in_dim(cells, size - width, size, axis=dim)
    where_am_i = lax.axis_index(axis)
    if count == 2:
        mine = jnp.where(where_am_i == 0, tail, head)
        got = lax.ppermute(mine, axis, [(0, 1), (1, 0)])
        return [(got, jnp.bool_(True))]
    ends = count - 1
    before = lax.ppermute(tail, axis, [(i, i + 1) for i in range(ends)])
    after = lax.ppermute(head, axis, [(i + 1, i) for i in range(ends)])
    return [(before, where_am_i > 0), (after, where_am_i < ends)]


def slot_ranks(owners):
    length = owners.shape[-1]
    earlier = lax.broadcasted_iota(jnp.int32, (length, length), 1) < lax.broadcasted_iota(
        jnp.int32, (length, length), 0
    )
    same_owner = owners[..., :, None] == owners[..., None, :]
    return jnp.sum(jnp.where(same_owner & earlier, 1, 0), axis=-1).astype(jnp.int32)


def near_kernel(frames, per_query, n_parts, q_ref, bias_ref, *refs):
    parts_k = refs[:n_parts]
    parts_v = refs[n_parts : 2 * n_parts]
    acc_ref, ml_ref, kbuf, vbuf = refs[2 * n_parts :]
    span = kbuf.shape[0] // frames
    for f in range(frames):
        start = f * span
        for k_ref, v_ref in zip(parts_k, parts_v):
            rows = k_ref.shape[1]
            kbuf[start : start + rows, :] = k_ref[f]
            vbuf[start : start + rows, :HD] = v_ref[f]
            start += rows
    vbuf[:, HD:] = jnp.ones((vbuf.shape[0], HD), jnp.bfloat16)
    for f in range(frames):
        keys = (f + 1) * span
        s = lax.dot_general(
            q_ref[f], kbuf[:keys], (((1,), (1,)), ((), ())), preferred_element_type=jnp.float32
        )
        s = s + bias_ref[:, :keys]
        m = jnp.max(s, axis=1, keepdims=True) * log2_scale
        p = jnp.exp2(s * log2_scale - m).astype(jnp.bfloat16)
        o = jnp.dot(p, vbuf[:keys], preferred_element_type=jnp.float32)
        acc_ref[f] = o[:, :HD]
        lane = lax.broadcasted_iota(jnp.int32, (per_query, HD), 1)
        ml_ref[0, f] = jnp.where(lane < HD // 2, m, o[:, HD:])


def far_kernel(
    frames, per_query, tokens, count_ref, slot_ref, q_ref, acc_in, ml_in, k_ref, v_ref, out_ref,
    kbuf, vbuf, m_sc, l_sc, acc_sc,
):
    count = count_ref[0]
    vbuf[:, HD:] = jnp.ones((vbuf.shape[0], HD), jnp.bfloat16)
    for f in range(frames):
        ml = ml_in[0, f]
        m_sc[f] = jnp.broadcast_to(ml[:, :1], (per_query, HD))
        l_sc[f] = jnp.broadcast_to(ml[:, HD // 2 : HD // 2 + 1], (per_query, HD))
        acc_sc[f] = acc_in[f]

    def chunk(c, carry):
        for i in range(CHUNK):
            slot = slot_ref[c * CHUNK + i]
            kbuf[i * tokens : (i + 1) * tokens, :] = k_ref[slot, 0]
            vbuf[i * tokens : (i + 1) * tokens, :HD] = v_ref[slot, 0]
        place = lax.broadcasted_iota(jnp.int32, (1, CHUNK * tokens), 1)
        bias = jnp.where(place < (count - c * CHUNK) * tokens, 0.0, masked_score)
        for f in range(frames):
            s = lax.dot_general(
                q_ref[f], kbuf[...], (((1,), (1,)), ((), ())), preferred_element_type=jnp.float32
            )
            s = s + bias
            m_old = m_sc[f]
            m_new = jnp.maximum(m_old, jnp.max(s, axis=1, keepdims=True) * log2_scale)
            p = jnp.exp2(s * log2_scale - m_new[:, :1]).astype(jnp.bfloat16)
            o = jnp.dot(p, vbuf[...], preferred_element_type=jnp.float32)
            a = jnp.exp2(m_old - m_new)
            acc_sc[f] = acc_sc[f] * a + o[:, :HD]
            l_sc[f] = l_sc[f] * a + o[:, HD:]
            m_sc[f] = m_new
        return carry

    lax.fori_loop(0, (count + CHUNK - 1) // CHUNK, chunk, 0)
    for f in range(frames):
        out_ref[f] = (acc_sc[f] / l_sc[f]).astype(jnp.bfloat16)


def near_attention(query, parts_k, parts_v, bias):
    frames, per_query, features = query.shape
    heads = features // HD
    span = sum(part.shape[1] for part in parts_k)

    def spec(rows):
        return pl.BlockSpec((frames, rows, HD), lambda h: (0, 0, h))

    part_specs = [spec(part.shape[1]) for part in parts_k]
    keys = frames * span
    return pl.pallas_call(
        functools.partial(near_kernel, frames, per_query, len(parts_k)),
        grid=(heads,),
        in_specs=[spec(per_query), pl.BlockSpec((1, keys), lambda h: (0, 0))]
        + part_specs
        + part_specs,
        out_specs=[
            spec(per_query),
            pl.BlockSpec((1, frames, per_query, HD), lambda h: (h, 0, 0, 0)),
        ],
        out_shape=[
            jax.ShapeDtypeStruct((frames, per_query, features), jnp.float32),
            jax.ShapeDtypeStruct((heads, frames, per_query, HD), jnp.float32),
        ],
        scratch_shapes=[
            pltpu.VMEM((keys, HD), jnp.bfloat16),
            pltpu.VMEM((keys, 2 * HD), jnp.bfloat16),
        ],
        compiler_params=pltpu.CompilerParams(vmem_limit_bytes=60 << 20),
        cost_estimate=pl.CostEstimate(
            flops=heads * frames * per_query * keys * HD * 6,
            bytes_accessed=30 << 20,
            transcendentals=heads * frames * per_query * keys,
        ),
        name="near",
    )(query, bias, *parts_k, *parts_v)


def pick_kernel(total, group, wanted_ref, keys_ref, values_ref, out_ref, held, in_sem, out_sem):
    groups = total // group

    def fetch(i, carry):
        block = wanted_ref[i]
        sem = in_sem.at[i // group]
        pltpu.make_async_copy(keys_ref.at[block], held.at[i, 0], sem).start()
        pltpu.make_async_copy(values_ref.at[block], held.at[i, 1], sem).start()
        return carry

    lax.fori_loop(0, total, fetch, 0)
    for g in range(groups):
        part = pl.ds(g * group, group)
        pltpu.make_async_copy(held.at[part], held.at[part], in_sem.at[g]).wait()
        pltpu.make_async_copy(held.at[part], out_ref.at[part], out_sem.at[g]).start()
    for g in range(groups):
        part = pl.ds(g * group, group)
        pltpu.make_async_copy(held.at[part], out_ref.at[part], out_sem.at[g]).wait()


def pick_blocks(wanted, keys, values):
    total = wanted.shape[0]
    group = 8 if total % 8 == 0 else 1
    shape = (total, 2) + keys.shape[1:]
    return pl.pallas_call(
        functools.partial(pick_kernel, total, group),
        grid_spec=pltpu.PrefetchScalarGridSpec(
            num_scalar_prefetch=1,
            grid=(),
            in_specs=[pl.BlockSpec(memory_space=pl.ANY)] * 2,
            out_specs=pl.BlockSpec(memory_space=pl.ANY),
            scratch_shapes=[
                pltpu.VMEM(shape, keys.dtype),
                pltpu.SemaphoreType.DMA((total // group,)),
                pltpu.SemaphoreType.DMA((total // group,)),
            ],
        ),
        out_shape=jax.ShapeDtypeStruct(shape, keys.dtype),
        compiler_params=pltpu.CompilerParams(vmem_limit_bytes=60 << 20),
        cost_estimate=pl.CostEstimate(flops=0, bytes_accessed=20 << 20, transcendentals=0),
        name="pick",
    )(wanted, keys, values)


def far_attention(query, acc, ml, blocks, count, slots):
    frames, per_query, features = query.shape
    all_slots, _, tokens, width = blocks.shape
    heads = width // HD
    spec = pl.BlockSpec((frames, per_query, HD), lambda h, *_: (0, 0, h))
    k_spec = pl.BlockSpec((all_slots, 1, tokens, HD), lambda h, *_: (0, 0, 0, h))
    v_spec = pl.BlockSpec((all_slots, 1, tokens, HD), lambda h, *_: (0, 1, 0, h))
    return pl.pallas_call(
        functools.partial(far_kernel, frames, per_query, tokens),
        grid_spec=pltpu.PrefetchScalarGridSpec(
            num_scalar_prefetch=2,
            grid=(heads,),
            in_specs=[
                spec,
                spec,
                pl.BlockSpec((1, frames, per_query, HD), lambda h, *_: (h, 0, 0, 0)),
                k_spec,
                v_spec,
            ],
            out_specs=pl.BlockSpec((frames, per_query, HD), lambda h, *_: (0, 0, h)),
            scratch_shapes=[
                pltpu.VMEM((CHUNK * tokens, HD), jnp.bfloat16),
                pltpu.VMEM((CHUNK * tokens, 2 * HD), jnp.bfloat16),
                pltpu.VMEM((frames, per_query, HD), jnp.float32),
                pltpu.VMEM((frames, per_query, HD), jnp.float32),
                pltpu.VMEM((frames, per_query, HD), jnp.float32),
            ],
        ),
        out_shape=jax.ShapeDtypeStruct((frames, per_query, width), jnp.bfloat16),
        compiler_params=pltpu.CompilerParams(vmem_limit_bytes=60 << 20),
        cost_estimate=pl.CostEstimate(
            flops=heads * frames * per_query * 1536 * HD * 6,
            bytes_accessed=30 << 20,
            transcendentals=heads * frames * per_query * 1536,
        ),
        name="far",
    )(count, slots, query, acc, ml, blocks, blocks)


def general(
    queries,
    keys_now,
    values_now,
    query_gain,
    key_gain,
    cached_keys,
    cached_values,
    block_lists,
    block_counts,
):
    frames, tile_rows, tile_cols, features = queries.shape
    owners_all = lax.axis_size("ty") * lax.axis_size("tx")
    full_width = features * lax.axis_size("ha")
    per_query = tile_rows * tile_cols
    per_tile, block_tokens = cached_keys.shape[:2]

    listed = block_lists[0]
    list_length = listed.shape[0]
    owners = listed // per_tile
    within = listed % per_tile
    slot_rank = slot_ranks(owners)
    capacity = max(2, 4 * list_length // (3 * owners_all))
    target = owners * capacity + slot_rank
    all_slots = lax.broadcasted_iota(jnp.int32, (1, owners_all * capacity), 1)
    matches = target[:, None] == all_slots
    outgoing = jnp.sum(jnp.where(matches, within[:, None], 0), axis=0).reshape(owners_all, capacity)
    wanted = lax.all_to_all(outgoing, ("ty", "tx"), split_axis=0, concat_axis=0, tiled=True)
    wanted = wanted.reshape(-1)

    out = pick_blocks(wanted, cached_keys, cached_values)
    now_keys, now_values, _ = lax.optimization_barrier((keys_now, values_now, wanted))
    paired = jnp.stack([now_keys, now_values])
    row_parts = neighbours(paired, "ty", 2, HALO)
    column = jnp.concatenate(
        [jnp.concatenate([part[..., :HALO, :], part[..., -HALO:, :]], axis=3) for part in
         [paired] + [got for got, _ in row_parts]],
        axis=2,
    )
    column_parts = neighbours(column, "tx", 3, HALO)
    out, column_got = lax.optimization_barrier((out, [got for got, _ in column_parts]))
    column_parts = [(got, ok) for got, (_, ok) in zip(column_got, column_parts)]
    back = lax.all_to_all(
        out.reshape((owners_all, capacity) + out.shape[1:]),
        ("ty", "tx"),
        split_axis=0,
        concat_axis=0,
        tiled=True,
    )
    far_blocks = back.reshape((-1,) + out.shape[1:])

    query_wide = queries.astype(jnp.float32)
    key_wide = keys_now.astype(jnp.float32)
    query_sq, key_sq = lax.psum(
        (jnp.sum(query_wide * query_wide, axis=-1), jnp.sum(key_wide * key_wide, axis=-1)), "ha"
    )

    def normed(wide, squares, gain):
        return (wide * lax.rsqrt(squares / full_width + epsilon)[..., None] * gain).astype(
            jnp.bfloat16
        )

    normed_key = normed(key_wide, key_sq, key_gain)
    normed_query = normed(query_wide, query_sq, query_gain)

    ok_rows = [jnp.ones((tile_rows,), bool)] + [
        jnp.broadcast_to(ok, (HALO,)) for _, ok in row_parts
    ]
    ok_rows = jnp.concatenate(ok_rows)
    margins_k, margins_v = [], []
    oks = [jnp.ones((per_query,), bool)]
    for got, ok in row_parts:
        oks.append(jnp.broadcast_to(ok, (HALO * tile_cols,)))
    for got, ok in column_parts:
        oks.append(jnp.repeat(ok_rows & ok, HALO))
    for got, _ in row_parts + column_parts:
        margins_k.append(got[0].reshape(frames, -1, features).astype(jnp.float32))
        margins_v.append(got[1].reshape(frames, -1, features))
    margin_sq = lax.psum(
        jnp.concatenate([jnp.sum(part * part, axis=-1) for part in margins_k], axis=1), "ha"
    )
    parts_k = [normed_key.reshape(frames, -1, features)]
    at = 0
    for part in margins_k:
        parts_k.append(normed(part, margin_sq[:, at : at + part.shape[1]], key_gain))
        at += part.shape[1]
    parts_v = [values_now.reshape(frames, -1, features)] + margins_v
    bias = jnp.where(jnp.concatenate(oks), 0.0, masked_score).astype(jnp.float32)
    bias = jnp.tile(bias, frames)[None]

    flat_query = normed_query.reshape(frames, per_query, features)
    acc, ml = near_attention(flat_query, parts_k, parts_v, bias)
    padding = (-list_length) % CHUNK
    slots = jnp.pad(target, (0, padding))
    attended = far_attention(flat_query, acc, ml, far_blocks, block_counts, slots)
    return attended.reshape(frames, tile_rows, tile_cols, features)


def share_kernel(rows, cols, count_ref, list_ref, notes_ref, send_sem, recv_sem):
    ty, tx, ha = lax.axis_index("ty"), lax.axis_index("tx"), lax.axis_index("ha")
    tiles = rows * cols
    me = ty * cols + tx
    peers = []
    for o in range(1, tiles):
        tile = lax.rem(me + o, tiles)
        peers.append((lax.div(tile, cols), lax.rem(tile, cols), ha))
    barrier = pltpu.get_barrier_semaphore()
    for peer in peers:
        pl.semaphore_signal(barrier, inc=1, device_id=peer, device_id_type=pl.DeviceIdType.MESH)
    notes_ref[me] = jnp.full(notes_ref.shape[1:], count_ref[0], jnp.int32)
    notes_ref[me, :, : list_ref.shape[1]] = list_ref[...]
    pl.semaphore_wait(barrier, tiles - 1)
    copies = []
    for i, peer in enumerate(peers):
        copy = pltpu.make_async_remote_copy(
            src_ref=notes_ref.at[me],
            dst_ref=notes_ref.at[me],
            send_sem=send_sem.at[i],
            recv_sem=recv_sem.at[i],
            device_id=peer,
            device_id_type=pl.DeviceIdType.MESH,
        )
        copy.start()
        copies.append(copy)
    for copy in copies:
        copy.wait_send()
    for i in range(tiles - 1):
        slot = notes_ref.at[lax.rem(me + 2 * tiles - 1 - i, tiles)]
        pltpu.make_async_copy(slot, slot, recv_sem.at[i]).wait()


def share(block_lists, block_counts):
    rows, cols = lax.axis_size("ty"), lax.axis_size("tx")
    tiles = rows * cols
    vmem = pl.BlockSpec(memory_space=pltpu.VMEM)
    return pl.pallas_call(
        functools.partial(share_kernel, rows, cols),
        in_specs=[pl.BlockSpec(memory_space=pltpu.SMEM), vmem],
        out_specs=vmem,
        out_shape=jax.ShapeDtypeStruct((tiles, 1, HD), jnp.int32),
        scratch_shapes=[pltpu.SemaphoreType.DMA((tiles - 1,))] * 2,
        compiler_params=pltpu.CompilerParams(collective_id=0, has_side_effects=True),
        name="share",
    )(block_counts, block_lists)


def plan_kernel(
    sizes, classes, length, per_tile, notes_ref, keys_ref, values_ref, across, beside, core, own,
    early_ref, late_ref, facts_ref, held, in_sem, out_sem, number_ref, slot_ref,
):
    tiles = notes_ref.shape[0]
    cols = lax.axis_size("tx")
    me = lax.axis_index("ty") * cols + lax.axis_index("tx")
    capacity = sizes[3]
    shift = per_tile.bit_length() - 1

    def owner_of(block):
        return lax.shift_right_logical(block, shift) if per_tile == 1 << shift else block // per_tile

    def pair(tile):
        return tile - lax.rem(tile, 2)

    def clear(i, carry):
        number_ref[i] = 0
        return carry

    lax.fori_loop(0, tiles * tiles, clear, 0)

    sections = [
        (0, (pair(me ^ 6), pair(me ^ 6) + 1, pair(me ^ 4), pair(me ^ 4) + 1)),
        (sizes[0], (pair(me ^ 2), pair(me ^ 2) + 1)),
        (sizes[0] + sizes[1], (me ^ 1,)),
        (sizes[0] + sizes[1] + sizes[2], (me,)),
    ]
    counts = []
    for start, targets in sections:
        at = jnp.int32(start)
        for target in targets:

            def scan(j, at, target=target):
                block = notes_ref[target, 0, j]
                owner = owner_of(block)
                cell = owner * tiles + target
                number_ref[cell] = number_ref[cell] + 1
                mine = owner == me

                @pl.when(mine)
                def _():
                    here = block - me * per_tile
                    pltpu.make_async_copy(keys_ref.at[here], held.at[at, 0], in_sem.at[at]).start()
                    pltpu.make_async_copy(values_ref.at[here], held.at[at, 1], in_sem.at[at]).start()

                return at + mine.astype(jnp.int32)

            at = lax.fori_loop(0, notes_ref[target, 0, length], scan, at)
        counts.append(at - start)

    for (start, _), count, out_ref in zip(sections, counts, (across, beside, core, own)):

        def store(i, carry, start=start, out_ref=out_ref):
            at = start + i
            pltpu.make_async_copy(held.at[at], held.at[at], in_sem.at[at]).wait()
            pltpu.make_async_copy(held.at[at], out_ref.at[i], out_sem.at[at]).start()
            return carry

        lax.fori_loop(0, count, store, 0)

    def number(owner, target):
        return number_ref[owner * tiles + target]

    def both(owner, target):
        return number(owner, target) + number(owner, target + 1)

    def most(owner, carry):
        diagonal = both(owner, pair(owner ^ 6))
        most_across, most_diagonal, most_beside = carry
        return (
            jnp.maximum(most_across, diagonal + both(owner, pair(owner ^ 4))),
            jnp.maximum(most_diagonal, diagonal),
            jnp.maximum(most_beside, both(owner, pair(owner ^ 2))),
        )

    need = lax.fori_loop(0, tiles, most, (jnp.int32(0),) * 3)
    which = jnp.int32(0)
    for limits in classes:
        short = (need[0] > limits[0]) | (need[1] > limits[1]) | (need[2] > limits[2])
        which = which + short.astype(jnp.int32)
    n_across, n_relayed, n_beside = (jnp.int32(classes[-1][i]) for i in range(3))
    for i, limits in reversed(list(enumerate(classes))):
        n_across = jnp.where(which == i, limits[0], n_across)
        n_relayed = jnp.where(which == i, limits[1], n_relayed)
        n_beside = jnp.where(which == i, limits[2], n_beside)

    def place(owner, carry):
        flip = owner ^ me
        other = lax.rem(flip, 2)
        before = jnp.where(lax.rem(me, 2) == 1, number(owner, pair(me)), 0)
        diagonal = both(owner, pair(owner ^ 6))
        near = jnp.where(flip == 0, 0, capacity)
        early = jnp.where(flip >= 2, 2 * capacity + other * n_beside + before, near)
        straight = other * n_across + diagonal + before
        turned = 2 * n_across + other * n_relayed + before
        late = jnp.where(flip >= 6, turned, straight)
        slot_ref[owner] = jnp.where(flip >= 4, late, early)
        return carry

    lax.fori_loop(0, tiles, place, 0)

    def blank(i, carry):
        early_ref[i] = 2 * capacity + 2 * n_beside
        late_ref[i] = 2 * n_across + 2 * n_relayed
        return carry

    lax.fori_loop(0, 4 * capacity, blank, 0)

    def point(j, carry):
        n_early, n_late = carry
        owner = owner_of(notes_ref[me, 0, j])
        slot = slot_ref[owner]
        slot_ref[owner] = slot + 1
        far = (owner ^ me) >= 4

        @pl.when(far)
        def _():
            late_ref[n_late] = slot

        @pl.when(jnp.logical_not(far))
        def _():
            early_ref[n_early] = slot

        step = far.astype(jnp.int32)
        return n_early + 1 - step, n_late + step

    n_early, n_late = lax.fori_loop(
        0, notes_ref[me, 0, length], point, (jnp.int32(0), jnp.int32(0))
    )
    facts_ref[0] = n_early
    facts_ref[1] = n_late
    facts_ref[2] = which

    for (start, _), count, out_ref in zip(sections, counts, (across, beside, core, own)):

        def settle(i, carry, start=start, out_ref=out_ref):
            at = start + i
            pltpu.make_async_copy(held.at[at], out_ref.at[i], out_sem.at[at]).wait()
            return carry

        lax.fori_loop(0, count, settle, 0)


def plan(notes, keys, values, capacity, classes, length):
    hbm = pl.BlockSpec(memory_space=pl.ANY)
    smem = pl.BlockSpec(memory_space=pltpu.SMEM)
    sizes = (4 * capacity, 2 * capacity, capacity, capacity)
    total, tiles = sum(sizes), notes.shape[0]
    return pl.pallas_call(
        functools.partial(plan_kernel, sizes, classes, length, keys.shape[0]),
        in_specs=[smem, hbm, hbm],
        out_specs=[hbm] * 4 + [smem] * 3,
        out_shape=[
            jax.ShapeDtypeStruct((size, 2) + keys.shape[1:], keys.dtype) for size in sizes
        ]
        + [jax.ShapeDtypeStruct((n,), jnp.int32) for n in (4 * capacity, 4 * capacity, 3)],
        scratch_shapes=[
            pltpu.VMEM((total, 2) + keys.shape[1:], keys.dtype),
            pltpu.SemaphoreType.DMA((total,)),
            pltpu.SemaphoreType.DMA((total,)),
            pltpu.SMEM((tiles * tiles,), jnp.int32),
            pltpu.SMEM((tiles,), jnp.int32),
        ],
        compiler_params=pltpu.CompilerParams(vmem_limit_bytes=60 << 20),
        cost_estimate=pl.CostEstimate(flops=0, bytes_accessed=16 << 20, transcendentals=0),
        name="plan",
    )(notes, keys, values)


def late_heads(heads):
    last = max(1, heads // 5)
    middle = max(1, 3 * heads // 10)
    return [(0, heads - middle - last), (heads - middle - last, middle), (heads - last, last)]


def fused_kernel(sizes, heads, early_ref, late_ref, facts_ref, *refs):
    n_across, n_relayed, n_beside, n_core = sizes
    (
        query, key, value, query_gain, key_gain, across, beside, core, own,
        out_ref,
        qh, qt, k_own, v_own, k_side, v_side, k_edge, v_edge, k_rows, v_rows,
        k_corner, v_corner, k_give, v_give,
        early, late, kbuf, vbuf, vtail, m_sc, acc_sc, sums,
        load_sem, send_sem, recv_sem, out_sem,
    ) = refs
    ty, tx, ha = lax.axis_index("ty"), lax.axis_index("tx"), lax.axis_index("ha")
    cols, depth = lax.axis_size("tx"), lax.axis_size("ha")
    frames, per_query, features = qh.shape
    width = k_rows.shape[1] // HALO
    tile_rows = per_query // width
    tokens = early.shape[2]
    n_slots = early_ref.shape[0]
    opposite = (1 - ty, tx, ha)
    partner = (ty, lax.rem(tx + 2, cols), ha)
    sibling = (ty, tx + 1 - 2 * lax.rem(tx, 2), ha)
    left, right = (ty, tx - 1, ha), (ty, tx + 1, ha)
    has_left, has_right = tx > 0, tx < cols - 1
    mesh_id = pl.DeviceIdType.MESH
    cuts = late_heads(heads)

    barrier = pltpu.get_barrier_semaphore()
    peers = [opposite, partner, sibling, (ty, 3 - tx, ha)]
    depth_peers = [(ty, tx, lax.rem(ha + o, depth)) for o in range(1, depth)]
    for peer in peers + depth_peers:
        pl.semaphore_signal(barrier, inc=1, device_id=peer, device_id_type=mesh_id)

    first_keys = pl.ds(0, tokens)
    n_early, n_late = early.shape[0], late.shape[0]
    def local_copies():
        return [
            (query, qh),
            (key, k_own),
            (value, v_own),
            (own, early.at[pl.ds(0, n_core)]),
            (value.at[0, first_keys], early.at[n_early - 1, 1]),
            (value.at[0, first_keys], late.at[n_late - 1, 1]),
        ]

    def load(i):
        return pltpu.make_async_copy(*local_copies()[i], load_sem.at[i])

    for i in range(len(local_copies())):
        load(i).start()

    pl.semaphore_wait(barrier, len(peers + depth_peers))

    started = []
    ends = iter(range(64))

    class Sent:
        def __init__(self, views, peer):
            self.views, self.peer, self.end = views, peer, next(ends)
            started.append(self)

        def copy(self):
            src, dst = self.views()
            return pltpu.make_async_remote_copy(
                src_ref=src, dst_ref=dst, send_sem=send_sem.at[self.end],
                recv_sem=recv_sem.at[self.end], device_id=self.peer, device_id_type=mesh_id,
            )

        def wait_recv(self):
            self.copy().wait_recv()

        def wait_send(self):
            self.copy().wait_send()

    def send(views, peer):
        sent = Sent(views, peer)
        sent.copy().start()
        return sent

    def give_sides(src, dst, side_first, side_last):
        i, j = next(ends), next(ends)

        def to_left():
            return pltpu.make_async_remote_copy(
                src_ref=side_first(src), dst_ref=side_last(dst), send_sem=send_sem.at[i],
                recv_sem=recv_sem.at[i], device_id=left, device_id_type=mesh_id,
            )

        def to_right():
            return pltpu.make_async_remote_copy(
                src_ref=side_last(src), dst_ref=side_first(dst), send_sem=send_sem.at[j],
                recv_sem=recv_sem.at[j], device_id=right, device_id_type=mesh_id,
            )

        @pl.when(has_left)
        def _():
            to_left().start()

        @pl.when(has_right)
        def _():
            to_right().start()

        @pl.when(jnp.logical_not(has_right))
        def _():
            pltpu.make_async_copy(side_last(src), side_last(dst), recv_sem.at[i]).start()

        @pl.when(jnp.logical_not(has_left))
        def _():
            pltpu.make_async_copy(side_first(src), side_first(dst), recv_sem.at[j]).start()

        def wait():
            pltpu.make_async_copy(side_last(dst), side_last(dst), recv_sem.at[i]).wait()
            pltpu.make_async_copy(side_first(dst), side_first(dst), recv_sem.at[j]).wait()

        def settle():
            @pl.when(has_left)
            def _():
                to_left().wait_send()

            @pl.when(has_right)
            def _():
                to_right().wait_send()

        return wait, settle

    def lanes_of(h):
        return pl.ds(pl.multiple_of(h * HD, HD), HD)

    n_below = n_across - n_relayed

    def slots(pool, first, count):
        return pool.at[pl.ds(first, count)]

    def above():
        return slots(late, 0, n_relayed)

    def below():
        return slots(late, n_relayed, n_below)

    def beside_at():
        return slots(early, 2 * n_core, n_beside)

    def relayed():
        return slots(late, 2 * n_across, n_relayed)

    got_above = send(lambda: (slots(across, 0, n_relayed), above()), opposite)
    got_beside = send(lambda: (slots(beside, 0, n_beside), beside_at()), partner)
    got_core = send(lambda: (core, slots(early, n_core, n_core)), sibling)
    got_below = send(lambda: (slots(across, n_relayed, n_below), below()), opposite)

    load(0).wait()
    load(1).wait()
    ones = jnp.ones((8, HD), jnp.float32)
    for at, ref in ((0, qh), (frames, k_own)):
        for f in range(frames):

            def add(h, total, ref=ref, f=f):
                wide = ref[f, :, lanes_of(h)].astype(jnp.float32)
                return total + wide * wide

            total = lax.fori_loop(0, heads, add, jnp.zeros((per_query, HD), jnp.float32))
            line = lax.dot_general(
                ones, total, (((1,), (1,)), ((), ())), preferred_element_type=jnp.float32,
                precision=lax.Precision.HIGHEST,
            )
            sums[0, :, (at + f) * per_query : (at + f + 1) * per_query] = line[:1]
    got_sums = [
        send(lambda o=o: (sums.at[0], sums.at[o]), depth_peers[o - 1]) for o in range(1, depth)
    ]
    load(2).wait()
    for copy in got_sums:
        copy.wait_recv()
    total = sums[ha]
    for z in range(1, depth):
        total = total + sums[lax.rem(ha - z + depth, depth)]
    scale = lax.rsqrt(total / (features * depth) + epsilon)

    for f in range(frames):
        scales = []
        for at in (0, frames):
            line = scale[:, (at + f) * per_query : (at + f + 1) * per_query]
            scales.append(jnp.broadcast_to(line, (HD, per_query)).T)

        def norm(h, carry, f=f, scales=scales):
            lanes = lanes_of(h)
            q = qh[f, :, lanes].astype(jnp.float32) * scales[0] * query_gain[:, lanes]
            q = q.astype(jnp.bfloat16).astype(jnp.float32) * log2_scale
            q = q.T
            high = q.astype(jnp.bfloat16)
            qt[h, f, :HD] = high
            qt[h, f, HD:] = (q - high.astype(jnp.float32)).astype(jnp.bfloat16)
            k = k_own[f, :, lanes].astype(jnp.float32) * scales[1] * key_gain[:, lanes]
            k_own[f, :, lanes] = k.astype(jnp.bfloat16)
            return carry

        lax.fori_loop(0, heads, norm, 0)

    def narrow(source, give, n_rows, first, count):
        def cut(h, carry):
            lanes = lanes_of(h)
            for f in range(frames):
                wide = source[f, :, lanes].astype(jnp.float32)
                for i, start in ((0, 0), (1, width - HALO)):
                    cells = [
                        wide[r * width + start : r * width + start + HALO] for r in range(n_rows)
                    ]
                    give[i, f, :, lanes] = jnp.concatenate(cells, axis=0).astype(jnp.bfloat16)
            return carry

        lax.fori_loop(first, first + count, cut, 0)

    rows_out = []
    rows_at = pl.ds((1 - ty) * (tile_rows - HALO) * width, HALO * width)
    for first, count in cuts:
        lanes = pl.ds(first * HD, count * HD)
        rows_out.append(
            [
                send(
                    lambda src=src, dst=dst, lanes=lanes: (
                        src.at[:, rows_at, lanes],
                        dst.at[:, :, lanes],
                    ),
                    opposite,
                )
                for src, dst in ((k_own, k_rows), (v_own, v_rows))
            ]
        )

    def whole(i):
        return lambda ref: ref.at[i]

    narrow(k_own, k_edge, tile_rows, 0, heads)
    narrow(v_own, v_edge, tile_rows, 0, heads)
    k_side_wait, k_side_settle = give_sides(k_edge, k_side, whole(0), whole(1))
    v_side_wait, v_side_settle = give_sides(v_edge, v_side, whole(0), whole(1))

    def put(at, k, v):
        n = k.shape[0]
        kbuf[at : at + n, :HD] = k
        kbuf[at : at + n, HD:] = k
        vbuf[at : at + n, :] = v

    def attend(h, *jobs):
        jobs = list(zip(jobs[::2], jobs[1::2]))
        scores = [
            jnp.dot(kbuf[:keys], qt[h, f], preferred_element_type=jnp.float32) for f, keys in jobs
        ]
        old = [m_sc[h, f, :1] for f, _ in jobs]
        held = [acc_sc[h, f] for f, _ in jobs]
        new = [jnp.maximum(m, jnp.max(s, axis=0, keepdims=True)) for m, s in zip(old, scores)]
        weights = [jnp.exp2(s - m).astype(jnp.bfloat16) for s, m in zip(scores, new)]
        sums_now = [
            jnp.dot(vtail[:, :keys], p, preferred_element_type=jnp.float32)
            for (_, keys), p in zip(jobs, weights)
        ]
        for (f, _), acc, m_old, m, o in zip(jobs, held, old, new, sums_now):
            acc_sc[h, f] = acc * jnp.exp2(m_old - m) + o
            m_sc[h, f] = jnp.broadcast_to(m, m_sc.shape[2:])

    span = per_query
    n_rows = k_rows.shape[1]
    parts = ((k_side, v_side), (k_corner, v_corner))
    pad = span - n_rows - 2 * sum(k.shape[2] for k, _ in parts)

    def put_own(h):
        lanes = lanes_of(h)
        m_sc[h] = jnp.full(m_sc.shape[1:], masked_score, jnp.float32)
        acc_sc[h] = jnp.zeros(acc_sc.shape[1:], jnp.float32)
        for f in range(frames):
            put(f * span, k_own[f, :, lanes], v_own[f, :, lanes])

    def put_rows(h):
        lanes = lanes_of(h)
        for f in range(frames):
            at = f * span
            put(at, k_rows[f, :, lanes], v_rows[f, :, lanes])
            at += n_rows
            for k, v in parts:
                for i in (0, 1):
                    put(at, k[i, f, :, lanes], v[i, f, :, lanes])
                    at += k.shape[2]
            if pad:
                put(at, k_rows[f, :pad, lanes], v_rows[f, :pad, lanes])

    def put_blocks(h, pool, slots_ref):
        lanes = lanes_of(h)
        for i in range(n_slots):
            slot = slots_ref[i]
            put(i * tokens, pool[slot, 0, :, lanes], pool[slot, 1, :, lanes])

    n_keys = frames * span
    spot = lax.broadcasted_iota(jnp.int32, (vtail.shape[0] - HD, n_keys), 1)

    def weigh(weight):
        vtail[HD:] = weight.astype(jnp.bfloat16)

    def weigh_blocks(valid):
        weigh(jnp.where(spot < valid * tokens, 1.0, 0.0))

    def weigh_rows():
        within = lax.rem(spot, span)
        weight = jnp.where(within < n_rows, 1.0, 0.0)
        at = n_rows
        for k, _ in parts:
            for there in (has_left, has_right):
                inside = (within >= at) & (within < at + k.shape[2])
                weight = jnp.where(inside, jnp.where(there, 1.0, 0.0), weight)
                at += k.shape[2]
        weigh(weight)

    assert n_slots * tokens == n_keys and pad >= 0
    settles = [k_side_settle, v_side_settle]

    later = {}

    def before_early():
        got_above.wait_recv()
        later["relay"] = send(lambda: (above(), relayed()), partner)
        got_beside.wait_recv()
        later["beside"] = send(
            lambda: (beside_at(), slots(early, 2 * n_core + n_beside, n_beside)), sibling
        )
        later["above"] = send(lambda: (above(), slots(late, n_across, n_relayed)), sibling)
        got_core.wait_recv()
        for i in range(3, len(local_copies())):
            load(i).wait()
        for pool, at in ((early, n_early), (late, n_late)):
            pool[at - 1, 0] = k_own[0, :tokens]
        later["beside"].wait_recv()

    def forward_late():
        got_below.wait_recv()
        later["below"] = send(
            lambda: (below(), slots(late, n_across + n_relayed, n_below)), sibling
        )
        later["relay"].wait_recv()
        later["relayed"] = send(
            lambda: (relayed(), slots(late, 2 * n_across + n_relayed, n_relayed)), sibling
        )

    def before_late():
        for name in ("above", "below", "relayed"):
            later[name].wait_recv()

    cut_waits = {}

    def begin_cut(cut):
        first, count = cuts[cut]
        if cut == 0:
            k_side_wait()
            v_side_wait()
        for copy in rows_out[cut]:
            copy.wait_recv()
        narrow(k_rows, k_give, HALO, first, count)
        narrow(v_rows, v_give, HALO, first, count)
        lanes = pl.ds(first * HD, count * HD)

        def side_of(i):
            return lambda ref: ref.at[i, :, :, lanes]

        waits = []
        for give, take in ((k_give, k_corner), (v_give, v_corner)):
            wait, settle = give_sides(give, take, side_of(0), side_of(1))
            waits.append(wait)
            settles.append(settle)
        cut_waits[cut] = waits

    def end_cut(cut):
        for wait in cut_waits[cut]:
            wait()

    def give_out(cut):
        lanes = pl.ds(cuts[cut][0] * HD, cuts[cut][1] * HD)
        return pltpu.make_async_copy(qh.at[:, :, lanes], out_ref.at[:, :, lanes], out_sem.at[cut])

    first_cut = cuts[0][1]
    starts = (0, heads, 2 * heads, 2 * heads + first_cut, 3 * heads + first_cut)

    def step(i, carry):
        own_now, early_now = i < starts[1], (i >= starts[1]) & (i < starts[2])
        late_now = (i >= starts[3]) & (i < starts[4])
        rows_now = ((i >= starts[2]) & (i < starts[3])) | (i >= starts[4])
        h = jnp.where(i < starts[1], i, i - heads)
        h = jnp.where(i < starts[2], h, i - starts[2])
        h = jnp.where(i < starts[3], h, i - starts[3])
        h = jnp.where(i < starts[4], h, i - starts[4] + first_cut)
        final = (late_now & (h < first_cut)) | (i >= starts[4])

        @pl.when(i == starts[0])
        def _():
            weigh(jnp.ones(spot.shape, jnp.float32))

        @pl.when(i == starts[1])
        def _():
            before_early()
            weigh_blocks(facts_ref[0])

        @pl.when((i == starts[2]) | (i == starts[4]))
        def _():
            weigh_rows()

        for cut in range(len(cuts)):
            at = starts[2] if cut == 0 else starts[4] - 1 if cut > 1 else starts[3] + heads // 2

            @pl.when(i == at)
            def _(cut=cut):
                begin_cut(cut)
                if cut == 0:
                    forward_late()

        @pl.when(i == starts[3])
        def _():
            before_late()
            weigh_blocks(facts_ref[1])

        for cut, (first, count) in enumerate(cuts):

            @pl.when(rows_now & (h == first))
            def _(cut=cut):
                end_cut(cut)

        @pl.when(own_now)
        def _():
            put_own(h)

        @pl.when(early_now)
        def _():
            put_blocks(h, early, early_ref)

        @pl.when(late_now)
        def _():
            put_blocks(h, late, late_ref)

        @pl.when(rows_now)
        def _():
            put_rows(h)

        vtail[:HD] = vbuf[...].T * vtail[HD : HD + 1]

        @pl.when(own_now | rows_now)
        def _():
            for pair in range(0, frames, 2):
                attend(h, pair, (pair + 1) * span, pair + 1, (pair + 2) * span)

        @pl.when(early_now | late_now)
        def _():
            def both(pair, carry):
                attend(h, 2 * pair, n_keys, 2 * pair + 1, n_keys)
                return carry

            lax.fori_loop(0, frames // 2, both, 0)

        @pl.when(final)
        def _():
            for f in range(frames):
                done = acc_sc[h, f, :HD] / acc_sc[h, f, HD : HD + 1]
                qh[f, :, lanes_of(h)] = done.T.astype(jnp.bfloat16)

        for cut, (first, count) in enumerate(cuts):

            @pl.when(final & (h == first + count - 1))
            def _(cut=cut):
                give_out(cut).start()

        return carry

    lax.fori_loop(0, 4 * heads, step, 0)
    for copy in started:
        copy.wait_send()
    for settle in settles:
        settle()
    for cut in range(len(cuts)):
        give_out(cut).wait()


def fused(sizes, number, early_slots, late_slots, facts, arrays):
    n_across, n_relayed, n_beside, n_core = sizes
    key, across = arrays[1], arrays[5]
    frames, tile_rows, width, features = key.shape
    per_query = tile_rows * width
    heads = features // HD
    depth = lax.axis_size("ha")
    tokens = across.shape[2]
    side, n_rows, edge = tile_rows * HALO, width * HALO, HALO * HALO
    kind = jnp.bfloat16
    hbm = pl.BlockSpec(memory_space=pl.ANY)
    smem = pl.BlockSpec(memory_space=pltpu.SMEM)
    vmem = pl.BlockSpec(memory_space=pltpu.VMEM)
    n_keys = max(
        frames * per_query, frames * (n_rows + 2 * side + 2 * edge), early_slots.shape[0] * tokens
    )
    n_ends = 40
    flat = (frames, per_query, features)
    whole = pltpu.VMEM(flat, kind)
    sides = pltpu.VMEM((2, frames, side, features), kind)
    corner = pltpu.VMEM((2, frames, edge, features), kind)
    rows = pltpu.VMEM((frames, n_rows, features), kind)
    scores = heads * frames * per_query * n_keys * 2
    query, key, value = (array.reshape(flat) for array in arrays[:3])
    gains = [array.reshape(1, features) for array in arrays[3:5]]
    return pl.pallas_call(
        functools.partial(fused_kernel, sizes, heads),
        in_specs=[smem] * 3 + [hbm] * 3 + [vmem] * 2 + [hbm] * 4,
        out_specs=hbm,
        out_shape=jax.ShapeDtypeStruct(flat, kind),
        scratch_shapes=[
            whole,
            pltpu.VMEM((heads, frames, 2 * HD, per_query), kind),
            whole,
            whole,
        ]
        + [sides] * 4
        + [rows] * 2
        + [corner] * 4
        + [
            pltpu.VMEM((2 * n_core + 2 * n_beside + 1, 2, tokens, features), kind),
            pltpu.VMEM((2 * n_across + 2 * n_relayed + 1, 2, tokens, features), kind),
            pltpu.VMEM((n_keys, 2 * HD), kind),
            pltpu.VMEM((n_keys, HD), kind),
            pltpu.VMEM((HD + 16, n_keys), kind),
            pltpu.VMEM((heads, frames, 8, per_query), jnp.float32),
            pltpu.VMEM((heads, frames, HD + 16, per_query), jnp.float32),
            pltpu.VMEM((depth, 1, 2 * frames * per_query), jnp.float32),
            pltpu.SemaphoreType.DMA((8,)),
            pltpu.SemaphoreType.DMA((n_ends,)),
            pltpu.SemaphoreType.DMA((n_ends,)),
            pltpu.SemaphoreType.DMA((len(late_heads(heads)),)),
        ],
        compiler_params=pltpu.CompilerParams(
            collective_id=number, has_side_effects=True, vmem_limit_bytes=63 << 20
        ),
        cost_estimate=pl.CostEstimate(
            flops=scores * HD * 6, bytes_accessed=60 << 20, transcendentals=scores
        ),
        name="fused",
    )(early_slots, late_slots, facts, query, key, value, *gains, *arrays[5:])


def local(*args):
    if lax.axis_size("ty") != 2 or lax.axis_size("tx") != 4:
        return general(*args)
    cached_keys, cached_values, block_lists, block_counts = args[5:]
    length = block_lists.shape[1]
    c = 4 * length // (3 * lax.axis_size("ty") * lax.axis_size("tx"))
    notes = share(block_lists, block_counts)
    classes = [
        (3 * c // 2 - 1, 5 * c // 4, 5 * c // 4),
        (7 * c // 4, 11 * c // 8, 11 * c // 8),
        (2 * c, 3 * c // 2, 3 * c // 2),
        (5 * c // 2, 2 * c, 2 * c),
    ]
    *packed, early_slots, late_slots, facts = plan(
        notes, cached_keys, cached_values, c, classes, length
    )

    def send(number, operands):
        early_slots, late_slots, facts, packed, args = operands
        sizes = classes[number] + (c,)
        out = fused(
            sizes, number + 1, early_slots, late_slots, facts, list(args[:5]) + list(packed)
        )
        return out.reshape(args[0].shape)

    def plain(operands):
        return general(*operands[-1])

    branches = [functools.partial(send, number) for number in range(len(classes))] + [plain]
    return lax.switch(facts[2], branches, (early_slots, late_slots, facts, packed, args))


def solution(mesh):
    return jax.shard_map(
        local,
        mesh=mesh,
        in_specs=(
            P(None, "ty", "tx", "ha"),
            P(None, "ty", "tx", "ha"),
            P(None, "ty", "tx", "ha"),
            P("ha"),
            P("ha"),
            P(("ty", "tx"), None, "ha"),
            P(("ty", "tx"), None, "ha"),
            P(("ty", "tx"), None),
            P(("ty", "tx")),
        ),
        out_specs=P(None, "ty", "tx", "ha"),
        check_vma=False,
    )
```

```python
import functools
import math

import jax
import jax.numpy as jnp
from jax import lax
from jax.experimental import pallas as pl
from jax.experimental.pallas import tpu as pltpu
from jax.sharding import PartitionSpec as P

HD = 128
HALO = 4
CHUNK = 16

epsilon = 1e-06
masked_score = -1e30
log2_scale = HD ** (-0.5) * math.log2(math.e)


def neighbours(cells, axis, dim, width):
    count = lax.axis_size(axis)
    size = cells.shape[dim]
    head = lax.slice_in_dim(cells, 0, width, axis=dim)
    tail = lax.slice_in_dim(cells, size - width, size, axis=dim)
    where_am_i = lax.axis_index(axis)
    if count == 2:
        mine = jnp.where(where_am_i == 0, tail, head)
        got = lax.ppermute(mine, axis, [(0, 1), (1, 0)])
        return [(got, jnp.bool_(True))]
    ends = count - 1
    before = lax.ppermute(tail, axis, [(i, i + 1) for i in range(ends)])
    after = lax.ppermute(head, axis, [(i + 1, i) for i in range(ends)])
    return [(before, where_am_i > 0), (after, where_am_i < ends)]


def slot_ranks(owners):
    length = owners.shape[-1]
    earlier = lax.broadcasted_iota(jnp.int32, (length, length), 1) < lax.broadcasted_iota(
        jnp.int32, (length, length), 0
    )
    same_owner = owners[..., :, None] == owners[..., None, :]
    return jnp.sum(jnp.where(same_owner & earlier, 1, 0), axis=-1).astype(jnp.int32)


def near_kernel(frames, per_query, n_parts, q_ref, bias_ref, *refs):
    parts_k = refs[:n_parts]
    parts_v = refs[n_parts : 2 * n_parts]
    acc_ref, ml_ref, kbuf, vbuf = refs[2 * n_parts :]
    span = kbuf.shape[0] // frames
    for f in range(frames):
        start = f * span
        for k_ref, v_ref in zip(parts_k, parts_v):
            rows = k_ref.shape[1]
            kbuf[start : start + rows, :] = k_ref[f]
            vbuf[start : start + rows, :HD] = v_ref[f]
            start += rows
    vbuf[:, HD:] = jnp.ones((vbuf.shape[0], HD), jnp.bfloat16)
    for f in range(frames):
        keys = (f + 1) * span
        s = lax.dot_general(
            q_ref[f], kbuf[:keys], (((1,), (1,)), ((), ())), preferred_element_type=jnp.float32
        )
        s = s + bias_ref[:, :keys]
        m = jnp.max(s, axis=1, keepdims=True) * log2_scale
        p = jnp.exp2(s * log2_scale - m).astype(jnp.bfloat16)
        o = jnp.dot(p, vbuf[:keys], preferred_element_type=jnp.float32)
        acc_ref[f] = o[:, :HD]
        lane = lax.broadcasted_iota(jnp.int32, (per_query, HD), 1)
        ml_ref[0, f] = jnp.where(lane < HD // 2, m, o[:, HD:])


def far_kernel(
    frames, per_query, tokens, count_ref, slot_ref, q_ref, acc_in, ml_in, k_ref, v_ref, out_ref,
    kbuf, vbuf, m_sc, l_sc, acc_sc,
):
    count = count_ref[0]
    vbuf[:, HD:] = jnp.ones((vbuf.shape[0], HD), jnp.bfloat16)
    for f in range(frames):
        ml = ml_in[0, f]
        m_sc[f] = jnp.broadcast_to(ml[:, :1], (per_query, HD))
        l_sc[f] = jnp.broadcast_to(ml[:, HD // 2 : HD // 2 + 1], (per_query, HD))
        acc_sc[f] = acc_in[f]

    def chunk(c, carry):
        for i in range(CHUNK):
            slot = slot_ref[c * CHUNK + i]
            kbuf[i * tokens : (i + 1) * tokens, :] = k_ref[slot, 0]
            vbuf[i * tokens : (i + 1) * tokens, :HD] = v_ref[slot, 0]
        place = lax.broadcasted_iota(jnp.int32, (1, CHUNK * tokens), 1)
        bias = jnp.where(place < (count - c * CHUNK) * tokens, 0.0, masked_score)
        for f in range(frames):
            s = lax.dot_general(
                q_ref[f], kbuf[...], (((1,), (1,)), ((), ())), preferred_element_type=jnp.float32
            )
            s = s + bias
            m_old = m_sc[f]
            m_new = jnp.maximum(m_old, jnp.max(s, axis=1, keepdims=True) * log2_scale)
            p = jnp.exp2(s * log2_scale - m_new[:, :1]).astype(jnp.bfloat16)
            o = jnp.dot(p, vbuf[...], preferred_element_type=jnp.float32)
            a = jnp.exp2(m_old - m_new)
            acc_sc[f] = acc_sc[f] * a + o[:, :HD]
            l_sc[f] = l_sc[f] * a + o[:, HD:]
            m_sc[f] = m_new
        return carry

    lax.fori_loop(0, (count + CHUNK - 1) // CHUNK, chunk, 0)
    for f in range(frames):
        out_ref[f] = (acc_sc[f] / l_sc[f]).astype(jnp.bfloat16)


def near_attention(query, parts_k, parts_v, bias):
    frames, per_query, features = query.shape
    heads = features // HD
    span = sum(part.shape[1] for part in parts_k)

    def spec(rows):
        return pl.BlockSpec((frames, rows, HD), lambda h: (0, 0, h))

    part_specs = [spec(part.shape[1]) for part in parts_k]
    keys = frames * span
    return pl.pallas_call(
        functools.partial(near_kernel, frames, per_query, len(parts_k)),
        grid=(heads,),
        in_specs=[spec(per_query), pl.BlockSpec((1, keys), lambda h: (0, 0))]
        + part_specs
        + part_specs,
        out_specs=[
            spec(per_query),
            pl.BlockSpec((1, frames, per_query, HD), lambda h: (h, 0, 0, 0)),
        ],
        out_shape=[
            jax.ShapeDtypeStruct((frames, per_query, features), jnp.float32),
            jax.ShapeDtypeStruct((heads, frames, per_query, HD), jnp.float32),
        ],
        scratch_shapes=[
            pltpu.VMEM((keys, HD), jnp.bfloat16),
            pltpu.VMEM((keys, 2 * HD), jnp.bfloat16),
        ],
        compiler_params=pltpu.CompilerParams(vmem_limit_bytes=60 << 20),
        cost_estimate=pl.CostEstimate(
            flops=heads * frames * per_query * keys * HD * 6,
            bytes_accessed=30 << 20,
            transcendentals=heads * frames * per_query * keys,
        ),
        name="near",
    )(query, bias, *parts_k, *parts_v)


def pick_kernel(total, group, wanted_ref, keys_ref, values_ref, out_ref, held, in_sem, out_sem):
    groups = total // group

    def fetch(i, carry):
        block = wanted_ref[i]
        sem = in_sem.at[i // group]
        pltpu.make_async_copy(keys_ref.at[block], held.at[i, 0], sem).start()
        pltpu.make_async_copy(values_ref.at[block], held.at[i, 1], sem).start()
        return carry

    lax.fori_loop(0, total, fetch, 0)
    for g in range(groups):
        part = pl.ds(g * group, group)
        pltpu.make_async_copy(held.at[part], held.at[part], in_sem.at[g]).wait()
        pltpu.make_async_copy(held.at[part], out_ref.at[part], out_sem.at[g]).start()
    for g in range(groups):
        part = pl.ds(g * group, group)
        pltpu.make_async_copy(held.at[part], out_ref.at[part], out_sem.at[g]).wait()


def pick_blocks(wanted, keys, values):
    total = wanted.shape[0]
    group = 8 if total % 8 == 0 else 1
    shape = (total, 2) + keys.shape[1:]
    return pl.pallas_call(
        functools.partial(pick_kernel, total, group),
        grid_spec=pltpu.PrefetchScalarGridSpec(
            num_scalar_prefetch=1,
            grid=(),
            in_specs=[pl.BlockSpec(memory_space=pl.ANY)] * 2,
            out_specs=pl.BlockSpec(memory_space=pl.ANY),
            scratch_shapes=[
                pltpu.VMEM(shape, keys.dtype),
                pltpu.SemaphoreType.DMA((total // group,)),
                pltpu.SemaphoreType.DMA((total // group,)),
            ],
        ),
        out_shape=jax.ShapeDtypeStruct(shape, keys.dtype),
        compiler_params=pltpu.CompilerParams(vmem_limit_bytes=60 << 20),
        cost_estimate=pl.CostEstimate(flops=0, bytes_accessed=20 << 20, transcendentals=0),
        name="pick",
    )(wanted, keys, values)


def far_attention(query, acc, ml, blocks, count, slots):
    frames, per_query, features = query.shape
    all_slots, _, tokens, width = blocks.shape
    heads = width // HD
    spec = pl.BlockSpec((frames, per_query, HD), lambda h, *_: (0, 0, h))
    k_spec = pl.BlockSpec((all_slots, 1, tokens, HD), lambda h, *_: (0, 0, 0, h))
    v_spec = pl.BlockSpec((all_slots, 1, tokens, HD), lambda h, *_: (0, 1, 0, h))
    return pl.pallas_call(
        functools.partial(far_kernel, frames, per_query, tokens),
        grid_spec=pltpu.PrefetchScalarGridSpec(
            num_scalar_prefetch=2,
            grid=(heads,),
            in_specs=[
                spec,
                spec,
                pl.BlockSpec((1, frames, per_query, HD), lambda h, *_: (h, 0, 0, 0)),
                k_spec,
                v_spec,
            ],
            out_specs=pl.BlockSpec((frames, per_query, HD), lambda h, *_: (0, 0, h)),
            scratch_shapes=[
                pltpu.VMEM((CHUNK * tokens, HD), jnp.bfloat16),
                pltpu.VMEM((CHUNK * tokens, 2 * HD), jnp.bfloat16),
                pltpu.VMEM((frames, per_query, HD), jnp.float32),
                pltpu.VMEM((frames, per_query, HD), jnp.float32),
                pltpu.VMEM((frames, per_query, HD), jnp.float32),
            ],
        ),
        out_shape=jax.ShapeDtypeStruct((frames, per_query, width), jnp.bfloat16),
        compiler_params=pltpu.CompilerParams(vmem_limit_bytes=60 << 20),
        cost_estimate=pl.CostEstimate(
            flops=heads * frames * per_query * 1536 * HD * 6,
            bytes_accessed=30 << 20,
            transcendentals=heads * frames * per_query * 1536,
        ),
        name="far",
    )(count, slots, query, acc, ml, blocks, blocks)


def general(
    queries,
    keys_now,
    values_now,
    query_gain,
    key_gain,
    cached_keys,
    cached_values,
    block_lists,
    block_counts,
):
    frames, tile_rows, tile_cols, features = queries.shape
    owners_all = lax.axis_size("ty") * lax.axis_size("tx")
    full_width = features * lax.axis_size("ha")
    per_query = tile_rows * tile_cols
    per_tile, block_tokens = cached_keys.shape[:2]

    listed = block_lists[0]
    list_length = listed.shape[0]
    owners = listed // per_tile
    within = listed % per_tile
    slot_rank = slot_ranks(owners)
    capacity = max(2, 4 * list_length // (3 * owners_all))
    target = owners * capacity + slot_rank
    all_slots = lax.broadcasted_iota(jnp.int32, (1, owners_all * capacity), 1)
    matches = target[:, None] == all_slots
    outgoing = jnp.sum(jnp.where(matches, within[:, None], 0), axis=0).reshape(owners_all, capacity)
    wanted = lax.all_to_all(outgoing, ("ty", "tx"), split_axis=0, concat_axis=0, tiled=True)
    wanted = wanted.reshape(-1)

    out = pick_blocks(wanted, cached_keys, cached_values)
    now_keys, now_values, _ = lax.optimization_barrier((keys_now, values_now, wanted))
    paired = jnp.stack([now_keys, now_values])
    row_parts = neighbours(paired, "ty", 2, HALO)
    column = jnp.concatenate(
        [jnp.concatenate([part[..., :HALO, :], part[..., -HALO:, :]], axis=3) for part in
         [paired] + [got for got, _ in row_parts]],
        axis=2,
    )
    column_parts = neighbours(column, "tx", 3, HALO)
    out, column_got = lax.optimization_barrier((out, [got for got, _ in column_parts]))
    column_parts = [(got, ok) for got, (_, ok) in zip(column_got, column_parts)]
    back = lax.all_to_all(
        out.reshape((owners_all, capacity) + out.shape[1:]),
        ("ty", "tx"),
        split_axis=0,
        concat_axis=0,
        tiled=True,
    )
    far_blocks = back.reshape((-1,) + out.shape[1:])

    query_wide = queries.astype(jnp.float32)
    key_wide = keys_now.astype(jnp.float32)
    query_sq, key_sq = lax.psum(
        (jnp.sum(query_wide * query_wide, axis=-1), jnp.sum(key_wide * key_wide, axis=-1)), "ha"
    )

    def normed(wide, squares, gain):
        return (wide * lax.rsqrt(squares / full_width + epsilon)[..., None] * gain).astype(
            jnp.bfloat16
        )

    normed_key = normed(key_wide, key_sq, key_gain)
    normed_query = normed(query_wide, query_sq, query_gain)

    ok_rows = [jnp.ones((tile_rows,), bool)] + [
        jnp.broadcast_to(ok, (HALO,)) for _, ok in row_parts
    ]
    ok_rows = jnp.concatenate(ok_rows)
    margins_k, margins_v = [], []
    oks = [jnp.ones((per_query,), bool)]
    for got, ok in row_parts:
        oks.append(jnp.broadcast_to(ok, (HALO * tile_cols,)))
    for got, ok in column_parts:
        oks.append(jnp.repeat(ok_rows & ok, HALO))
    for got, _ in row_parts + column_parts:
        margins_k.append(got[0].reshape(frames, -1, features).astype(jnp.float32))
        margins_v.append(got[1].reshape(frames, -1, features))
    margin_sq = lax.psum(
        jnp.concatenate([jnp.sum(part * part, axis=-1) for part in margins_k], axis=1), "ha"
    )
    parts_k = [normed_key.reshape(frames, -1, features)]
    at = 0
    for part in margins_k:
        parts_k.append(normed(part, margin_sq[:, at : at + part.shape[1]], key_gain))
        at += part.shape[1]
    parts_v = [values_now.reshape(frames, -1, features)] + margins_v
    bias = jnp.where(jnp.concatenate(oks), 0.0, masked_score).astype(jnp.float32)
    bias = jnp.tile(bias, frames)[None]

    flat_query = normed_query.reshape(frames, per_query, features)
    acc, ml = near_attention(flat_query, parts_k, parts_v, bias)
    padding = (-list_length) % CHUNK
    slots = jnp.pad(target, (0, padding))
    attended = far_attention(flat_query, acc, ml, far_blocks, block_counts, slots)
    return attended.reshape(frames, tile_rows, tile_cols, features)


def share_kernel(rows, cols, count_ref, list_ref, notes_ref, send_sem, recv_sem):
    ty, tx, ha = lax.axis_index("ty"), lax.axis_index("tx"), lax.axis_index("ha")
    tiles = rows * cols
    me = ty * cols + tx
    peers = []
    for o in range(1, tiles):
        tile = lax.rem(me + o, tiles)
        peers.append((lax.div(tile, cols), lax.rem(tile, cols), ha))
    barrier = pltpu.get_barrier_semaphore()
    for peer in peers:
        pl.semaphore_signal(barrier, inc=1, device_id=peer, device_id_type=pl.DeviceIdType.MESH)
    notes_ref[me] = jnp.full(notes_ref.shape[1:], count_ref[0], jnp.int32)
    notes_ref[me, :, : list_ref.shape[1]] = list_ref[...]
    pl.semaphore_wait(barrier, tiles - 1)
    copies = []
    for i, peer in enumerate(peers):
        copy = pltpu.make_async_remote_copy(
            src_ref=notes_ref.at[me],
            dst_ref=notes_ref.at[me],
            send_sem=send_sem.at[i],
            recv_sem=recv_sem.at[i],
            device_id=peer,
            device_id_type=pl.DeviceIdType.MESH,
        )
        copy.start()
        copies.append(copy)
    for copy in copies:
        copy.wait_send()
    for i in range(tiles - 1):
        slot = notes_ref.at[lax.rem(me + 2 * tiles - 1 - i, tiles)]
        pltpu.make_async_copy(slot, slot, recv_sem.at[i]).wait()


def share(block_lists, block_counts):
    rows, cols = lax.axis_size("ty"), lax.axis_size("tx")
    tiles = rows * cols
    vmem = pl.BlockSpec(memory_space=pltpu.VMEM)
    return pl.pallas_call(
        functools.partial(share_kernel, rows, cols),
        in_specs=[pl.BlockSpec(memory_space=pltpu.SMEM), vmem],
        out_specs=vmem,
        out_shape=jax.ShapeDtypeStruct((tiles, 1, HD), jnp.int32),
        scratch_shapes=[pltpu.SemaphoreType.DMA((tiles - 1,))] * 2,
        compiler_params=pltpu.CompilerParams(collective_id=0, has_side_effects=True),
        name="share",
    )(block_counts, block_lists)


def plan_kernel(
    sizes, classes, length, per_tile, notes_ref, keys_ref, values_ref, across, beside, core, own,
    early_ref, late_ref, facts_ref, held, in_sem, out_sem, number_ref, slot_ref,
):
    tiles = notes_ref.shape[0]
    cols = lax.axis_size("tx")
    me = lax.axis_index("ty") * cols + lax.axis_index("tx")
    capacity = sizes[3]
    shift = per_tile.bit_length() - 1

    def owner_of(block):
        return lax.shift_right_logical(block, shift) if per_tile == 1 << shift else block // per_tile

    def pair(tile):
        return tile - lax.rem(tile, 2)

    def clear(i, carry):
        number_ref[i] = 0
        return carry

    lax.fori_loop(0, tiles * tiles, clear, 0)

    sections = [
        (0, (pair(me ^ 6), pair(me ^ 6) + 1, pair(me ^ 4), pair(me ^ 4) + 1)),
        (sizes[0], (pair(me ^ 2), pair(me ^ 2) + 1)),
        (sizes[0] + sizes[1], (me ^ 1,)),
        (sizes[0] + sizes[1] + sizes[2], (me,)),
    ]
    counts = []
    for start, targets in sections:
        at = jnp.int32(start)
        for target in targets:

            def scan(j, at, target=target):
                block = notes_ref[target, 0, j]
                owner = owner_of(block)
                cell = owner * tiles + target
                number_ref[cell] = number_ref[cell] + 1
                mine = owner == me

                @pl.when(mine)
                def _():
                    here = block - me * per_tile
                    pltpu.make_async_copy(keys_ref.at[here], held.at[at, 0], in_sem.at[at]).start()
                    pltpu.make_async_copy(values_ref.at[here], held.at[at, 1], in_sem.at[at]).start()

                return at + mine.astype(jnp.int32)

            at = lax.fori_loop(0, notes_ref[target, 0, length], scan, at)
        counts.append(at - start)

    for (start, _), count, out_ref in zip(sections, counts, (across, beside, core, own)):

        def store(i, carry, start=start, out_ref=out_ref):
            at = start + i
            pltpu.make_async_copy(held.at[at], held.at[at], in_sem.at[at]).wait()
            pltpu.make_async_copy(held.at[at], out_ref.at[i], out_sem.at[at]).start()
            return carry

        lax.fori_loop(0, count, store, 0)

    def number(owner, target):
        return number_ref[owner * tiles + target]

    def both(owner, target):
        return number(owner, target) + number(owner, target + 1)

    def most(owner, carry):
        diagonal = both(owner, pair(owner ^ 6))
        most_across, most_diagonal, most_beside = carry
        return (
            jnp.maximum(most_across, diagonal + both(owner, pair(owner ^ 4))),
            jnp.maximum(most_diagonal, diagonal),
            jnp.maximum(most_beside, both(owner, pair(owner ^ 2))),
        )

    need = lax.fori_loop(0, tiles, most, (jnp.int32(0),) * 3)
    which = jnp.int32(0)
    for limits in classes:
        short = (need[0] > limits[0]) | (need[1] > limits[1]) | (need[2] > limits[2])
        which = which + short.astype(jnp.int32)
    n_across, n_relayed, n_beside = (jnp.int32(classes[-1][i]) for i in range(3))
    for i, limits in reversed(list(enumerate(classes))):
        n_across = jnp.where(which == i, limits[0], n_across)
        n_relayed = jnp.where(which == i, limits[1], n_relayed)
        n_beside = jnp.where(which == i, limits[2], n_beside)

    def place(owner, carry):
        flip = owner ^ me
        other = lax.rem(flip, 2)
        before = jnp.where(lax.rem(me, 2) == 1, number(owner, pair(me)), 0)
        diagonal = both(owner, pair(owner ^ 6))
        near = jnp.where(flip == 0, 0, capacity)
        early = jnp.where(flip >= 2, 2 * capacity + other * n_beside + before, near)
        straight = other * n_across + diagonal + before
        turned = 2 * n_across + other * n_relayed + before
        late = jnp.where(flip >= 6, turned, straight)
        slot_ref[owner] = jnp.where(flip >= 4, late, early)
        return carry

    lax.fori_loop(0, tiles, place, 0)

    def blank(i, carry):
        early_ref[i] = 2 * capacity + 2 * n_beside
        late_ref[i] = 2 * n_across + 2 * n_relayed
        return carry

    lax.fori_loop(0, 4 * capacity, blank, 0)

    def point(j, carry):
        n_early, n_late = carry
        owner = owner_of(notes_ref[me, 0, j])
        slot = slot_ref[owner]
        slot_ref[owner] = slot + 1
        far = (owner ^ me) >= 4

        @pl.when(far)
        def _():
            late_ref[n_late] = slot

        @pl.when(jnp.logical_not(far))
        def _():
            early_ref[n_early] = slot

        step = far.astype(jnp.int32)
        return n_early + 1 - step, n_late + step

    n_early, n_late = lax.fori_loop(
        0, notes_ref[me, 0, length], point, (jnp.int32(0), jnp.int32(0))
    )
    facts_ref[0] = n_early
    facts_ref[1] = n_late
    facts_ref[2] = which

    for (start, _), count, out_ref in zip(sections, counts, (across, beside, core, own)):

        def settle(i, carry, start=start, out_ref=out_ref):
            at = start + i
            pltpu.make_async_copy(held.at[at], out_ref.at[i], out_sem.at[at]).wait()
            return carry

        lax.fori_loop(0, count, settle, 0)


def plan(notes, keys, values, capacity, classes, length):
    hbm = pl.BlockSpec(memory_space=pl.ANY)
    smem = pl.BlockSpec(memory_space=pltpu.SMEM)
    sizes = (4 * capacity, 2 * capacity, capacity, capacity)
    total, tiles = sum(sizes), notes.shape[0]
    return pl.pallas_call(
        functools.partial(plan_kernel, sizes, classes, length, keys.shape[0]),
        in_specs=[smem, hbm, hbm],
        out_specs=[hbm] * 4 + [smem] * 3,
        out_shape=[
            jax.ShapeDtypeStruct((size, 2) + keys.shape[1:], keys.dtype) for size in sizes
        ]
        + [jax.ShapeDtypeStruct((n,), jnp.int32) for n in (4 * capacity, 4 * capacity, 3)],
        scratch_shapes=[
            pltpu.VMEM((total, 2) + keys.shape[1:], keys.dtype),
            pltpu.SemaphoreType.DMA((total,)),
            pltpu.SemaphoreType.DMA((total,)),
            pltpu.SMEM((tiles * tiles,), jnp.int32),
            pltpu.SMEM((tiles,), jnp.int32),
        ],
        compiler_params=pltpu.CompilerParams(vmem_limit_bytes=60 << 20),
        cost_estimate=pl.CostEstimate(flops=0, bytes_accessed=16 << 20, transcendentals=0),
        name="plan",
    )(notes, keys, values)


def late_heads(heads):
    last = max(1, heads // 5)
    middle = max(1, 3 * heads // 10)
    return [(0, heads - middle - last), (heads - middle - last, middle), (heads - last, last)]


def fused_kernel(sizes, heads, early_ref, late_ref, facts_ref, *refs):
    n_across, n_relayed, n_beside, n_core = sizes
    (
        query, key, value, query_gain, key_gain, across, beside, core, own,
        out_ref,
        qh, qt, k_own, v_own, k_side, v_side, k_edge, v_edge, k_rows, v_rows,
        k_corner, v_corner, k_give, v_give,
        early, late, kbuf, vbuf, vtail, m_sc, acc_sc, sums,
        load_sem, send_sem, recv_sem, out_sem,
    ) = refs
    ty, tx, ha = lax.axis_index("ty"), lax.axis_index("tx"), lax.axis_index("ha")
    cols, depth = lax.axis_size("tx"), lax.axis_size("ha")
    frames, per_query, features = qh.shape
    width = k_rows.shape[1] // HALO
    tile_rows = per_query // width
    tokens = early.shape[2]
    n_slots = early_ref.shape[0]
    opposite = (1 - ty, tx, ha)
    partner = (ty, lax.rem(tx + 2, cols), ha)
    sibling = (ty, tx + 1 - 2 * lax.rem(tx, 2), ha)
    left, right = (ty, tx - 1, ha), (ty, tx + 1, ha)
    has_left, has_right = tx > 0, tx < cols - 1
    mesh_id = pl.DeviceIdType.MESH
    cuts = late_heads(heads)

    barrier = pltpu.get_barrier_semaphore()
    peers = [opposite, partner, sibling, (ty, 3 - tx, ha)]
    depth_peers = [(ty, tx, lax.rem(ha + o, depth)) for o in range(1, depth)]
    for peer in peers + depth_peers:
        pl.semaphore_signal(barrier, inc=1, device_id=peer, device_id_type=mesh_id)

    first_keys = pl.ds(0, tokens)
    n_early, n_late = early.shape[0], late.shape[0]
    def local_copies():
        return [
            (query, qh),
            (key, k_own),
            (value, v_own),
            (own, early.at[pl.ds(0, n_core)]),
            (value.at[0, first_keys], early.at[n_early - 1, 1]),
            (value.at[0, first_keys], late.at[n_late - 1, 1]),
        ]

    def load(i):
        return pltpu.make_async_copy(*local_copies()[i], load_sem.at[i])

    for i in range(len(local_copies())):
        load(i).start()

    pl.semaphore_wait(barrier, len(peers + depth_peers))

    started = []
    ends = iter(range(64))

    class Sent:
        def __init__(self, views, peer):
            self.views, self.peer, self.end = views, peer, next(ends)
            started.append(self)

        def copy(self):
            src, dst = self.views()
            return pltpu.make_async_remote_copy(
                src_ref=src, dst_ref=dst, send_sem=send_sem.at[self.end],
                recv_sem=recv_sem.at[self.end], device_id=self.peer, device_id_type=mesh_id,
            )

        def wait_recv(self):
            self.copy().wait_recv()

        def wait_send(self):
            self.copy().wait_send()

    def send(views, peer):
        sent = Sent(views, peer)
        sent.copy().start()
        return sent

    def give_sides(src, dst, side_first, side_last):
        i, j = next(ends), next(ends)

        def to_left():
            return pltpu.make_async_remote_copy(
                src_ref=side_first(src), dst_ref=side_last(dst), send_sem=send_sem.at[i],
                recv_sem=recv_sem.at[i], device_id=left, device_id_type=mesh_id,
            )

        def to_right():
            return pltpu.make_async_remote_copy(
                src_ref=side_last(src), dst_ref=side_first(dst), send_sem=send_sem.at[j],
                recv_sem=recv_sem.at[j], device_id=right, device_id_type=mesh_id,
            )

        @pl.when(has_left)
        def _():
            to_left().start()

        @pl.when(has_right)
        def _():
            to_right().start()

        @pl.when(jnp.logical_not(has_right))
        def _():
            pltpu.make_async_copy(side_last(src), side_last(dst), recv_sem.at[i]).start()

        @pl.when(jnp.logical_not(has_left))
        def _():
            pltpu.make_async_copy(side_first(src), side_first(dst), recv_sem.at[j]).start()

        def wait():
            pltpu.make_async_copy(side_last(dst), side_last(dst), recv_sem.at[i]).wait()
            pltpu.make_async_copy(side_first(dst), side_first(dst), recv_sem.at[j]).wait()

        def settle():
            @pl.when(has_left)
            def _():
                to_left().wait_send()

            @pl.when(has_right)
            def _():
                to_right().wait_send()

        return wait, settle

    def lanes_of(h):
        return pl.ds(pl.multiple_of(h * HD, HD), HD)

    n_below = n_across - n_relayed

    def slots(pool, first, count):
        return pool.at[pl.ds(first, count)]

    def above():
        return slots(late, 0, n_relayed)

    def below():
        return slots(late, n_relayed, n_below)

    def beside_at():
        return slots(early, 2 * n_core, n_beside)

    def relayed():
        return slots(late, 2 * n_across, n_relayed)

    got_above = send(lambda: (slots(across, 0, n_relayed), above()), opposite)
    got_beside = send(lambda: (slots(beside, 0, n_beside), beside_at()), partner)
    got_core = send(lambda: (core, slots(early, n_core, n_core)), sibling)

    load(0).wait()
    load(1).wait()
    ones = jnp.ones((8, HD), jnp.float32)
    for at, ref in ((0, qh), (frames, k_own)):
        for f in range(frames):

            def add(h, total, ref=ref, f=f):
                wide = ref[f, :, lanes_of(h)].astype(jnp.float32)
                return total + wide * wide

            total = lax.fori_loop(0, heads, add, jnp.zeros((per_query, HD), jnp.float32))
            line = lax.dot_general(
                ones, total, (((1,), (1,)), ((), ())), preferred_element_type=jnp.float32,
                precision=lax.Precision.HIGHEST,
            )
            sums[0, :, (at + f) * per_query : (at + f + 1) * per_query] = line[:1]
    got_sums = [
        send(lambda o=o: (sums.at[0], sums.at[o]), depth_peers[o - 1]) for o in range(1, depth)
    ]
    load(2).wait()
    for copy in got_sums:
        copy.wait_recv()
    total = sums[ha]
    for z in range(1, depth):
        total = total + sums[lax.rem(ha - z + depth, depth)]
    scale = lax.rsqrt(total / (features * depth) + epsilon)

    for f in range(frames):
        scales = []
        for at in (0, frames):
            line = scale[:, (at + f) * per_query : (at + f + 1) * per_query]
            scales.append(jnp.broadcast_to(line, (HD, per_query)).T)

        def norm(h, carry, f=f, scales=scales):
            lanes = lanes_of(h)
            q = qh[f, :, lanes].astype(jnp.float32) * scales[0] * query_gain[:, lanes]
            q = q.astype(jnp.bfloat16).astype(jnp.float32) * log2_scale
            q = q.T
            high = q.astype(jnp.bfloat16)
            qt[h, f, :HD] = high
            qt[h, f, HD:] = (q - high.astype(jnp.float32)).astype(jnp.bfloat16)
            k = k_own[f, :, lanes].astype(jnp.float32) * scales[1] * key_gain[:, lanes]
            k_own[f, :, lanes] = k.astype(jnp.bfloat16)
            return carry

        lax.fori_loop(0, heads, norm, 0)

    def narrow(source, give, n_rows, first, count):
        def cut(h, carry):
            lanes = lanes_of(h)
            for f in range(frames):
                wide = source[f, :, lanes].astype(jnp.float32)
                for i, start in ((0, 0), (1, width - HALO)):
                    cells = [
                        wide[r * width + start : r * width + start + HALO] for r in range(n_rows)
                    ]
                    give[i, f, :, lanes] = jnp.concatenate(cells, axis=0).astype(jnp.bfloat16)
            return carry

        lax.fori_loop(first, first + count, cut, 0)

    rows_out, got_below = [], None
    rows_at = pl.ds((1 - ty) * (tile_rows - HALO) * width, HALO * width)
    for first, count in cuts:
        lanes = pl.ds(first * HD, count * HD)
        rows_out.append(
            [
                send(
                    lambda src=src, dst=dst, lanes=lanes: (
                        src.at[:, rows_at, lanes],
                        dst.at[:, :, lanes],
                    ),
                    opposite,
                )
                for src, dst in ((k_own, k_rows), (v_own, v_rows))
            ]
        )
        if got_below is None:
            got_below = send(
                lambda: (slots(across, n_relayed, n_below), below()), opposite
            )

    def whole(i):
        return lambda ref: ref.at[i]

    narrow(k_own, k_edge, tile_rows, 0, heads)
    narrow(v_own, v_edge, tile_rows, 0, heads)
    k_side_wait, k_side_settle = give_sides(k_edge, k_side, whole(0), whole(1))
    v_side_wait, v_side_settle = give_sides(v_edge, v_side, whole(0), whole(1))

    def put(at, k, v):
        n = k.shape[0]
        kbuf[at : at + n, :HD] = k
        kbuf[at : at + n, HD:] = k
        vbuf[at : at + n, :] = v

    def attend(h, *jobs):
        jobs = list(zip(jobs[::2], jobs[1::2]))
        scores = [
            jnp.dot(kbuf[:keys], qt[h, f], preferred_element_type=jnp.float32) for f, keys in jobs
        ]
        old = [m_sc[h, f, :1] for f, _ in jobs]
        held = [acc_sc[h, f] for f, _ in jobs]
        new = [jnp.maximum(m, jnp.max(s, axis=0, keepdims=True)) for m, s in zip(old, scores)]
        weights = [jnp.exp2(s - m).astype(jnp.bfloat16) for s, m in zip(scores, new)]
        sums_now = [
            jnp.dot(vtail[:, :keys], p, preferred_element_type=jnp.float32)
            for (_, keys), p in zip(jobs, weights)
        ]
        for (f, _), acc, m_old, m, o in zip(jobs, held, old, new, sums_now):
            acc_sc[h, f] = acc * jnp.exp2(m_old - m) + o
            m_sc[h, f] = jnp.broadcast_to(m, m_sc.shape[2:])

    span = per_query
    n_rows = k_rows.shape[1]
    parts = ((k_side, v_side), (k_corner, v_corner))
    pad = span - n_rows - 2 * sum(k.shape[2] for k, _ in parts)

    def put_own(h):
        lanes = lanes_of(h)
        m_sc[h] = jnp.full(m_sc.shape[1:], masked_score, jnp.float32)
        acc_sc[h] = jnp.zeros(acc_sc.shape[1:], jnp.float32)
        for f in range(frames):
            put(f * span, k_own[f, :, lanes], v_own[f, :, lanes])

    def put_rows(h):
        lanes = lanes_of(h)
        for f in range(frames):
            at = f * span
            put(at, k_rows[f, :, lanes], v_rows[f, :, lanes])
            at += n_rows
            for k, v in parts:
                for i in (0, 1):
                    put(at, k[i, f, :, lanes], v[i, f, :, lanes])
                    at += k.shape[2]
            if pad:
                put(at, k_rows[f, :pad, lanes], v_rows[f, :pad, lanes])

    def put_blocks(h, pool, slots_ref):
        lanes = lanes_of(h)
        for i in range(n_slots):
            slot = slots_ref[i]
            put(i * tokens, pool[slot, 0, :, lanes], pool[slot, 1, :, lanes])

    n_keys = frames * span
    spot = lax.broadcasted_iota(jnp.int32, (vtail.shape[0] - HD, n_keys), 1)

    def weigh(weight):
        vtail[HD:] = weight.astype(jnp.bfloat16)

    def weigh_blocks(valid):
        weigh(jnp.where(spot < valid * tokens, 1.0, 0.0))

    def weigh_rows():
        within = lax.rem(spot, span)
        weight = jnp.where(within < n_rows, 1.0, 0.0)
        at = n_rows
        for k, _ in parts:
            for there in (has_left, has_right):
                inside = (within >= at) & (within < at + k.shape[2])
                weight = jnp.where(inside, jnp.where(there, 1.0, 0.0), weight)
                at += k.shape[2]
        weigh(weight)

    assert n_slots * tokens == n_keys and pad >= 0
    settles = [k_side_settle, v_side_settle]

    later = {}

    def before_early():
        got_above.wait_recv()
        later["relay"] = send(lambda: (above(), relayed()), partner)
        got_beside.wait_recv()
        later["beside"] = send(
            lambda: (beside_at(), slots(early, 2 * n_core + n_beside, n_beside)), sibling
        )
        later["above"] = send(lambda: (above(), slots(late, n_across, n_relayed)), sibling)
        got_core.wait_recv()
        for i in range(3, len(local_copies())):
            load(i).wait()
        for pool, at in ((early, n_early), (late, n_late)):
            pool[at - 1, 0] = k_own[0, :tokens]
        later["beside"].wait_recv()

    def forward_late():
        got_below.wait_recv()
        later["below"] = send(
            lambda: (below(), slots(late, n_across + n_relayed, n_below)), sibling
        )
        later["relay"].wait_recv()
        later["relayed"] = send(
            lambda: (relayed(), slots(late, 2 * n_across + n_relayed, n_relayed)), sibling
        )

    def before_late():
        for name in ("above", "below", "relayed"):
            later[name].wait_recv()

    cut_waits = {}

    def begin_cut(cut):
        first, count = cuts[cut]
        if cut == 0:
            k_side_wait()
            v_side_wait()
        for copy in rows_out[cut]:
            copy.wait_recv()
        narrow(k_rows, k_give, HALO, first, count)
        narrow(v_rows, v_give, HALO, first, count)
        lanes = pl.ds(first * HD, count * HD)

        def side_of(i):
            return lambda ref: ref.at[i, :, :, lanes]

        waits = []
        for give, take in ((k_give, k_corner), (v_give, v_corner)):
            wait, settle = give_sides(give, take, side_of(0), side_of(1))
            waits.append(wait)
            settles.append(settle)
        cut_waits[cut] = waits

    def end_cut(cut):
        for wait in cut_waits[cut]:
            wait()

    def give_out(cut):
        lanes = pl.ds(cuts[cut][0] * HD, cuts[cut][1] * HD)
        return pltpu.make_async_copy(qh.at[:, :, lanes], out_ref.at[:, :, lanes], out_sem.at[cut])

    first_cut = cuts[0][1]
    starts = (0, heads, 2 * heads, 2 * heads + first_cut, 3 * heads + first_cut)

    def step(i, carry):
        own_now, early_now = i < starts[1], (i >= starts[1]) & (i < starts[2])
        late_now = (i >= starts[3]) & (i < starts[4])
        rows_now = ((i >= starts[2]) & (i < starts[3])) | (i >= starts[4])
        h = jnp.where(i < starts[1], i, i - heads)
        h = jnp.where(i < starts[2], h, i - starts[2])
        h = jnp.where(i < starts[3], h, i - starts[3])
        h = jnp.where(i < starts[4], h, i - starts[4] + first_cut)
        final = (late_now & (h < first_cut)) | (i >= starts[4])

        @pl.when(i == starts[0])
        def _():
            weigh(jnp.ones(spot.shape, jnp.float32))

        @pl.when(i == starts[1])
        def _():
            before_early()
            weigh_blocks(facts_ref[0])

        @pl.when((i == starts[2]) | (i == starts[4]))
        def _():
            weigh_rows()

        @pl.when(i == max(starts[2], starts[3] - 2))
        def _():
            forward_late()

        for cut in range(len(cuts)):
            at = starts[2] if cut == 0 else starts[4] - 1 if cut > 1 else starts[3] + heads // 2

            @pl.when(i == at)
            def _(cut=cut):
                begin_cut(cut)

        @pl.when(i == starts[3])
        def _():
            before_late()
            weigh_blocks(facts_ref[1])

        for cut, (first, count) in enumerate(cuts):

            @pl.when(rows_now & (h == first))
            def _(cut=cut):
                end_cut(cut)

        @pl.when(own_now)
        def _():
            put_own(h)

        @pl.when(early_now)
        def _():
            put_blocks(h, early, early_ref)

        @pl.when(late_now)
        def _():
            put_blocks(h, late, late_ref)

        @pl.when(rows_now)
        def _():
            put_rows(h)

        vtail[:HD] = vbuf[...].T * vtail[HD : HD + 1]

        @pl.when(own_now | rows_now)
        def _():
            for pair in range(0, frames, 2):
                attend(h, pair, (pair + 1) * span, pair + 1, (pair + 2) * span)

        @pl.when(early_now | late_now)
        def _():
            def both(pair, carry):
                attend(h, 2 * pair, n_keys, 2 * pair + 1, n_keys)
                return carry

            lax.fori_loop(0, frames // 2, both, 0)

        @pl.when(final)
        def _():
            for f in range(frames):
                done = acc_sc[h, f, :HD] / acc_sc[h, f, HD : HD + 1]
                qh[f, :, lanes_of(h)] = done.T.astype(jnp.bfloat16)

        for cut, (first, count) in enumerate(cuts):

            @pl.when(final & (h == first + count - 1))
            def _(cut=cut):
                give_out(cut).start()

        return carry

    lax.fori_loop(0, 4 * heads, step, 0)
    for copy in started:
        copy.wait_send()
    for settle in settles:
        settle()
    for cut in range(len(cuts)):
        give_out(cut).wait()


def fused(sizes, number, early_slots, late_slots, facts, arrays):
    n_across, n_relayed, n_beside, n_core = sizes
    key, across = arrays[1], arrays[5]
    frames, tile_rows, width, features = key.shape
    per_query = tile_rows * width
    heads = features // HD
    depth = lax.axis_size("ha")
    tokens = across.shape[2]
    side, n_rows, edge = tile_rows * HALO, width * HALO, HALO * HALO
    kind = jnp.bfloat16
    hbm = pl.BlockSpec(memory_space=pl.ANY)
    smem = pl.BlockSpec(memory_space=pltpu.SMEM)
    vmem = pl.BlockSpec(memory_space=pltpu.VMEM)
    n_keys = max(
        frames * per_query, frames * (n_rows + 2 * side + 2 * edge), early_slots.shape[0] * tokens
    )
    n_ends = 40
    flat = (frames, per_query, features)
    whole = pltpu.VMEM(flat, kind)
    sides = pltpu.VMEM((2, frames, side, features), kind)
    corner = pltpu.VMEM((2, frames, edge, features), kind)
    rows = pltpu.VMEM((frames, n_rows, features), kind)
    scores = heads * frames * per_query * n_keys * 2
    query, key, value = (array.reshape(flat) for array in arrays[:3])
    gains = [array.reshape(1, features) for array in arrays[3:5]]
    return pl.pallas_call(
        functools.partial(fused_kernel, sizes, heads),
        in_specs=[smem] * 3 + [hbm] * 3 + [vmem] * 2 + [hbm] * 4,
        out_specs=hbm,
        out_shape=jax.ShapeDtypeStruct(flat, kind),
        scratch_shapes=[
            whole,
            pltpu.VMEM((heads, frames, 2 * HD, per_query), kind),
            whole,
            whole,
        ]
        + [sides] * 4
        + [rows] * 2
        + [corner] * 4
        + [
            pltpu.VMEM((2 * n_core + 2 * n_beside + 1, 2, tokens, features), kind),
            pltpu.VMEM((2 * n_across + 2 * n_relayed + 1, 2, tokens, features), kind),
            pltpu.VMEM((n_keys, 2 * HD), kind),
            pltpu.VMEM((n_keys, HD), kind),
            pltpu.VMEM((HD + 16, n_keys), kind),
            pltpu.VMEM((heads, frames, 8, per_query), jnp.float32),
            pltpu.VMEM((heads, frames, HD + 16, per_query), jnp.float32),
            pltpu.VMEM((depth, 1, 2 * frames * per_query), jnp.float32),
            pltpu.SemaphoreType.DMA((8,)),
            pltpu.SemaphoreType.DMA((n_ends,)),
            pltpu.SemaphoreType.DMA((n_ends,)),
            pltpu.SemaphoreType.DMA((len(late_heads(heads)),)),
        ],
        compiler_params=pltpu.CompilerParams(
            collective_id=number, has_side_effects=True, vmem_limit_bytes=63 << 20
        ),
        cost_estimate=pl.CostEstimate(
            flops=scores * HD * 6, bytes_accessed=60 << 20, transcendentals=scores
        ),
        name="fused",
    )(early_slots, late_slots, facts, query, key, value, *gains, *arrays[5:])


def local(*args):
    if lax.axis_size("ty") != 2 or lax.axis_size("tx") != 4:
        return general(*args)
    cached_keys, cached_values, block_lists, block_counts = args[5:]
    length = block_lists.shape[1]
    c = 4 * length // (3 * lax.axis_size("ty") * lax.axis_size("tx"))
    notes = share(block_lists, block_counts)
    classes = [
        (3 * c // 2 - 1, 5 * c // 4, 5 * c // 4),
        (7 * c // 4, 11 * c // 8, 11 * c // 8),
        (2 * c, 3 * c // 2, 3 * c // 2),
        (5 * c // 2, 2 * c, 2 * c),
    ]
    *packed, early_slots, late_slots, facts = plan(
        notes, cached_keys, cached_values, c, classes, length
    )

    def send(number, operands):
        early_slots, late_slots, facts, packed, args = operands
        sizes = classes[number] + (c,)
        out = fused(
            sizes, number + 1, early_slots, late_slots, facts, list(args[:5]) + list(packed)
        )
        return out.reshape(args[0].shape)

    def plain(operands):
        return general(*operands[-1])

    branches = [functools.partial(send, number) for number in range(len(classes))] + [plain]
    return lax.switch(facts[2], branches, (early_slots, late_slots, facts, packed, args))


def solution(mesh):
    return jax.shard_map(
        local,
        mesh=mesh,
        in_specs=(
            P(None, "ty", "tx", "ha"),
            P(None, "ty", "tx", "ha"),
            P(None, "ty", "tx", "ha"),
            P("ha"),
            P("ha"),
            P(("ty", "tx"), None, "ha"),
            P(("ty", "tx"), None, "ha"),
            P(("ty", "tx"), None),
            P(("ty", "tx")),
        ),
        out_specs=P(None, "ty", "tx", "ha"),
        check_vma=False,
    )
```
